32 devices in a mesh: groups: 2 (over y), seq: 4 (over z), head: 2 (over x), side: 2 (over core).
Axes of the slice: x: 2, y: 2, z: 4, core: 2. Of those that a mesh axis runs over, the one named last changes fastest.
Arguments:
- hidden: bfloat16 [32, 8192], P('groups', ('seq', 'side')), parts along dimension 0
- gain: float32 [8192], P(('seq', 'side')), may hold values from 0.25 to 1.75
- w_query: bfloat16 [8192, 8192], P(('seq', 'side'), 'head')
- w_key: bfloat16 [8192, 1024], P(('seq', 'side'), 'head')
- w_value: bfloat16 [8192, 1024], P(('seq', 'side'), 'head'), may hold values from -0.0625 to 0.0625
- w_out: bfloat16 [8192, 8192], P('head', ('seq', 'side')), may hold values from -0.0625 to 0.0625
- prefix_keys: bfloat16 [2, 8, 32768, 128], P('groups', 'head', ('seq', 'side')), parts along dimension 0, may hold values from -6 to 6
- prefix_values: bfloat16 [2, 8, 32768, 128], P('groups', 'head', ('seq', 'side')), parts along dimension 0
- suffix_keys: bfloat16 [256, 8, 128, 128], P(('groups', 'seq', 'side'), 'head'), parts along dimension 0, may hold values from -15 to 15
- suffix_values: bfloat16 [256, 8, 128, 128], P(('groups', 'seq', 'side'), 'head'), parts along dimension 0, may hold values from -6 to 6
- suffix_lengths: int32 [32], P('groups'), parts along dimension 0, may hold values from 1 to 1024, 8192 in all
- page_table: int32 [32, 8], P('groups'), parts along dimension 0, may hold values from 0 to 15, as said below
Outputs:
- hidden_out: bfloat16 [32, 8192], P('groups', ('seq', 'side')), parts along dimension 0
- update: float32 [32, 8192], P('groups', ('seq', 'side')), parts along dimension 0
The draws below stay inside these ranges and needn't reach their ends.
There are 2 independent parts, one for each index of `groups`. The reference program is written for one: setup_inputs(seed, part) draws one part's arguments, and reference() takes and returns one part's arrays. A program takes and returns all parts, laid end to end along the dimension named above; an argument that names none is the same for every part. Nothing has to cross between parts.
Inputs may be any that keep to these rules, and one draw needn't show every extreme that they name: `suffix_lengths`: the lengths sum to 8192 and the longest is exactly 1024. `page_table`: entries are slots within the holding block (s // 2) xor 1; the 2 samples of one block of sample rows use every slot of their holding block exactly once.
All inputs are finite; a program needn't handle non-finite values.
Results may differ from the reference program's by a relative error of at most 0.0081.
Values may be sent and summed in bfloat16 or wider, within the bound.
A program may use at most 128 MiB of HBM per device.

```python
import math
import jax
import jax.numpy as jnp
import numpy as np
from jax import lax

D = 8192
QH = 64
KVH = 8
HD = 128
GROUP = 8
SAMP_DEV = 2
GEN = 16
SAMPLES = 16
PROMPTS = 1
PREFIX = 32768
SUFFIX = 1024
PAGE = 128
PAGES = 8
SLOTS_DEV = 16
POOL = 128
STEPS = 3


def draw_hidden(key, part):
    base = jnp.clip(jax.random.normal(key, (SAMPLES, D), jnp.float32), -6.0, 6.0)
    column = jnp.arange(D, dtype=jnp.float32) / D
    ramp = 1.0 + 2.0 * column
    return (base * ramp).astype(jnp.bfloat16)


def head_ranks(key):
    return jax.random.permutation(jax.random.fold_in(key, 13), KVH)


def head_signs(key):
    rank = head_ranks(key)
    return jnp.where(rank % 2 == 0, -1.0, 1.0).astype(jnp.float32)


def projection_pair(key):
    query = jax.random.normal(jax.random.fold_in(key, 11), (D, QH * HD), jnp.float32) / math.sqrt(D)
    noise = jax.random.normal(jax.random.fold_in(key, 12), (D, KVH * HD), jnp.float32) / math.sqrt(D)
    grouped = query.reshape(D, KVH, GROUP, HD).mean(axis=2).reshape(D, KVH * HD)
    signs = jnp.repeat(head_signs(key), HD)[None, :]
    keyed = 6.0 * signs * grouped + noise
    return (query, keyed)


def draw_w_query(key, part):
    return projection_pair(key)[0].astype(jnp.bfloat16)


def draw_w_key(key, part):
    return projection_pair(key)[1].astype(jnp.bfloat16)


def draw_prefix_values(key, part):
    shape = (PROMPTS, KVH, PREFIX, HD)
    center = 0.5 * jax.random.normal(jax.random.fold_in(key, 21), (PROMPTS, KVH, 1, HD), jnp.float32)
    noise = jnp.clip(jax.random.normal(jax.random.fold_in(key, 22), shape, jnp.float32), -5.0, 5.0)
    return jnp.clip(center + noise, -6.0, 6.0).astype(jnp.bfloat16)


def draw_page_table(key, part):
    blocks = SAMPLES // SAMP_DEV
    keys = jax.random.split(key, blocks)
    perms = jax.vmap(lambda one: jax.random.permutation(one, SLOTS_DEV))(keys)
    return perms.reshape(SAMPLES, PAGES).astype(jnp.int32)


def block_scale(stream_key, dims, shards, least, top_value):
    def one(dim, parts):
        draws = jax.random.uniform(jax.random.fold_in(jax.random.fold_in(stream_key, 6), dim), (parts,), jnp.float32, least / len(shards), top_value / len(shards))
        return jnp.repeat(jnp.exp(draws), dims[dim] // parts).reshape((-1,) + (1,) * (len(dims) - dim - 1))

    level = one(*shards[0])
    for cut in shards[1:]:
        level = level * one(*cut)
    return level


def split_up(amount, total, most, skew):
    weights = [(1 << 20) // math.isqrt(standing ** skew) + 1 for standing in range(2, amount + 1)]
    surplus, counts = total - most - (amount - 1), [1] * (amount - 1)
    while surplus > 0:
        candidates = [i for i in range(amount - 1) if counts[i] < most]
        mass, left = sum([weights[i] for i in candidates]), surplus
        for i in candidates:
            addition = min(most - counts[i], max(1, left * weights[i] // mass), surplus)
            counts[i] = counts[i] + addition
            surplus = surplus - addition
    return np.array([most] + counts)


def ragged_sizes(own_key, count, total, reach, slope):
    if count == 2:
        one = jax.random.randint(own_key, (), max(1, total - reach), min(reach, total - 1) + 1)
        return jnp.stack([one, total - one])
    sizes = jnp.asarray(split_up(count, total, reach, slope), jnp.int32)
    twos = (count - 1) // 2
    donor, taker = sizes[1:1 + 2 * twos:2], sizes[2:2 + 2 * twos:2]
    margin = jnp.minimum(donor - 1, reach - taker)
    shifted = jax.random.randint(jax.random.fold_in(own_key, 1), (twos,), 0, 1 << 20) % (margin + 1)
    sizes = sizes.at[1:1 + 2 * twos:2].set(donor - shifted).at[2:2 + 2 * twos:2].set(taker + shifted)
    return sizes[jax.random.permutation(jax.random.fold_in(own_key, 2), count)]


def bell_draw(rng, dims, deviation, limit, cuts=(), kind=jnp.bfloat16):
    level = block_scale(rng, dims, cuts, -0.22, 0.18) if cuts else 1.0
    values = jax.random.normal(rng, dims, jnp.float32) * deviation * level
    return jnp.minimum(jnp.maximum(values, -limit), limit).astype(kind)


def setup_inputs(seed: int = 0, part: int = 0) -> dict:
    seeds = jax.random.split(jax.random.key(seed), 13)
    part_splits = jax.random.split(jax.random.fold_in(seeds[12], part), 13)
    hidden = draw_hidden(jax.random.fold_in(jax.random.fold_in(seeds[12], part), 71), part)
    gain = jnp.clip(1.0 + 0.15 * jax.random.normal(seeds[1], (D,), jnp.float32), 0.25, 1.75)
    w_query = draw_w_query(jax.random.fold_in(seeds[12], 71), part)
    w_key = draw_w_key(jax.random.fold_in(seeds[12], 71), part)
    w_value = bell_draw(seeds[4], (D, KVH * HD), D ** -0.5, 0.0625, ((0, 8), (1, 2)))
    w_out = bell_draw(seeds[5], (QH * HD, D), (QH * HD) ** -0.5, 0.0625, ((0, 2), (1, 8)))
    prefix_keys = bell_draw(part_splits[6], (PROMPTS, KVH, PREFIX, HD), 1.0, 6.0, ((1, 2), (2, 8)))
    prefix_values = draw_prefix_values(jax.random.fold_in(jax.random.fold_in(seeds[12], part), 71), part)
    suffix_keys = bell_draw(part_splits[8], (POOL, KVH, PAGE, HD), 2.5, 15.0, ((0, 8), (1, 2)))
    suffix_values = bell_draw(part_splits[9], (POOL, KVH, PAGE, HD), 1.0, 6.0, ((0, 8), (1, 2)))
    suffix_lengths = ragged_sizes(part_splits[10], SAMPLES, SAMPLES * SUFFIX // 2, SUFFIX, 2).astype(jnp.int32)
    page_table = draw_page_table(jax.random.fold_in(jax.random.fold_in(seeds[12], part), 71), part)
    return dict(hidden=hidden, gain=gain, w_query=w_query, w_key=w_key, w_value=w_value, w_out=w_out, prefix_keys=prefix_keys, prefix_values=prefix_values, suffix_keys=suffix_keys, suffix_values=suffix_values, suffix_lengths=suffix_lengths, page_table=page_table)


def rotate(vectors, position):
    half = vectors.shape[-1] // 2
    freq = 500000.0 ** (-(jnp.arange(half, dtype=jnp.float32) * 2.0 / vectors.shape[-1]))
    angle = position[..., None] * freq
    cosine = jnp.cos(angle)
    sine = jnp.sin(angle)
    lower = vectors[..., :half]
    upper = vectors[..., half:]
    return jnp.concatenate([lower * cosine - upper * sine, upper * cosine + lower * sine], axis=-1)

def rounded(weights):
    return lax.optimization_barrier(weights.astype(jnp.bfloat16)).astype(jnp.float32)

def reference(hidden, gain, w_query, w_key, w_value, w_out, prefix_keys, prefix_values, suffix_keys, suffix_values, suffix_lengths, page_table):
    scale = 1.0 / math.sqrt(HD)
    holder = jnp.bitwise_xor(jnp.arange(SAMPLES, dtype=jnp.int32) // SAMP_DEV, 1)
    slots = (holder[:, None] * SLOTS_DEV + page_table).astype(jnp.int32)
    page_keys = suffix_keys[slots].reshape(PROMPTS, GEN, PAGES, KVH, PAGE, HD)
    page_values = suffix_values[slots].reshape(PROMPTS, GEN, PAGES, KVH, PAGE, HD)
    lengths = suffix_lengths.reshape(PROMPTS, GEN)
    w_proj = jnp.concatenate([w_query, w_key, w_value], axis=1)
    query_width = QH * HD
    key_width = KVH * HD
    state = hidden
    update = jnp.zeros((SAMPLES, D), jnp.float32)
    new_keys = []
    new_values = []
    for step in range(STEPS):
        wide = state.astype(jnp.float32)
        scaled = (wide * gain).astype(jnp.bfloat16)
        proj = jnp.dot(scaled, w_proj, preferred_element_type=jnp.float32)
        inverse = lax.rsqrt(lax.optimization_barrier(jnp.mean(wide * wide, axis=1)) + 1e-05)[:, None]
        position = (PREFIX + suffix_lengths + step).astype(jnp.float32)
        query = rotate((proj[:, :query_width] * inverse).reshape(SAMPLES, KVH, GROUP, HD), position[:, None, None]).astype(jnp.bfloat16)
        new_keys.append(rotate((proj[:, query_width:query_width + key_width] * inverse).reshape(SAMPLES, KVH, HD), position[:, None]).astype(jnp.bfloat16))
        new_values.append((proj[:, query_width + key_width:] * inverse).reshape(SAMPLES, KVH, HD).astype(jnp.bfloat16))
        fresh_k = jnp.stack(new_keys, axis=1).reshape(PROMPTS, GEN, step + 1, KVH, HD)
        fresh_v = jnp.stack(new_values, axis=1).reshape(PROMPTS, GEN, step + 1, KVH, HD)

        def one_prompt(items):
            query_p, pre_k, pre_v, suf_k, suf_v, length_p, new_k, new_v = items
            qf = query_p.astype(jnp.float32)
            s_pre = jnp.einsum('gkhd,kld->gkhl', qf, pre_k.astype(jnp.float32)) * scale
            s_suf = jnp.einsum('gkhd,gpkjd->gkhpj', qf, suf_k.astype(jnp.float32)).reshape(GEN, KVH, GROUP, SUFFIX) * scale
            live = (jnp.arange(SUFFIX, dtype=jnp.int32)[None, :] < length_p[:, None])[:, None, None, :]
            s_suf = jnp.where(live, s_suf, -jnp.inf)
            s_new = jnp.einsum('gkhd,gukd->gkhu', qf, new_k.astype(jnp.float32)) * scale
            top = jnp.maximum(jnp.maximum(lax.optimization_barrier(jnp.max(s_pre, axis=-1)), lax.optimization_barrier(jnp.max(s_suf, axis=-1))), lax.optimization_barrier(jnp.max(s_new, axis=-1)))
            e_pre = jnp.exp(s_pre - top[..., None])
            e_suf = jnp.exp(s_suf - top[..., None])
            e_new = jnp.exp(s_new - top[..., None])
            total = lax.optimization_barrier(jnp.sum(e_pre, axis=-1)) + lax.optimization_barrier(jnp.sum(e_suf, axis=-1)) + lax.optimization_barrier(jnp.sum(e_new, axis=-1))
            acc = jnp.einsum('gkhl,kld->gkhd', rounded(e_pre), pre_v.astype(jnp.float32))
            acc = acc + jnp.einsum('gkhpj,gpkjd->gkhd', rounded(e_suf).reshape(GEN, KVH, GROUP, PAGES, PAGE), suf_v.astype(jnp.float32))
            acc = acc + jnp.einsum('gkhu,gukd->gkhd', rounded(e_new), new_v.astype(jnp.float32))
            return (acc / total[..., None]).astype(jnp.bfloat16)
        mixed = lax.map(one_prompt, (query.reshape(PROMPTS, GEN, KVH, GROUP, HD), prefix_keys, prefix_values, page_keys, page_values, lengths, fresh_k, fresh_v))
        mixed = mixed.reshape(SAMPLES, query_width)
        delta = jnp.dot(mixed, w_out, preferred_element_type=jnp.float32)
        update = update + delta
        state = (wide + delta).astype(jnp.bfloat16)
    return (state, update)
```

```python
import functools
import math

import jax
import jax.numpy as jnp
import numpy as np
from jax import lax
from jax.experimental import pallas as pl
from jax.experimental.pallas import tpu as pltpu
from jax.sharding import PartitionSpec as P

HD = 128
STEPS = 3
LOW = -1e30
BASE2 = math.log2(math.e) / math.sqrt(HD)
LOG2E = math.log2(math.e)
MESH = pl.DeviceIdType.MESH
F32 = jnp.float32
BF16 = jnp.bfloat16
NT = (((1,), (1,)), ((), ()))
TN = (((0,), (0,)), ((), ()))


def kernel(
    ranks, sides, heads, prompts, kv, group, width,
    lens, table_hbm, x_in, gain, freq, wq, wk, wv, wo, pk, pv, sk, sv,
    h_hbm, u_hbm, c_hbm,
    table, cosine, sine, h_out, u_out, w_s, wo_s, pk_s, pv_s, sk_s, sv_s, bias, send_a, recv_a, own_a, sq_send, sq_recv,
    qkv, fresh_k, fresh_v, outs, lse, recv_b, recv_l, mix, part, cbuf,
    load_sem, send_sem, recv_sem, send_c, recv_c, out_sem,
):
    samples = x_in.shape[0]
    gen = samples // prompts
    own_count = samples // ranks
    q_heads = kv * group
    all_heads = q_heads + 2 * kv
    blocks = all_heads * prompts
    per = qkv.shape[0] // ranks
    unit_rows = group * gen
    units = prompts * kv
    rows = units * unit_rows // ranks
    row_blocks = rows // gen
    span = pk_s.shape[2]
    slots, page = sk_s.shape[0], sk_s.shape[2]
    pages = table.shape[0]
    suffix = slots * page
    own_rows = own_count * group

    me = lax.axis_index("seq") * sides + lax.axis_index("side")
    head_me = lax.axis_index("head")

    def rank_id(d):
        return {"seq": lax.div(d, sides), "side": lax.rem(d, sides)}

    per_unit = group + 2
    owners = per_unit // per
    loads = []
    for k in range(kv):
        base = k * per_unit * HD
        for source, first, count in ((wq, 0, group), (wk, group, 1), (wv, group + 1, 1)):
            loads.append(
                pltpu.make_async_copy(
                    source.at[:, pl.ds(k * count * HD, count * HD)],
                    w_s.at[:, pl.ds(base + first * HD, count * HD)],
                    load_sem.at[len(loads)],
                )
            )
    table_load = pltpu.make_async_copy(table_hbm, table, out_sem.at[0])
    table_load.start()
    for load in loads:
        load.start()
    later = [
        pltpu.make_async_copy(source, target, load_sem.at[len(loads) + n])
        for n, (source, target) in enumerate(
            ((pk, pk_s), (pv, pv_s), (sk, sk_s), (sv, sv_s), (wo, wo_s))
        )
    ]

    barrier = pltpu.get_barrier_semaphore()
    for o in range(1, ranks):
        pl.semaphore_signal(
            barrier, inc=1, device_id=rank_id(lax.rem(me + o, ranks)), device_id_type=MESH
        )
    for o in range(1, heads):
        pl.semaphore_signal(
            barrier, inc=1, device_id={"head": lax.rem(head_me + o, heads)}, device_id_type=MESH
        )

    start = (me + 1 - 2 * lax.rem(me, 2)) * own_count
    own_prompt = lax.div(start, gen)
    own_first = lax.rem(start, gen)
    line = lax.broadcasted_iota(jnp.int32, (own_rows, suffix), 0)
    column = lax.broadcasted_iota(jnp.int32, (own_rows, suffix), 1)
    which = lax.rem(line, own_count)
    slot = lax.div(column, page)
    offset = lax.rem(column, page)
    place = jnp.full((own_rows, suffix), 1 << 28, jnp.int32)
    length = jnp.zeros((own_rows, suffix), jnp.int32)
    table_load.wait()
    table_line = lax.broadcasted_iota(jnp.int32, table.shape, 1)
    for j in range(own_count):
        mine = which == j
        entries = jnp.sum(
            jnp.where(table_line == start + j, table[...], 0), axis=1, keepdims=True
        )
        length = jnp.where(mine, lens[start + j], length)
        for n in range(pages):
            hit = jnp.logical_and(mine, slot == entries[n : n + 1, :])
            place = jnp.where(hit, n * page + offset, place)
    bias[...] = jnp.where(place < length, 0.0, LOW).astype(F32)
    sample_line = lax.broadcasted_iota(jnp.int32, (samples, HD), 0)
    position = jnp.full((samples, HD), span * ranks, jnp.int32)
    for n in range(samples):
        position = jnp.where(sample_line == n, position + lens[n], position)
    low_half = lax.broadcasted_iota(jnp.int32, (samples, HD), 1) < HD // 2
    for n in range(STEPS):
        angle = (position + n).astype(F32) * freq[...]
        turn = jnp.sin(angle)
        cosine[n] = jnp.cos(angle)
        sine[n] = jnp.where(low_half, -turn, turn)
    fresh_k[...] = jnp.zeros_like(fresh_k)
    fresh_v[...] = jnp.zeros_like(fresh_v)
    h_out[...] = x_in[...]
    u_out[...] = jnp.zeros_like(u_out)

    pl.semaphore_wait(barrier, ranks - 1 + heads - 1)

    sel_row = lax.broadcasted_iota(jnp.int32, (own_rows, unit_rows), 0)
    sel_col = lax.broadcasted_iota(jnp.int32, (own_rows, unit_rows), 1)
    target = lax.div(sel_row, own_count) * gen + own_first + lax.rem(sel_row, own_count)
    chosen = jnp.where(sel_col == target, 1.0, 0.0).astype(F32)
    gen_line = lax.broadcasted_iota(jnp.int32, (gen, HD), 0)

    def spread(lines, fill):
        found = []
        for g in range(group):
            value = jnp.full((gen, HD), fill, F32)
            for j in range(own_count):
                row = lines[g * own_count + j : g * own_count + j + 1]
                value = jnp.where(gen_line == own_first + j, row, value)
            found.append(value)
        return jnp.concatenate(found, axis=0)


    my_block = me * row_blocks
    my_unit = lax.div(my_block, group)
    my_q = my_unit * per_unit + lax.rem(my_block, group)
    my_k = my_unit * per_unit + group
    my_shift = lax.rem(me * rows, unit_rows)

    def copy(src, dst, phase, o, d):
        return pltpu.make_async_remote_copy(
            src_ref=src,
            dst_ref=dst,
            send_sem=send_sem.at[phase, o],
            recv_sem=recv_sem.at[phase, o],
            device_id=rank_id(d),
            device_id_type=MESH,
        )

    def sq_copy(o, d):
        return copy(sq_send, sq_recv.at[o], 0, o, d)

    def a_copy(o, d):
        return copy(send_a.at[d], recv_a.at[o], 1, o, d)

    def q_copy(o, d, owner):
        place = qkv.at[pl.ds(owner * per, per)]
        return copy(place, place, 2, o, d)

    def b_copy(o, d):
        return copy(outs.at[pl.ds(pl.multiple_of(d * rows, rows), rows)], recv_b.at[o], 3, o, d)

    def l_copy(o, d):
        return copy(lse.at[lax.div(d * rows, unit_rows)], recv_l.at[o], 4, o, d)

    def m_copy(o, d, owner):
        place = mix.at[pl.ds(owner * row_blocks, row_blocks)]
        return copy(place, place, 5, o, d)

    def c_copy(t, o):
        return pltpu.make_async_remote_copy(
            src_ref=cbuf.at[t, head_me],
            dst_ref=cbuf.at[t, head_me],
            send_sem=send_c.at[t, o],
            recv_sem=recv_c.at[t, o],
            device_id={"head": lax.rem(head_me + o, heads)},
            device_id_type=MESH,
        )

    def c_arrival(t, o):
        source = lax.rem(head_me + heads - o, heads)
        return pltpu.make_async_remote_copy(
            src_ref=cbuf.at[t, source],
            dst_ref=cbuf.at[t, source],
            send_sem=send_c.at[t, o],
            recv_sem=recv_c.at[t, o],
            device_id={"head": source},
            device_id_type=MESH,
        )

    def ahead(o):
        return lax.rem(me + o, ranks)

    def behind(o):
        return lax.rem(me + ranks - o, ranks)

    far_first = sorted(range(1, ranks), key=lambda o: abs(2 * o - ranks))

    def step(t, carry):
        wide = h_out[...].astype(F32)
        scaled = (wide * gain[...]).astype(BF16)
        squares = jnp.sum(wide * wide, axis=1, keepdims=True)
        diag_r = lax.broadcasted_iota(jnp.int32, (samples, HD), 0)
        diag_c = lax.broadcasted_iota(jnp.int32, (samples, HD), 1)
        sq_send[...] = jnp.sum(jnp.where(diag_r == diag_c, squares, 0.0), axis=0, keepdims=True)
        for o in range(1, ranks):
            sq_copy(o, ahead(o)).start()

        @pl.when(t == 0)
        def _():
            for load in loads:
                load.wait()
            for load in later:
                load.start()

        def chunk(d):
            if prompts == 1 and blocks == per * ranks:
                wide_cols = per * HD
                cols = pl.ds(pl.multiple_of(d * wide_cols, wide_cols), wide_cols)
                got = jnp.dot(scaled, w_s[:, cols], preferred_element_type=F32)
                return [got[:, i * HD : (i + 1) * HD] for i in range(per)]
            found = []
            for i in range(per):
                b = jnp.minimum(d * per + i, blocks - 1)
                p = lax.div(b, all_heads)
                cols = pl.ds(pl.multiple_of(lax.rem(b, all_heads) * HD, HD), HD)
                got = jnp.dot(scaled, w_s[:, cols], preferred_element_type=F32)
                pick = got[0:gen]
                for n in range(1, prompts):
                    pick = jnp.where(p == n, got[n * gen : (n + 1) * gen], pick)
                found.append(pick)
            return found

        for o in far_first:
            d = ahead(o)
            for i, piece in enumerate(chunk(d)):
                send_a[d, i] = piece.astype(BF16)
            a_copy(o, d).start()
        for i, piece in enumerate(chunk(me)):
            own_a[i] = piece

        total = sq_send[...]
        for o in range(1, ranks):
            sq_copy(o, ahead(o)).wait_recv()
            total = total + sq_recv[o]
        total = jnp.sum(jnp.where(diag_r == diag_c, total, 0.0), axis=1, keepdims=True)
        inverse = lax.rsqrt(total / width + 1e-05)
        for o in range(1, ranks):
            a_copy(o, ahead(o)).wait_recv()
        for i in range(per):
            value = own_a[i]
            for o in range(1, ranks):
                value = value + recv_a[o, i].astype(F32)
            b = jnp.minimum(me * per + i, blocks - 1)
            p = lax.div(b, all_heads)
            plain = lax.rem(b, per_unit) == per_unit - 1
            inv, cos, sin = inverse[0:gen], cosine[t, 0:gen], sine[t, 0:gen]
            for n in range(1, prompts):
                band = slice(n * gen, (n + 1) * gen)
                inv = jnp.where(p == n, inverse[band], inv)
                cos = jnp.where(p == n, cosine[t, band], cos)
                sin = jnp.where(p == n, sine[t, band], sin)
            value = value * inv
            turned = value * cos + pltpu.roll(value, HD // 2, 1) * sin
            qkv[me * per + i] = jnp.where(plain, value, turned).astype(BF16)
        for o in far_first:
            q_copy(o, ahead(o), me).start()

        def q_arrived(owner):
            @pl.when(owner != me)
            def _():
                q_copy(lax.rem(me - owner + ranks, ranks), owner, owner).wait_recv()

        @pl.when(t == 0)
        def _():
            for load in later[:4]:
                load.wait()

        def unit(i, carry):
            u = lax.rem(my_unit + 2 * lax.div(i, 2), units)
            u = u + lax.rem(i, 2) * (1 - 2 * lax.rem(u, 2))
            for n in range(owners):
                q_arrived(u * owners + n)
            p = lax.div(u, kv)
            k = lax.rem(u, kv)
            q = qkv[pl.ds(u * per_unit, group)].reshape(unit_rows, HD)
            size = min(span, 1024)
            q_own = jnp.dot(chosen.astype(BF16), q, preferred_element_type=F32).astype(BF16)
            scores = [
                lax.dot_general(q, pk_s[p, k, c : c + size], NT, preferred_element_type=F32)
                for c in range(0, span, size)
            ]
            near = lax.dot_general(
                q_own, sk_s[:, k].reshape(suffix, HD), NT, preferred_element_type=F32
            ) + bias[...]

            def soft(s, values):
                top = jnp.max(s, axis=1, keepdims=True)
                e = jnp.exp2((s - top) * BASE2)
                total = jnp.sum(e, axis=1, keepdims=True)
                return top, total, jnp.dot(e.astype(BF16), values, preferred_element_type=F32)

            parts = [
                soft(s, pv_s[p, k, n * size : (n + 1) * size]) for n, s in enumerate(scores)
            ]
            near_top, near_sum, near_acc = soft(near, sv_s[:, k].reshape(suffix, HD))
            near_top = jnp.where(p == own_prompt, near_top, LOW)
            parts.append(
                (
                    spread(jnp.broadcast_to(near_top, (own_rows, HD)), LOW),
                    spread(jnp.broadcast_to(near_sum, (own_rows, HD)), 0.0),
                    spread(near_acc, 0.0),
                )
            )
            best = functools.reduce(jnp.maximum, [part[0] for part in parts])
            amount = jnp.zeros((unit_rows, HD), F32)
            acc = jnp.zeros((unit_rows, HD), F32)
            for part_top, part_sum, part_acc in parts:
                weight = jnp.exp2((part_top - best) * BASE2)
                amount = amount + weight * part_sum
                acc = acc + weight * part_acc
            outs[pl.ds(pl.multiple_of(u * unit_rows, unit_rows), unit_rows)] = (
                acc / amount
            ).astype(BF16)
            level = best * BASE2 + jnp.log(amount) * LOG2E
            eye_r = lax.broadcasted_iota(jnp.int32, (unit_rows, unit_rows), 0)
            eye_c = lax.broadcasted_iota(jnp.int32, (unit_rows, unit_rows), 1)
            lse[u] = jnp.sum(jnp.where(eye_r == eye_c, level, 0.0), axis=0, keepdims=True)
            for j in range(unit_rows // rows):
                d = u * (unit_rows // rows) + j

                @pl.when(d != me)
                def _():
                    o = lax.rem(d - me + ranks, ranks)
                    l_copy(o, d).start()
                    b_copy(o, d).start()

            return carry

        lax.fori_loop(0, units, unit, 0)
        for n in range(units * owners, ranks):
            q_arrived(n)

        fresh_k[t] = qkv[my_k].astype(F32)
        fresh_v[t] = qkv[my_k + 1].astype(F32)
        mine = qkv[pl.ds(my_q, row_blocks)].reshape(rows, HD).astype(F32)
        new_scores = []
        for n in range(STEPS):
            keys = jnp.concatenate([fresh_k[n]] * row_blocks, axis=0)
            s = jnp.sum(mine * keys, axis=1, keepdims=True) * BASE2
            new_scores.append(jnp.where(n <= t, s, LOW))
        pick_r = lax.broadcasted_iota(jnp.int32, (rows, unit_rows), 0)
        pick_c = lax.broadcasted_iota(jnp.int32, (rows, unit_rows), 1)

        def as_column(row):
            return jnp.sum(jnp.where(pick_c == pick_r + my_shift, row, 0.0), axis=1, keepdims=True)

        levels = [as_column(lse[my_unit])]
        for o in range(1, ranks):
            l_copy(o, ahead(o)).wait_recv()
            levels.append(as_column(recv_l[o]))
        best = functools.reduce(jnp.maximum, levels + new_scores)
        amount = jnp.zeros((rows, 1), F32)
        acc = jnp.zeros((rows, HD), F32)
        for n in range(STEPS):
            e = jnp.where(n <= t, jnp.exp2(new_scores[n] - best), 0.0)
            amount = amount + e
            acc = acc + e * jnp.concatenate([fresh_v[n]] * row_blocks, axis=0)
        for o in range(ranks):
            e = jnp.exp2(levels[o] - best)
            amount = amount + e
            if o == 0:
                got = outs[pl.ds(pl.multiple_of(me * rows, rows), rows)]
            else:
                b_copy(o, ahead(o)).wait_recv()
                got = recv_b[o]
            acc = acc + e * got.astype(F32)
        mix[pl.ds(my_block, row_blocks)] = (
            (acc / amount).astype(BF16).reshape(row_blocks, gen, HD)
        )
        for o in far_first:
            m_copy(o, ahead(o), me).start()

        @pl.when(t == 0)
        def _():
            later[4].wait()

        part[...] = jnp.zeros_like(part)
        for o in [0] + far_first[::-1]:
            d = behind(o)
            if o > 0:
                m_copy(o, ahead(o), d).wait_recv()
            b = d * row_blocks
            p = lax.div(b, q_heads)
            left = jnp.concatenate([mix[b + i] for i in range(row_blocks)], axis=1)
            depth = row_blocks * HD
            right = wo_s[pl.ds(pl.multiple_of(lax.rem(b, q_heads) * HD, HD), depth)]
            band = pl.ds(pl.multiple_of(p * gen, gen), gen)
            part[band] += jnp.dot(left, right, preferred_element_type=F32)
        cbuf[t, head_me] = part[...].astype(BF16)
        for o in range(1, heads):
            c_copy(t, o).start()
        for o in range(1, ranks):
            sq_copy(o, ahead(o)).wait_send()
            a_copy(o, ahead(o)).wait_send()
            q_copy(o, ahead(o), me).wait_send()
            l_copy(o, ahead(o)).wait_send()
            b_copy(o, ahead(o)).wait_send()
            m_copy(o, ahead(o), me).wait_send()
        for o in range(1, heads):
            c_arrival(t, o).wait_recv()

        @pl.when(t < STEPS - 1)
        def _():
            delta = cbuf[t, 0].astype(F32)
            for n in range(1, heads):
                delta = delta + cbuf[t, n].astype(F32)
            u_out[...] += delta
            h_out[...] = (h_out[...].astype(F32) + delta).astype(BF16)

        for o in range(1, heads):
            c_copy(t, o).wait_send()
        return carry

    lax.fori_loop(0, STEPS, step, 0)
    stores = [
        pltpu.make_async_copy(h_out, h_hbm, out_sem.at[0]),
        pltpu.make_async_copy(u_out, u_hbm, out_sem.at[1]),
        pltpu.make_async_copy(cbuf.at[STEPS - 1], c_hbm, out_sem.at[2]),
    ]
    for store in stores:
        store.start()
    for store in stores:
        store.wait()


def local(
    ranks, sides, heads,
    hidden, gain, w_query, w_key, w_value, w_out, prefix_keys, prefix_values,
    suffix_keys, suffix_values, suffix_lengths, page_table,
):
    samples, depth = hidden.shape
    prompts, kv, span, _ = prefix_keys.shape
    group = w_query.shape[1] // w_key.shape[1]
    gen = samples // prompts
    slots, _, page, _ = suffix_keys.shape
    own_rows = samples // ranks * group
    all_heads = kv * (group + 2)
    per = -(-all_heads * prompts // ranks)
    unit_rows = group * gen
    units = prompts * kv
    rows = units * unit_rows // ranks

    power = -np.arange(HD // 2, dtype=np.float64) * 2.0 / HD
    freq = np.tile(500000.0 ** power, 2).astype(np.float32).reshape(1, HD)

    vmem = pl.BlockSpec(memory_space=pltpu.VMEM)
    smem = pl.BlockSpec(memory_space=pltpu.SMEM)
    hbm = pl.BlockSpec(memory_space=pl.ANY)
    store = pl.BlockSpec(memory_space=pltpu.HBM)
    held, added, last = pl.pallas_call(
        functools.partial(
            kernel, ranks, sides, heads, prompts, kv, group, float(depth * ranks)
        ),
        out_shape=(
            jax.ShapeDtypeStruct((samples, depth), BF16),
            jax.ShapeDtypeStruct((samples, depth), F32),
            jax.ShapeDtypeStruct((heads, samples, depth), BF16),
        ),
        in_specs=[smem, store] + [vmem] * 3 + [hbm] * 8,
        out_specs=(store, store, store),
        scratch_shapes=[
            pltpu.VMEM(page_table.shape[::-1], jnp.int32),
            pltpu.VMEM((STEPS, samples, HD), F32),
            pltpu.VMEM((STEPS, samples, HD), F32),
            pltpu.VMEM((samples, depth), BF16),
            pltpu.VMEM((samples, depth), F32),
            pltpu.VMEM((depth, all_heads * HD), BF16),
            pltpu.VMEM(w_out.shape, BF16),
            pltpu.VMEM(prefix_keys.shape, BF16),
            pltpu.VMEM(prefix_values.shape, BF16),
            pltpu.VMEM(suffix_keys.shape, BF16),
            pltpu.VMEM(suffix_values.shape, BF16),
            pltpu.VMEM((own_rows, slots * page), F32),
            pltpu.VMEM((ranks, per, gen, HD), BF16),
            pltpu.VMEM((ranks, per, gen, HD), BF16),
            pltpu.VMEM((per, gen, HD), F32),
            pltpu.VMEM((1, HD), F32),
            pltpu.VMEM((ranks, 1, HD), F32),
            pltpu.VMEM((ranks * per, gen, HD), BF16),
            pltpu.VMEM((STEPS, gen, HD), F32),
            pltpu.VMEM((STEPS, gen, HD), F32),
            pltpu.VMEM((units * unit_rows, HD), BF16),
            pltpu.VMEM((units, 1, unit_rows), F32),
            pltpu.VMEM((ranks, rows, HD), BF16),
            pltpu.VMEM((ranks, 1, unit_rows), F32),
            pltpu.VMEM((prompts * kv * group, gen, HD), BF16),
            pltpu.VMEM((samples, depth), F32),
            pltpu.VMEM((STEPS, heads, samples, depth), BF16),
            pltpu.SemaphoreType.DMA((3 * kv + 5,)),
            pltpu.SemaphoreType.DMA((6, ranks)),
            pltpu.SemaphoreType.DMA((6, ranks)),
            pltpu.SemaphoreType.DMA((STEPS, heads)),
            pltpu.SemaphoreType.DMA((STEPS, heads)),
            pltpu.SemaphoreType.DMA((3,)),
        ],
        compiler_params=pltpu.CompilerParams(
            collective_id=0, has_side_effects=True, vmem_limit_bytes=60 * 1024 * 1024
        ),
    )(
        suffix_lengths, page_table.T, hidden, gain.reshape(1, depth), freq,
        w_query, w_key, w_value, w_out, prefix_keys, prefix_values, suffix_keys, suffix_values,
    )
    delta = last[0].astype(F32)
    for n in range(1, heads):
        delta = delta + last[n].astype(F32)
    return (held.astype(F32) + delta).astype(BF16), added + delta


def solution(mesh):
    placed = (
        P("groups", ("seq", "side")),
        P(("seq", "side")),
        P(("seq", "side"), "head"),
        P(("seq", "side"), "head"),
        P(("seq", "side"), "head"),
        P("head", ("seq", "side")),
        P("groups", "head", ("seq", "side"), None),
        P("groups", "head", ("seq", "side"), None),
        P(("groups", "seq", "side"), "head", None, None),
        P(("groups", "seq", "side"), "head", None, None),
        P("groups"),
        P("groups", None),
    )
    ranks = mesh.shape["seq"] * mesh.shape["side"]
    return jax.shard_map(
        functools.partial(local, ranks, mesh.shape["side"], mesh.shape["head"]),
        mesh=mesh,
        in_specs=placed,
        out_specs=(P("groups", ("seq", "side")), P("groups", ("seq", "side"))),
        check_vma=False,
    )
```

```python
import functools
import math

import jax
import jax.numpy as jnp
import numpy as np
from jax import lax
from jax.experimental import pallas as pl
from jax.experimental.pallas import tpu as pltpu
from jax.sharding import PartitionSpec as P

HD = 128
STEPS = 3
LOW = -1e30
BASE2 = math.log2(math.e) / math.sqrt(HD)
LOG2E = math.log2(math.e)
MESH = pl.DeviceIdType.MESH
F32 = jnp.float32
BF16 = jnp.bfloat16
NT = (((1,), (1,)), ((), ()))
TN = (((0,), (0,)), ((), ()))


def kernel(
    ranks, sides, heads, prompts, kv, group, width,
    lens, table_hbm, x_in, gain, freq, wq, wk, wv, wo, pk, pv, sk, sv,
    h_hbm, u_hbm, c_hbm,
    table, cosine, sine, h_out, u_out, w_s, wo_s, pk_s, pv_s, sk_s, sv_s, bias, send_a, recv_a, own_a, sq_send, sq_recv,
    qkv, fresh_k, fresh_v, outs, lse, recv_b, recv_l, mix, part, cbuf,
    load_sem, send_sem, recv_sem, send_c, recv_c, out_sem,
):
    samples = x_in.shape[0]
    gen = samples // prompts
    own_count = samples // ranks
    q_heads = kv * group
    all_heads = q_heads + 2 * kv
    blocks = all_heads * prompts
    per = qkv.shape[0] // ranks
    unit_rows = group * gen
    units = prompts * kv
    rows = units * unit_rows // ranks
    row_blocks = rows // gen
    span = pk_s.shape[2]
    slots, page = sk_s.shape[0], sk_s.shape[2]
    pages = table.shape[0]
    suffix = slots * page
    own_rows = own_count * group

    me = lax.axis_index("seq") * sides + lax.axis_index("side")
    head_me = lax.axis_index("head")

    def rank_id(d):
        return {"seq": lax.div(d, sides), "side": lax.rem(d, sides)}

    per_unit = group + 2
    owners = per_unit // per
    loads = []
    for k in range(kv):
        base = k * per_unit * HD
        for source, first, count in ((wq, 0, group), (wk, group, 1), (wv, group + 1, 1)):
            loads.append(
                pltpu.make_async_copy(
                    source.at[:, pl.ds(k * count * HD, count * HD)],
                    w_s.at[:, pl.ds(base + first * HD, count * HD)],
                    load_sem.at[len(loads)],
                )
            )
    table_load = pltpu.make_async_copy(table_hbm, table, out_sem.at[0])
    table_load.start()
    for load in loads:
        load.start()
    later = [
        pltpu.make_async_copy(source, target, load_sem.at[len(loads) + n])
        for n, (source, target) in enumerate(
            ((pk, pk_s), (pv, pv_s), (sk, sk_s), (sv, sv_s), (wo, wo_s))
        )
    ]

    barrier = pltpu.get_barrier_semaphore()
    for o in range(1, ranks):
        pl.semaphore_signal(
            barrier, inc=1, device_id=rank_id(lax.rem(me + o, ranks)), device_id_type=MESH
        )
    for o in range(1, heads):
        pl.semaphore_signal(
            barrier, inc=1, device_id={"head": lax.rem(head_me + o, heads)}, device_id_type=MESH
        )

    start = (me + 1 - 2 * lax.rem(me, 2)) * own_count
    own_prompt = lax.div(start, gen)
    own_first = lax.rem(start, gen)
    line = lax.broadcasted_iota(jnp.int32, (own_rows, suffix), 0)
    column = lax.broadcasted_iota(jnp.int32, (own_rows, suffix), 1)
    which = lax.rem(line, own_count)
    slot = lax.div(column, page)
    offset = lax.rem(column, page)
    place = jnp.full((own_rows, suffix), 1 << 28, jnp.int32)
    length = jnp.zeros((own_rows, suffix), jnp.int32)
    table_load.wait()
    table_line = lax.broadcasted_iota(jnp.int32, table.shape, 1)
    for j in range(own_count):
        mine = which == j
        entries = jnp.sum(
            jnp.where(table_line == start + j, table[...], 0), axis=1, keepdims=True
        )
        length = jnp.where(mine, lens[start + j], length)
        for n in range(pages):
            hit = jnp.logical_and(mine, slot == entries[n : n + 1, :])
            place = jnp.where(hit, n * page + offset, place)
    bias[...] = jnp.where(place < length, 0.0, LOW).astype(F32)
    sample_line = lax.broadcasted_iota(jnp.int32, (samples, HD), 0)
    position = jnp.full((samples, HD), span * ranks, jnp.int32)
    for n in range(samples):
        position = jnp.where(sample_line == n, position + lens[n], position)
    low_half = lax.broadcasted_iota(jnp.int32, (samples, HD), 1) < HD // 2
    for n in range(STEPS):
        angle = (position + n).astype(F32) * freq[...]
        turn = jnp.sin(angle)
        cosine[n] = jnp.cos(angle)
        sine[n] = jnp.where(low_half, -turn, turn)
    fresh_k[...] = jnp.zeros_like(fresh_k)
    fresh_v[...] = jnp.zeros_like(fresh_v)
    h_out[...] = x_in[...]
    u_out[...] = jnp.zeros_like(u_out)

    pl.semaphore_wait(barrier, ranks - 1 + heads - 1)

    sel_row = lax.broadcasted_iota(jnp.int32, (own_rows, unit_rows), 0)
    sel_col = lax.broadcasted_iota(jnp.int32, (own_rows, unit_rows), 1)
    target = lax.div(sel_row, own_count) * gen + own_first + lax.rem(sel_row, own_count)
    chosen = jnp.where(sel_col == target, 1.0, 0.0).astype(F32)
    gen_line = lax.broadcasted_iota(jnp.int32, (gen, HD), 0)

    def spread(lines, fill):
        found = []
        for g in range(group):
            value = jnp.full((gen, HD), fill, F32)
            for j in range(own_count):
                row = lines[g * own_count + j : g * own_count + j + 1]
                value = jnp.where(gen_line == own_first + j, row, value)
            found.append(value)
        return jnp.concatenate(found, axis=0)


    my_block = me * row_blocks
    my_unit = lax.div(my_block, group)
    my_q = my_unit * per_unit + lax.rem(my_block, group)
    my_k = my_unit * per_unit + group
    my_shift = lax.rem(me * rows, unit_rows)

    def copy(src, dst, phase, o, d):
        return pltpu.make_async_remote_copy(
            src_ref=src,
            dst_ref=dst,
            send_sem=send_sem.at[phase, o],
            recv_sem=recv_sem.at[phase, o],
            device_id=rank_id(d),
            device_id_type=MESH,
        )

    def sq_copy(o, d):
        return copy(sq_send, sq_recv.at[o], 0, o, d)

    def a_copy(o, d):
        return copy(send_a.at[d], recv_a.at[o], 1, o, d)

    def q_copy(o, d, owner):
        place = qkv.at[pl.ds(owner * per, per)]
        return copy(place, place, 2, o, d)

    def b_copy(o, d):
        return copy(outs.at[pl.ds(pl.multiple_of(d * rows, rows), rows)], recv_b.at[o], 3, o, d)

    def l_copy(o, d):
        return copy(lse.at[lax.div(d * rows, unit_rows)], recv_l.at[o], 4, o, d)

    def m_copy(o, d, owner):
        place = mix.at[pl.ds(owner * row_blocks, row_blocks)]
        return copy(place, place, 5, o, d)

    def c_copy(t, o):
        return pltpu.make_async_remote_copy(
            src_ref=cbuf.at[t, head_me],
            dst_ref=cbuf.at[t, head_me],
            send_sem=send_c.at[t, o],
            recv_sem=recv_c.at[t, o],
            device_id={"head": lax.rem(head_me + o, heads)},
            device_id_type=MESH,
        )

    def c_arrival(t, o):
        source = lax.rem(head_me + heads - o, heads)
        return pltpu.make_async_remote_copy(
            src_ref=cbuf.at[t, source],
            dst_ref=cbuf.at[t, source],
            send_sem=send_c.at[t, o],
            recv_sem=recv_c.at[t, o],
            device_id={"head": source},
            device_id_type=MESH,
        )

    def ahead(o):
        return lax.rem(me + o, ranks)

    def behind(o):
        return lax.rem(me + ranks - o, ranks)

    far_first = sorted(range(1, ranks), key=lambda o: abs(2 * o - ranks))

    def step(t, carry):
        wide = h_out[...].astype(F32)
        scaled = (wide * gain[...]).astype(BF16)
        squares = jnp.sum(wide * wide, axis=1, keepdims=True)
        diag_r = lax.broadcasted_iota(jnp.int32, (samples, HD), 0)
        diag_c = lax.broadcasted_iota(jnp.int32, (samples, HD), 1)
        sq_send[...] = jnp.sum(jnp.where(diag_r == diag_c, squares, 0.0), axis=0, keepdims=True)
        for o in range(1, ranks):
            sq_copy(o, ahead(o)).start()

        @pl.when(t == 0)
        def _():
            for load in loads:
                load.wait()
            for load in later:
                load.start()

        def chunk(d):
            if prompts == 1 and blocks == per * ranks:
                wide_cols = per * HD
                cols = pl.ds(pl.multiple_of(d * wide_cols, wide_cols), wide_cols)
                got = jnp.dot(scaled, w_s[:, cols], preferred_element_type=F32)
                return [got[:, i * HD : (i + 1) * HD] for i in range(per)]
            found = []
            for i in range(per):
                b = jnp.minimum(d * per + i, blocks - 1)
                p = lax.div(b, all_heads)
                cols = pl.ds(pl.multiple_of(lax.rem(b, all_heads) * HD, HD), HD)
                got = jnp.dot(scaled, w_s[:, cols], preferred_element_type=F32)
                pick = got[0:gen]
                for n in range(1, prompts):
                    pick = jnp.where(p == n, got[n * gen : (n + 1) * gen], pick)
                found.append(pick)
            return found

        for o in far_first:
            d = ahead(o)
            for i, piece in enumerate(chunk(d)):
                send_a[d, i] = piece.astype(BF16)
            a_copy(o, d).start()
        for i, piece in enumerate(chunk(me)):
            own_a[i] = piece

        total = sq_send[...]
        for o in range(1, ranks):
            sq_copy(o, ahead(o)).wait_recv()
            total = total + sq_recv[o]
        total = jnp.sum(jnp.where(diag_r == diag_c, total, 0.0), axis=1, keepdims=True)
        inverse = lax.rsqrt(total / width + 1e-05)
        for o in range(1, ranks):
            a_copy(o, ahead(o)).wait_recv()
        for i in range(per):
            value = own_a[i]
            for o in range(1, ranks):
                value = value + recv_a[o, i].astype(F32)
            b = jnp.minimum(me * per + i, blocks - 1)
            p = lax.div(b, all_heads)
            plain = lax.rem(b, per_unit) == per_unit - 1
            inv, cos, sin = inverse[0:gen], cosine[t, 0:gen], sine[t, 0:gen]
            for n in range(1, prompts):
                band = slice(n * gen, (n + 1) * gen)
                inv = jnp.where(p == n, inverse[band], inv)
                cos = jnp.where(p == n, cosine[t, band], cos)
                sin = jnp.where(p == n, sine[t, band], sin)
            value = value * inv
            turned = value * cos + pltpu.roll(value, HD // 2, 1) * sin
            qkv[me * per + i] = jnp.where(plain, value, turned).astype(BF16)
        for o in far_first:
            q_copy(o, ahead(o), me).start()

        def q_arrived(owner):
            @pl.when(owner != me)
            def _():
                q_copy(lax.rem(me - owner + ranks, ranks), owner, owner).wait_recv()

        @pl.when(t == 0)
        def _():
            for load in later[:4]:
                load.wait()

        def unit(i, carry):
            u = lax.rem(my_unit + 2 * lax.div(i, 2), units)
            u = u + lax.rem(i, 2) * (1 - 2 * lax.rem(u, 2))
            for n in range(owners):
                q_arrived(u * owners + n)
            p = lax.div(u, kv)
            k = lax.rem(u, kv)
            q = qkv[pl.ds(u * per_unit, group)].reshape(unit_rows, HD)
            size = min(span, 1024)
            q_own = jnp.dot(chosen.astype(BF16), q, preferred_element_type=F32).astype(BF16)
            scores = [
                lax.dot_general(q, pk_s[p, k, c : c + size], NT, preferred_element_type=F32)
                for c in range(0, span, size)
            ]
            near = lax.dot_general(
                q_own, sk_s[:, k].reshape(suffix, HD), NT, preferred_element_type=F32
            ) + bias[...]

            def soft(s, values):
                top = jnp.max(s, axis=1, keepdims=True)
                e = jnp.exp2((s - top) * BASE2)
                total = jnp.sum(e, axis=1, keepdims=True)
                return top, total, jnp.dot(e.astype(BF16), values, preferred_element_type=F32)

            parts = [
                soft(s, pv_s[p, k, n * size : (n + 1) * size]) for n, s in enumerate(scores)
            ]
            near_top, near_sum, near_acc = soft(near, sv_s[:, k].reshape(suffix, HD))
            near_top = jnp.where(p == own_prompt, near_top, LOW)
            parts.append(
                (
                    spread(jnp.broadcast_to(near_top, (own_rows, HD)), LOW),
                    spread(jnp.broadcast_to(near_sum, (own_rows, HD)), 0.0),
                    spread(near_acc, 0.0),
                )
            )
            best = functools.reduce(jnp.maximum, [part[0] for part in parts])
            amount = jnp.zeros((unit_rows, HD), F32)
            acc = jnp.zeros((unit_rows, HD), F32)
            for part_top, part_sum, part_acc in parts:
                weight = jnp.exp2((part_top - best) * BASE2)
                amount = amount + weight * part_sum
                acc = acc + weight * part_acc
            outs[pl.ds(pl.multiple_of(u * unit_rows, unit_rows), unit_rows)] = (
                acc / amount
            ).astype(BF16)
            level = best * BASE2 + jnp.log(amount) * LOG2E
            eye_r = lax.broadcasted_iota(jnp.int32, (unit_rows, unit_rows), 0)
            eye_c = lax.broadcasted_iota(jnp.int32, (unit_rows, unit_rows), 1)
            lse[u] = jnp.sum(jnp.where(eye_r == eye_c, level, 0.0), axis=0, keepdims=True)
            for j in range(unit_rows // rows):
                d = u * (unit_rows // rows) + j

                @pl.when(d != me)
                def _():
                    o = lax.rem(d - me + ranks, ranks)
                    l_copy(o, d).start()
                    b_copy(o, d).start()

            return carry

        lax.fori_loop(0, units, unit, 0)
        for n in range(units * owners, ranks):
            q_arrived(n)

        fresh_k[t] = qkv[my_k].astype(F32)
        fresh_v[t] = qkv[my_k + 1].astype(F32)
        mine = qkv[pl.ds(my_q, row_blocks)].reshape(rows, HD).astype(F32)
        new_scores = []
        for n in range(STEPS):
            keys = jnp.concatenate([fresh_k[n]] * row_blocks, axis=0)
            s = jnp.sum(mine * keys, axis=1, keepdims=True) * BASE2
            new_scores.append(jnp.where(n <= t, s, LOW))
        pick_r = lax.broadcasted_iota(jnp.int32, (rows, unit_rows), 0)
        pick_c = lax.broadcasted_iota(jnp.int32, (rows, unit_rows), 1)

        def as_column(row):
            return jnp.sum(jnp.where(pick_c == pick_r + my_shift, row, 0.0), axis=1, keepdims=True)

        levels = [as_column(lse[my_unit])]
        for o in range(1, ranks):
            l_copy(o, ahead(o)).wait_recv()
            levels.append(as_column(recv_l[o]))
        best = functools.reduce(jnp.maximum, levels + new_scores)
        amount = jnp.zeros((rows, 1), F32)
        acc = jnp.zeros((rows, HD), F32)
        for n in range(STEPS):
            e = jnp.where(n <= t, jnp.exp2(new_scores[n] - best), 0.0)
            amount = amount + e
            acc = acc + e * jnp.concatenate([fresh_v[n]] * row_blocks, axis=0)
        for o in range(ranks):
            e = jnp.exp2(levels[o] - best)
            amount = amount + e
            if o == 0:
                got = outs[pl.ds(pl.multiple_of(me * rows, rows), rows)]
            else:
                b_copy(o, ahead(o)).wait_recv()
                got = recv_b[o]
            acc = acc + e * got.astype(F32)
        mix[pl.ds(my_block, row_blocks)] = (
            (acc / amount).astype(BF16).reshape(row_blocks, gen, HD)
        )
        for o in far_first:
            m_copy(o, ahead(o), me).start()

        @pl.when(t == 0)
        def _():
            later[4].wait()

        part[...] = jnp.zeros_like(part)
        for o in [0] + far_first[::-1]:
            d = behind(o)
            if o > 0:
                m_copy(o, ahead(o), d).wait_recv()
            b = d * row_blocks
            p = lax.div(b, q_heads)
            left = jnp.concatenate([mix[b + i] for i in range(row_blocks)], axis=1)
            depth = row_blocks * HD
            right = wo_s[pl.ds(pl.multiple_of(lax.rem(b, q_heads) * HD, HD), depth)]
            band = pl.ds(pl.multiple_of(p * gen, gen), gen)
            part[band] += jnp.dot(left, right, preferred_element_type=F32)
        cbuf[t, head_me] = part[...].astype(BF16)
        for o in range(1, heads):
            c_copy(t, o).start()
        for o in range(1, ranks):
            sq_copy(o, ahead(o)).wait_send()
            a_copy(o, ahead(o)).wait_send()
            q_copy(o, ahead(o), me).wait_send()
            l_copy(o, ahead(o)).wait_send()
            b_copy(o, ahead(o)).wait_send()
            m_copy(o, ahead(o), me).wait_send()
        for o in range(1, heads):
            c_arrival(t, o).wait_recv()

        @pl.when(t < STEPS - 1)
        def _():
            delta = cbuf[t, 0].astype(F32)
            for n in range(1, heads):
                delta = delta + cbuf[t, n].astype(F32)
            u_out[...] += delta
            h_out[...] = (h_out[...].astype(F32) + delta).astype(BF16)

        for o in range(1, heads):
            c_copy(t, o).wait_send()
        return carry

    lax.fori_loop(0, STEPS, step, 0)
    stores = [
        pltpu.make_async_copy(h_out, h_hbm, out_sem.at[0]),
        pltpu.make_async_copy(u_out, u_hbm, out_sem.at[1]),
        pltpu.make_async_copy(cbuf.at[STEPS - 1], c_hbm, out_sem.at[2]),
    ]
    for store in stores:
        store.start()
    for store in stores:
        store.wait()


def chip_kernel(
    chips, sides, heads, kv, group, width,
    lens, table_hbm, x_in, gain, freq, wq, wk, wv, wo, pk, pv, sk, sv,
    h_hbm, u_hbm, c_hbm,
    table, cosine, sine, h_out, u_out, w_s, wo_s, pk_s, pv_s, sk_s, sv_s, bias,
    send_a, recv_a, own_a, sq_send, sq_recv, qkv, fresh_k, fresh_v,
    box_o, box_l, got_o, got_l, zone, zone_l, zone_c, mix, cbuf,
    load_sem, send_sem, recv_sem, send_p, recv_p, send_z, recv_z, send_m, recv_m,
    send_c, recv_c, out_sem,
):
    samples = x_in.shape[0]
    depth = x_in.shape[1]
    gen = samples
    ranks = chips * sides
    own_count = samples // ranks
    per_unit = group + 2
    per = per_unit // sides
    unit_rows = group * gen
    pairs = kv // 2
    span = pk_s.shape[2]
    slots, page = sk_s.shape[0], sk_s.shape[2]
    pages = table.shape[0]
    suffix = slots * page
    own_rows = own_count * group
    pieces = recv_c.shape[2]
    piece = depth // pieces

    z = lax.axis_index("seq")
    side = lax.axis_index("side")
    me = z * sides + side
    head_me = lax.axis_index("head")
    order = list(range(chips - 1, -1, -1))
    peers = [(x, y) for x in order for y in range(sides) if x or y]

    def flip(v, x):
        bit = 1
        while bit <= x:
            if x & bit:
                v = v + bit * (1 - 2 * lax.rem(lax.div(v, bit), 2))
            bit *= 2
        return v

    def peer_rank(x, y):
        return flip(z, x) * sides + flip(side, y)

    def rank_id(d):
        return {"seq": lax.div(d, sides), "side": lax.rem(d, sides)}

    unit_width = per_unit * HD

    def w_loads(u):
        found = []
        base = u * unit_width
        for n, (source, first, count) in enumerate(((wq, 0, group), (wk, group, 1), (wv, group + 1, 1))):
            found.append(
                pltpu.make_async_copy(
                    source.at[:, pl.ds(pl.multiple_of(u * count * HD, HD), count * HD)],
                    w_s.at[:, pl.ds(pl.multiple_of(base + first * HD, HD), count * HD)],
                    load_sem.at[u * 3 + n],
                )
            )
        return found

    for x in order:
        for load in w_loads(flip(z, x)):
            load.start()
    table_load = pltpu.make_async_copy(table_hbm, table, out_sem.at[0])
    table_load.start()
    later = [
        pltpu.make_async_copy(source, target, load_sem.at[3 * kv + n])
        for n, (source, target) in enumerate(
            ((pk, pk_s), (pv, pv_s), (sk, sk_s), (sv, sv_s), (wo, wo_s))
        )
    ]

    barrier = pltpu.get_barrier_semaphore()
    for x, y in peers:
        pl.semaphore_signal(
            barrier, inc=1, device_id=rank_id(peer_rank(x, y)), device_id_type=MESH
        )
    for o in range(1, heads):
        pl.semaphore_signal(
            barrier, inc=1, device_id={"head": lax.rem(head_me + o, heads)}, device_id_type=MESH
        )

    h_out[...] = x_in[...]
    u_out[...] = jnp.zeros_like(u_out)
    fresh_k[...] = jnp.zeros_like(fresh_k)
    fresh_v[...] = jnp.zeros_like(fresh_v)
    start = (me + 1 - 2 * lax.rem(me, 2)) * own_count

    def prepare():
        sample_line = lax.broadcasted_iota(jnp.int32, (samples, HD), 0)
        position = jnp.full((samples, HD), span * ranks, jnp.int32)
        for n in range(samples):
            position = jnp.where(sample_line == n, position + lens[n], position)
        low_half = lax.broadcasted_iota(jnp.int32, (samples, HD), 1) < HD // 2
        for n in range(STEPS):
            angle = (position + n).astype(F32) * freq[...]
            turn = jnp.sin(angle)
            cosine[n] = jnp.cos(angle)
            sine[n] = jnp.where(low_half, -turn, turn)
        line = lax.broadcasted_iota(jnp.int32, (own_rows, suffix), 0)
        column = lax.broadcasted_iota(jnp.int32, (own_rows, suffix), 1)
        which = lax.rem(line, own_count)
        slot = lax.div(column, page)
        offset = lax.rem(column, page)
        place = jnp.full((own_rows, suffix), 1 << 28, jnp.int32)
        length = jnp.zeros((own_rows, suffix), jnp.int32)
        table_load.wait()
        table_line = lax.broadcasted_iota(jnp.int32, table.shape, 1)
        for j in range(own_count):
            mine = which == j
            entries = jnp.sum(
                jnp.where(table_line == start + j, table[...], 0), axis=1, keepdims=True
            )
            length = jnp.where(mine, lens[start + j], length)
            for n in range(pages):
                hit = jnp.logical_and(mine, slot == entries[n : n + 1, :])
                place = jnp.where(hit, n * page + offset, place)
        bias[...] = jnp.where(place < length, 0.0, LOW).astype(F32)

    pl.semaphore_wait(barrier, ranks - 1 + heads - 1)

    sel_row = lax.broadcasted_iota(jnp.int32, (own_rows, unit_rows), 0)
    sel_col = lax.broadcasted_iota(jnp.int32, (own_rows, unit_rows), 1)
    target = lax.div(sel_row, own_count) * gen + start + lax.rem(sel_row, own_count)
    chosen = jnp.where(sel_col == target, 1.0, 0.0).astype(BF16)
    gen_line = lax.broadcasted_iota(jnp.int32, (gen, HD), 0)

    def spread(lines, fill):
        found = []
        for g in range(group):
            value = jnp.full((gen, HD), fill, F32)
            for j in range(own_count):
                row = lines[g * own_count + j : g * own_count + j + 1]
                value = jnp.where(gen_line == start + j, row, value)
            found.append(value)
        return jnp.concatenate(found, axis=0)

    def eye():
        rows = lax.broadcasted_iota(jnp.int32, (unit_rows, unit_rows), 0)
        return rows == lax.broadcasted_iota(jnp.int32, (unit_rows, unit_rows), 1)

    def push(src, dst, phase, x, y):
        return pltpu.make_async_remote_copy(
            src_ref=src,
            dst_ref=dst,
            send_sem=send_sem.at[phase, x * sides + y],
            recv_sem=recv_sem.at[phase, me],
            device_id=rank_id(peer_rank(x, y)),
            device_id_type=MESH,
        )

    def arrived(dst, phase, source):
        pltpu.make_async_remote_copy(
            src_ref=dst,
            dst_ref=dst,
            send_sem=send_sem.at[phase, 0],
            recv_sem=recv_sem.at[phase, source],
            device_id=rank_id(source),
            device_id_type=MESH,
        ).wait_recv()

    def sq_copy(x, y):
        return push(sq_send, sq_recv.at[me], 0, x, y)

    def a_copy(x, y):
        return push(
            send_a.at[x, pl.ds(flip(side, y) * per, per)], recv_a.at[me], 1, x, y
        )

    def q_copy(x, y):
        place = qkv.at[pl.ds(me * per, per)]
        return push(place, place, 2, x, y)

    def p_copy(j, n):
        src, dst = ((box_o, got_o), (box_l, got_l))[n]
        return pltpu.make_async_remote_copy(
            src_ref=src.at[j, 1],
            dst_ref=dst.at[j],
            send_sem=send_p.at[j, n],
            recv_sem=recv_p.at[j, n],
            device_id={"side": 1 - side},
            device_id_type=MESH,
        )

    def z_copy(v, x, n, source, dest):
        buffer = (zone_l, zone)[n]
        return pltpu.make_async_remote_copy(
            src_ref=buffer.at[v, source],
            dst_ref=buffer.at[v, source],
            send_sem=send_z.at[v, x, n],
            recv_sem=recv_z.at[v, source, n],
            device_id={"seq": dest},
            device_id_type=MESH,
        )

    def m_copy(v, owner):
        place = mix.at[pl.ds((2 * v + owner) * group, group)]
        return pltpu.make_async_remote_copy(
            src_ref=place,
            dst_ref=place,
            send_sem=send_m.at[v],
            recv_sem=recv_m.at[v],
            device_id={"side": 1 - side},
            device_id_type=MESH,
        )

    def c_copy(t, o, n, source, dest):
        place = cbuf.at[t, source, :, pl.ds(n * piece, piece)]
        return pltpu.make_async_remote_copy(
            src_ref=place,
            dst_ref=place,
            send_sem=send_c.at[t, o, n],
            recv_sem=recv_c.at[t, o, n],
            device_id={"head": dest},
            device_id_type=MESH,
        )

    def c_send(t, o, n):
        return c_copy(t, o, n, head_me, lax.rem(head_me + o, heads))

    def c_arrival(t, o, n):
        source = lax.rem(head_me + heads - o, heads)
        return c_copy(t, o, n, source, source)

    def out_part(u, first, count):
        left = jnp.concatenate([mix[u * group + i] for i in range(group)], axis=1)
        rows = pl.ds(pl.multiple_of(u * group * HD, HD), group * HD)
        return jnp.dot(
            left, wo_s[rows, first : first + count], preferred_element_type=F32
        )

    def step(t, carry):
        wide = h_out[...].astype(F32)
        scaled = (wide * gain[...]).astype(BF16)
        squares = jnp.sum(wide * wide, axis=1, keepdims=True)
        diag_r = lax.broadcasted_iota(jnp.int32, (samples, HD), 0)
        diag_c = lax.broadcasted_iota(jnp.int32, (samples, HD), 1)
        sq_send[...] = jnp.sum(jnp.where(diag_r == diag_c, squares, 0.0), axis=0, keepdims=True)
        for x, y in peers:
            sq_copy(x, y).start()

        for x in order:
            u = flip(z, x)

            @pl.when(t == 0)
            def _():
                for load in w_loads(u):
                    load.wait()

            cols = pl.ds(pl.multiple_of(u * unit_width, HD), unit_width)
            got = jnp.dot(scaled, w_s[:, cols], preferred_element_type=F32)
            for i in range(per_unit):
                send_a[x, i] = got[:, i * HD : (i + 1) * HD].astype(BF16)
                if x == 0:
                    own_a[i] = got[:, i * HD : (i + 1) * HD]
            for y in range(sides):
                if x or y:
                    a_copy(x, y).start()

        @pl.when(t == 0)
        def _():
            for load in later:
                load.start()
            prepare()

        total = sq_send[...]
        for x, y in peers:
            d = peer_rank(x, y)
            arrived(sq_recv.at[d], 0, d)
            total = total + sq_recv[d]
        total = jnp.sum(jnp.where(diag_r == diag_c, total, 0.0), axis=1, keepdims=True)
        inverse = lax.rsqrt(total / width + 1e-05)
        for x, y in peers:
            d = peer_rank(x, y)
            arrived(recv_a.at[d], 1, d)
        for i in range(per):
            value = own_a[side * per + i]
            for x, y in peers:
                value = value + recv_a[peer_rank(x, y), i].astype(F32)
            plain = side * per + i == per_unit - 1
            value = value * inverse
            turned = value * cosine[t] + pltpu.roll(value, HD // 2, 1) * sine[t]
            qkv[me * per + i] = jnp.where(plain, value, turned).astype(BF16)
        for x, y in [(0, 1)] + peers[::-1][1:]:
            q_copy(x, y).start()

        @pl.when(t == 0)
        def _():
            for load in later[:4]:
                load.wait()

        def pair_at(j):
            return lax.rem(lax.div(z, 2) + j, pairs)

        def merge(j, with_new):
            v = pair_at(j)
            for n in range(2):
                p_copy(j, n).wait_recv()
            levels = [box_l[j, 0], got_l[j]]
            values = [box_o[j, 0], got_o[j]]
            if with_new:
                keep = jnp.logical_and(lax.rem(z, 2) == side, j == 0)
                fresh_k[t] = qkv[z * per_unit + group].astype(F32)
                fresh_v[t] = qkv[z * per_unit + group + 1].astype(F32)
                mine = qkv[pl.ds(z * per_unit, group)].reshape(unit_rows, HD).astype(F32)
                for n in range(STEPS):
                    keys = jnp.concatenate([fresh_k[n]] * group, axis=0)
                    score = jnp.sum(mine * keys, axis=1, keepdims=True) * BASE2
                    score = jnp.where(jnp.logical_and(n <= t, keep), score, LOW)
                    levels.append(jnp.broadcast_to(score, (unit_rows, HD)))
                    values.append(jnp.concatenate([fresh_v[n]] * group, axis=0))
            best = functools.reduce(jnp.maximum, levels)
            amount = jnp.zeros((unit_rows, HD), F32)
            acc = jnp.zeros((unit_rows, HD), F32)
            for level, value in zip(levels, values):
                e = jnp.exp2(level - best)
                amount = amount + e
                acc = acc + e * value
            zone[v, z] = (acc / amount).astype(BF16)
            level = best + jnp.log(amount) * LOG2E
            zone_c[v] = level
            zone_l[v, z] = jnp.sum(jnp.where(eye(), level, 0.0), axis=0, keepdims=True)
            for x in order[:-1]:
                for n in range(2):
                    z_copy(v, x, n, z, flip(z, x)).start()

        def unit(i, carry):
            j = lax.div(i, 2)
            sub = lax.rem(i, 2)
            near_pair = lax.rem(z + sub, 2)
            far_pair = lax.rem(1 - side + sub, 2)
            late = lax.div(j + pairs - 1, pairs)
            parity = near_pair + late * (far_pair - near_pair)
            u = 2 * pair_at(j) + parity
            k = u
            for n in range(sides):
                owner = u * sides + n

                @pl.when(owner != me)
                def _():
                    arrived(qkv.at[pl.ds(owner * per, per)], 2, owner)

            q = qkv[pl.ds(u * per_unit, group)].reshape(unit_rows, HD)
            size = min(span, 1024)
            q_own = jnp.dot(chosen, q, preferred_element_type=F32).astype(BF16)
            scores = [
                lax.dot_general(q, pk_s[0, k, c : c + size], NT, preferred_element_type=F32)
                for c in range(0, span, size)
            ]
            near = lax.dot_general(
                q_own, sk_s[:, k].reshape(suffix, HD), NT, preferred_element_type=F32
            ) + bias[...]

            def soft(s, values):
                top = jnp.max(s, axis=1, keepdims=True)
                e = jnp.exp2((s - top) * BASE2)
                total = jnp.sum(e, axis=1, keepdims=True)
                return top, total, jnp.dot(e.astype(BF16), values, preferred_element_type=F32)

            parts = [
                soft(s, pv_s[0, k, n * size : (n + 1) * size]) for n, s in enumerate(scores)
            ]
            near_top, near_sum, near_acc = soft(near, sv_s[:, k].reshape(suffix, HD))
            parts.append(
                (
                    spread(jnp.broadcast_to(near_top, (own_rows, HD)), LOW),
                    spread(jnp.broadcast_to(near_sum, (own_rows, HD)), 0.0),
                    spread(near_acc, 0.0),
                )
            )
            best = functools.reduce(jnp.maximum, [part[0] for part in parts])
            amount = jnp.zeros((unit_rows, HD), F32)
            acc = jnp.zeros((unit_rows, HD), F32)
            for part_top, part_sum, part_acc in parts:
                weight = jnp.exp2((part_top - best) * BASE2)
                amount = amount + weight * part_sum
                acc = acc + weight * part_acc
            away = lax.rem(parity + side, 2)
            box_o[j, away] = acc / amount
            box_l[j, away] = best * BASE2 + jnp.log(amount) * LOG2E

            @pl.when(away == 1)
            def _():
                for n in range(2):
                    p_copy(j, n).start()

            @pl.when(jnp.logical_and(sub == 0, j > 0))
            def _():
                merge(j - 1, True)

            return carry

        lax.fori_loop(0, kv, unit, 0)
        merge(pairs - 1, False)

        @pl.when(t == 0)
        def _():
            later[4].wait()

        for v in range(pairs):
            levels, values = [zone_c[v]], [zone[v, z]]
            for x in order[:-1]:
                source = flip(z, x)
                for n in range(2):
                    z_copy(v, x, n, source, source).wait_recv()
                levels.append(
                    jnp.sum(jnp.where(eye(), zone_l[v, source], 0.0), axis=1, keepdims=True)
                )
                values.append(zone[v, source])
            best = functools.reduce(jnp.maximum, levels)
            amount = jnp.zeros((unit_rows, HD), F32)
            acc = jnp.zeros((unit_rows, HD), F32)
            for level, value in zip(levels, values):
                e = jnp.exp2(level - best)
                amount = amount + e
                acc = acc + e * value.astype(F32)
            mix[pl.ds((2 * v + side) * group, group)] = (
                (acc / amount).astype(BF16).reshape(group, gen, HD)
            )
            m_copy(v, side).start()

        part = jnp.zeros((samples, depth), F32)
        for v in range(pairs):
            part = part + out_part(2 * v + side, 0, depth)
        for v in range(pairs):
            m_copy(v, 1 - side).wait_recv()
        for n in range(pieces):
            total = part[:, n * piece : (n + 1) * piece]
            for v in range(pairs):
                total = total + out_part(2 * v + 1 - side, n * piece, piece)
            cbuf[t, head_me, :, n * piece : (n + 1) * piece] = total.astype(BF16)
            for o in range(1, heads):
                c_send(t, o, n).start()
        for x, y in peers:
            sq_copy(x, y).wait_send()
            a_copy(x, y).wait_send()
            q_copy(x, y).wait_send()
        for j in range(pairs):
            for n in range(2):
                p_copy(j, n).wait_send()
            for x in order[:-1]:
                for n in range(2):
                    z_copy(j, x, n, z, flip(z, x)).wait_send()
            m_copy(j, side).wait_send()
        for n in range(pieces):
            for o in range(1, heads):
                c_arrival(t, o, n).wait_recv()

        @pl.when(t < STEPS - 1)
        def _():
            delta = cbuf[t, 0].astype(F32)
            for n in range(1, heads):
                delta = delta + cbuf[t, n].astype(F32)
            u_out[...] += delta
            h_out[...] = (h_out[...].astype(F32) + delta).astype(BF16)

        for n in range(pieces):
            for o in range(1, heads):
                c_send(t, o, n).wait_send()
        return carry

    lax.fori_loop(0, STEPS, step, 0)
    stores = [
        pltpu.make_async_copy(h_out, h_hbm, out_sem.at[0]),
        pltpu.make_async_copy(u_out, u_hbm, out_sem.at[1]),
        pltpu.make_async_copy(cbuf.at[STEPS - 1], c_hbm, out_sem.at[2]),
    ]
    for store in stores:
        store.start()
    for store in stores:
        store.wait()


def local(
    ranks, sides, heads,
    hidden, gain, w_query, w_key, w_value, w_out, prefix_keys, prefix_values,
    suffix_keys, suffix_values, suffix_lengths, page_table,
):
    samples, depth = hidden.shape
    prompts, kv, span, _ = prefix_keys.shape
    group = w_query.shape[1] // w_key.shape[1]
    gen = samples // prompts
    slots, _, page, _ = suffix_keys.shape
    own_rows = samples // ranks * group
    all_heads = kv * (group + 2)
    per = -(-all_heads * prompts // ranks)
    unit_rows = group * gen
    units = prompts * kv
    rows = units * unit_rows // ranks

    power = -np.arange(HD // 2, dtype=np.float64) * 2.0 / HD
    freq = np.tile(500000.0 ** power, 2).astype(np.float32).reshape(1, HD)

    chips = ranks // sides
    paired = (
        prompts == 1
        and sides == 2
        and kv == chips
        and kv >= 4
        and chips & (chips - 1) == 0
        and samples % ranks == 0
        and group % 2 == 0
    )
    weights = [
        pltpu.VMEM((depth, all_heads * HD), BF16),
        pltpu.VMEM(w_out.shape, BF16),
        pltpu.VMEM(prefix_keys.shape, BF16),
        pltpu.VMEM(prefix_values.shape, BF16),
        pltpu.VMEM(suffix_keys.shape, BF16),
        pltpu.VMEM(suffix_values.shape, BF16),
        pltpu.VMEM((own_rows, slots * page), F32),
    ]
    state = [
        pltpu.VMEM(page_table.shape[::-1], jnp.int32),
        pltpu.VMEM((STEPS, samples, HD), F32),
        pltpu.VMEM((STEPS, samples, HD), F32),
        pltpu.VMEM((samples, depth), BF16),
        pltpu.VMEM((samples, depth), F32),
    ]
    dma = pltpu.SemaphoreType.DMA
    if paired:
        pairs = kv // 2
        pieces = 2
        body = functools.partial(
            chip_kernel, chips, sides, heads, kv, group, float(depth * ranks)
        )
        scratch = state + weights + [
            pltpu.VMEM((chips, group + 2, gen, HD), BF16),
            pltpu.VMEM((ranks, per, gen, HD), BF16),
            pltpu.VMEM((group + 2, gen, HD), F32),
            pltpu.VMEM((1, HD), F32),
            pltpu.VMEM((ranks, 1, HD), F32),
            pltpu.VMEM((all_heads, gen, HD), BF16),
            pltpu.VMEM((STEPS, gen, HD), F32),
            pltpu.VMEM((STEPS, gen, HD), F32),
            pltpu.VMEM((pairs, 2, unit_rows, HD), F32),
            pltpu.VMEM((pairs, 2, unit_rows, HD), F32),
            pltpu.VMEM((pairs, unit_rows, HD), F32),
            pltpu.VMEM((pairs, unit_rows, HD), F32),
            pltpu.VMEM((pairs, chips, unit_rows, HD), BF16),
            pltpu.VMEM((pairs, chips, 1, unit_rows), F32),
            pltpu.VMEM((pairs, unit_rows, HD), F32),
            pltpu.VMEM((kv * group, gen, HD), BF16),
            pltpu.VMEM((STEPS, heads, samples, depth), BF16),
            dma((3 * kv + 5,)),
            dma((3, ranks)),
            dma((3, ranks)),
            dma((pairs, 2)),
            dma((pairs, 2)),
            dma((pairs, chips, 2)),
            dma((pairs, chips, 2)),
            dma((pairs,)),
            dma((pairs,)),
            dma((STEPS, heads, pieces)),
            dma((STEPS, heads, pieces)),
            dma((3,)),
        ]
    else:
        body = functools.partial(
            kernel, ranks, sides, heads, prompts, kv, group, float(depth * ranks)
        )
        scratch = state + weights + [
            pltpu.VMEM((ranks, per, gen, HD), BF16),
            pltpu.VMEM((ranks, per, gen, HD), BF16),
            pltpu.VMEM((per, gen, HD), F32),
            pltpu.VMEM((1, HD), F32),
            pltpu.VMEM((ranks, 1, HD), F32),
            pltpu.VMEM((ranks * per, gen, HD), BF16),
            pltpu.VMEM((STEPS, gen, HD), F32),
            pltpu.VMEM((STEPS, gen, HD), F32),
            pltpu.VMEM((units * unit_rows, HD), BF16),
            pltpu.VMEM((units, 1, unit_rows), F32),
            pltpu.VMEM((ranks, rows, HD), BF16),
            pltpu.VMEM((ranks, 1, unit_rows), F32),
            pltpu.VMEM((prompts * kv * group, gen, HD), BF16),
            pltpu.VMEM((samples, depth), F32),
            pltpu.VMEM((STEPS, heads, samples, depth), BF16),
            dma((3 * kv + 5,)),
            dma((6, ranks)),
            dma((6, ranks)),
            dma((STEPS, heads)),
            dma((STEPS, heads)),
            dma((3,)),
        ]

    vmem = pl.BlockSpec(memory_space=pltpu.VMEM)
    smem = pl.BlockSpec(memory_space=pltpu.SMEM)
    hbm = pl.BlockSpec(memory_space=pl.ANY)
    store = pl.BlockSpec(memory_space=pltpu.HBM)
    held, added, last = pl.pallas_call(
        body,
        out_shape=(
            jax.ShapeDtypeStruct((samples, depth), BF16),
            jax.ShapeDtypeStruct((samples, depth), F32),
            jax.ShapeDtypeStruct((heads, samples, depth), BF16),
        ),
        in_specs=[smem, store] + [vmem] * 3 + [hbm] * 8,
        out_specs=(store, store, store),
        scratch_shapes=scratch,
        compiler_params=pltpu.CompilerParams(
            collective_id=0, has_side_effects=True, vmem_limit_bytes=60 * 1024 * 1024
        ),
    )(
        suffix_lengths, page_table.T, hidden, gain.reshape(1, depth), freq,
        w_query, w_key, w_value, w_out, prefix_keys, prefix_values, suffix_keys, suffix_values,
    )
    delta = last[0].astype(F32)
    for n in range(1, heads):
        delta = delta + last[n].astype(F32)
    return (held.astype(F32) + delta).astype(BF16), added + delta


def solution(mesh):
    placed = (
        P("groups", ("seq", "side")),
        P(("seq", "side")),
        P(("seq", "side"), "head"),
        P(("seq", "side"), "head"),
        P(("seq", "side"), "head"),
        P("head", ("seq", "side")),
        P("groups", "head", ("seq", "side"), None),
        P("groups", "head", ("seq", "side"), None),
        P(("groups", "seq", "side"), "head", None, None),
        P(("groups", "seq", "side"), "head", None, None),
        P("groups"),
        P("groups", None),
    )
    ranks = mesh.shape["seq"] * mesh.shape["side"]
    return jax.shard_map(
        functools.partial(local, ranks, mesh.shape["side"], mesh.shape["head"]),
        mesh=mesh,
        in_specs=placed,
        out_specs=(P("groups", ("seq", "side")), P("groups", ("seq", "side"))),
        check_vma=False,
    )
```

```python
import functools
import math

import jax
import jax.numpy as jnp
import numpy as np
from jax import lax
from jax.experimental import pallas as pl
from jax.experimental.pallas import tpu as pltpu
from jax.sharding import PartitionSpec as P

HD = 128
STEPS = 3
LOW = -1e30
BASE2 = math.log2(math.e) / math.sqrt(HD)
LOG2E = math.log2(math.e)
MESH = pl.DeviceIdType.MESH
F32 = jnp.float32
BF16 = jnp.bfloat16
NT = (((1,), (1,)), ((), ()))
TN = (((0,), (0,)), ((), ()))


def kernel(
    ranks, sides, heads, prompts, kv, group, width,
    lens, table_hbm, x_in, gain, freq, wq, wk, wv, wo, pk, pv, sk, sv,
    h_hbm, u_hbm, c_hbm,
    table, cosine, sine, h_out, u_out, w_s, wo_s, pk_s, pv_s, sk_s, sv_s, bias, send_a, recv_a, own_a, sq_send, sq_recv,
    qkv, fresh_k, fresh_v, outs, lse, recv_b, recv_l, mix, part, cbuf,
    load_sem, send_sem, recv_sem, send_c, recv_c, out_sem,
):
    samples = x_in.shape[0]
    gen = samples // prompts
    own_count = samples // ranks
    q_heads = kv * group
    all_heads = q_heads + 2 * kv
    blocks = all_heads * prompts
    per = qkv.shape[0] // ranks
    unit_rows = group * gen
    units = prompts * kv
    rows = units * unit_rows // ranks
    row_blocks = rows // gen
    span = pk_s.shape[2]
    slots, page = sk_s.shape[0], sk_s.shape[2]
    pages = table.shape[0]
    suffix = slots * page
    own_rows = own_count * group

    me = lax.axis_index("seq") * sides + lax.axis_index("side")
    head_me = lax.axis_index("head")

    def rank_id(d):
        return {"seq": lax.div(d, sides), "side": lax.rem(d, sides)}

    per_unit = group + 2
    owners = per_unit // per
    loads = []
    for k in range(kv):
        base = k * per_unit * HD
        for source, first, count in ((wq, 0, group), (wk, group, 1), (wv, group + 1, 1)):
            loads.append(
                pltpu.make_async_copy(
                    source.at[:, pl.ds(k * count * HD, count * HD)],
                    w_s.at[:, pl.ds(base + first * HD, count * HD)],
                    load_sem.at[len(loads)],
                )
            )
    table_load = pltpu.make_async_copy(table_hbm, table, out_sem.at[0])
    table_load.start()
    for load in loads:
        load.start()
    later = [
        pltpu.make_async_copy(source, target, load_sem.at[len(loads) + n])
        for n, (source, target) in enumerate(
            ((pk, pk_s), (pv, pv_s), (sk, sk_s), (sv, sv_s), (wo, wo_s))
        )
    ]

    barrier = pltpu.get_barrier_semaphore()
    for o in range(1, ranks):
        pl.semaphore_signal(
            barrier, inc=1, device_id=rank_id(lax.rem(me + o, ranks)), device_id_type=MESH
        )
    for o in range(1, heads):
        pl.semaphore_signal(
            barrier, inc=1, device_id={"head": lax.rem(head_me + o, heads)}, device_id_type=MESH
        )

    start = (me + 1 - 2 * lax.rem(me, 2)) * own_count
    own_prompt = lax.div(start, gen)
    own_first = lax.rem(start, gen)
    line = lax.broadcasted_iota(jnp.int32, (own_rows, suffix), 0)
    column = lax.broadcasted_iota(jnp.int32, (own_rows, suffix), 1)
    which = lax.rem(line, own_count)
    slot = lax.div(column, page)
    offset = lax.rem(column, page)
    place = jnp.full((own_rows, suffix), 1 << 28, jnp.int32)
    length = jnp.zeros((own_rows, suffix), jnp.int32)
    table_load.wait()
    table_line = lax.broadcasted_iota(jnp.int32, table.shape, 1)
    for j in range(own_count):
        mine = which == j
        entries = jnp.sum(
            jnp.where(table_line == start + j, table[...], 0), axis=1, keepdims=True
        )
        length = jnp.where(mine, lens[start + j], length)
        for n in range(pages):
            hit = jnp.logical_and(mine, slot == entries[n : n + 1, :])
            place = jnp.where(hit, n * page + offset, place)
    bias[...] = jnp.where(place < length, 0.0, LOW).astype(F32)
    sample_line = lax.broadcasted_iota(jnp.int32, (samples, HD), 0)
    position = jnp.full((samples, HD), span * ranks, jnp.int32)
    for n in range(samples):
        position = jnp.where(sample_line == n, position + lens[n], position)
    low_half = lax.broadcasted_iota(jnp.int32, (samples, HD), 1) < HD // 2
    for n in range(STEPS):
        angle = (position + n).astype(F32) * freq[...]
        turn = jnp.sin(angle)
        cosine[n] = jnp.cos(angle)
        sine[n] = jnp.where(low_half, -turn, turn)
    fresh_k[...] = jnp.zeros_like(fresh_k)
    fresh_v[...] = jnp.zeros_like(fresh_v)
    h_out[...] = x_in[...]
    u_out[...] = jnp.zeros_like(u_out)

    pl.semaphore_wait(barrier, ranks - 1 + heads - 1)

    sel_row = lax.broadcasted_iota(jnp.int32, (own_rows, unit_rows), 0)
    sel_col = lax.broadcasted_iota(jnp.int32, (own_rows, unit_rows), 1)
    target = lax.div(sel_row, own_count) * gen + own_first + lax.rem(sel_row, own_count)
    chosen = jnp.where(sel_col == target, 1.0, 0.0).astype(F32)
    gen_line = lax.broadcasted_iota(jnp.int32, (gen, HD), 0)

    def spread(lines, fill):
        found = []
        for g in range(group):
            value = jnp.full((gen, HD), fill, F32)
            for j in range(own_count):
                row = lines[g * own_count + j : g * own_count + j + 1]
                value = jnp.where(gen_line == own_first + j, row, value)
            found.append(value)
        return jnp.concatenate(found, axis=0)


    my_block = me * row_blocks
    my_unit = lax.div(my_block, group)
    my_q = my_unit * per_unit + lax.rem(my_block, group)
    my_k = my_unit * per_unit + group
    my_shift = lax.rem(me * rows, unit_rows)

    def copy(src, dst, phase, o, d):
        return pltpu.make_async_remote_copy(
            src_ref=src,
            dst_ref=dst,
            send_sem=send_sem.at[phase, o],
            recv_sem=recv_sem.at[phase, o],
            device_id=rank_id(d),
            device_id_type=MESH,
        )

    def sq_copy(o, d):
        return copy(sq_send, sq_recv.at[o], 0, o, d)

    def a_copy(o, d):
        return copy(send_a.at[d], recv_a.at[o], 1, o, d)

    def q_copy(o, d, owner):
        place = qkv.at[pl.ds(owner * per, per)]
        return copy(place, place, 2, o, d)

    def b_copy(o, d):
        return copy(outs.at[pl.ds(pl.multiple_of(d * rows, rows), rows)], recv_b.at[o], 3, o, d)

    def l_copy(o, d):
        return copy(lse.at[lax.div(d * rows, unit_rows)], recv_l.at[o], 4, o, d)

    def m_copy(o, d, owner):
        place = mix.at[pl.ds(owner * row_blocks, row_blocks)]
        return copy(place, place, 5, o, d)

    def c_copy(t, o):
        return pltpu.make_async_remote_copy(
            src_ref=cbuf.at[t, head_me],
            dst_ref=cbuf.at[t, head_me],
            send_sem=send_c.at[t, o],
            recv_sem=recv_c.at[t, o],
            device_id={"head": lax.rem(head_me + o, heads)},
            device_id_type=MESH,
        )

    def c_arrival(t, o):
        source = lax.rem(head_me + heads - o, heads)
        return pltpu.make_async_remote_copy(
            src_ref=cbuf.at[t, source],
            dst_ref=cbuf.at[t, source],
            send_sem=send_c.at[t, o],
            recv_sem=recv_c.at[t, o],
            device_id={"head": source},
            device_id_type=MESH,
        )

    def ahead(o):
        return lax.rem(me + o, ranks)

    def behind(o):
        return lax.rem(me + ranks - o, ranks)

    far_first = sorted(range(1, ranks), key=lambda o: abs(2 * o - ranks))

    def step(t, carry):
        wide = h_out[...].astype(F32)
        scaled = (wide * gain[...]).astype(BF16)
        squares = jnp.sum(wide * wide, axis=1, keepdims=True)
        diag_r = lax.broadcasted_iota(jnp.int32, (samples, HD), 0)
        diag_c = lax.broadcasted_iota(jnp.int32, (samples, HD), 1)
        sq_send[...] = jnp.sum(jnp.where(diag_r == diag_c, squares, 0.0), axis=0, keepdims=True)
        for o in range(1, ranks):
            sq_copy(o, ahead(o)).start()

        @pl.when(t == 0)
        def _():
            for load in loads:
                load.wait()
            for load in later:
                load.start()

        def chunk(d):
            if prompts == 1 and blocks == per * ranks:
                wide_cols = per * HD
                cols = pl.ds(pl.multiple_of(d * wide_cols, wide_cols), wide_cols)
                got = jnp.dot(scaled, w_s[:, cols], preferred_element_type=F32)
                return [got[:, i * HD : (i + 1) * HD] for i in range(per)]
            found = []
            for i in range(per):
                b = jnp.minimum(d * per + i, blocks - 1)
                p = lax.div(b, all_heads)
                cols = pl.ds(pl.multiple_of(lax.rem(b, all_heads) * HD, HD), HD)
                got = jnp.dot(scaled, w_s[:, cols], preferred_element_type=F32)
                pick = got[0:gen]
                for n in range(1, prompts):
                    pick = jnp.where(p == n, got[n * gen : (n + 1) * gen], pick)
                found.append(pick)
            return found

        for o in far_first:
            d = ahead(o)
            for i, piece in enumerate(chunk(d)):
                send_a[d, i] = piece.astype(BF16)
            a_copy(o, d).start()
        for i, piece in enumerate(chunk(me)):
            own_a[i] = piece

        total = sq_send[...]
        for o in range(1, ranks):
            sq_copy(o, ahead(o)).wait_recv()
            total = total + sq_recv[o]
        total = jnp.sum(jnp.where(diag_r == diag_c, total, 0.0), axis=1, keepdims=True)
        inverse = lax.rsqrt(total / width + 1e-05)
        for o in range(1, ranks):
            a_copy(o, ahead(o)).wait_recv()
        for i in range(per):
            value = own_a[i]
            for o in range(1, ranks):
                value = value + recv_a[o, i].astype(F32)
            b = jnp.minimum(me * per + i, blocks - 1)
            p = lax.div(b, all_heads)
            plain = lax.rem(b, per_unit) == per_unit - 1
            inv, cos, sin = inverse[0:gen], cosine[t, 0:gen], sine[t, 0:gen]
            for n in range(1, prompts):
                band = slice(n * gen, (n + 1) * gen)
                inv = jnp.where(p == n, inverse[band], inv)
                cos = jnp.where(p == n, cosine[t, band], cos)
                sin = jnp.where(p == n, sine[t, band], sin)
            value = value * inv
            turned = value * cos + pltpu.roll(value, HD // 2, 1) * sin
            qkv[me * per + i] = jnp.where(plain, value, turned).astype(BF16)
        for o in far_first:
            q_copy(o, ahead(o), me).start()

        def q_arrived(owner):
            @pl.when(owner != me)
            def _():
                q_copy(lax.rem(me - owner + ranks, ranks), owner, owner).wait_recv()

        @pl.when(t == 0)
        def _():
            for load in later[:4]:
                load.wait()

        def unit(i, carry):
            u = lax.rem(my_unit + 2 * lax.div(i, 2), units)
            u = u + lax.rem(i, 2) * (1 - 2 * lax.rem(u, 2))
            for n in range(owners):
                q_arrived(u * owners + n)
            p = lax.div(u, kv)
            k = lax.rem(u, kv)
            q = qkv[pl.ds(u * per_unit, group)].reshape(unit_rows, HD)
            size = min(span, 1024)
            q_own = jnp.dot(chosen.astype(BF16), q, preferred_element_type=F32).astype(BF16)
            scores = [
                lax.dot_general(q, pk_s[p, k, c : c + size], NT, preferred_element_type=F32)
                for c in range(0, span, size)
            ]
            near = lax.dot_general(
                q_own, sk_s[:, k].reshape(suffix, HD), NT, preferred_element_type=F32
            ) + bias[...]

            def soft(s, values):
                top = jnp.max(s, axis=1, keepdims=True)
                e = jnp.exp2((s - top) * BASE2)
                total = jnp.sum(e, axis=1, keepdims=True)
                return top, total, jnp.dot(e.astype(BF16), values, preferred_element_type=F32)

            parts = [
                soft(s, pv_s[p, k, n * size : (n + 1) * size]) for n, s in enumerate(scores)
            ]
            near_top, near_sum, near_acc = soft(near, sv_s[:, k].reshape(suffix, HD))
            near_top = jnp.where(p == own_prompt, near_top, LOW)
            parts.append(
                (
                    spread(jnp.broadcast_to(near_top, (own_rows, HD)), LOW),
                    spread(jnp.broadcast_to(near_sum, (own_rows, HD)), 0.0),
                    spread(near_acc, 0.0),
                )
            )
            best = functools.reduce(jnp.maximum, [part[0] for part in parts])
            amount = jnp.zeros((unit_rows, HD), F32)
            acc = jnp.zeros((unit_rows, HD), F32)
            for part_top, part_sum, part_acc in parts:
                weight = jnp.exp2((part_top - best) * BASE2)
                amount = amount + weight * part_sum
                acc = acc + weight * part_acc
            outs[pl.ds(pl.multiple_of(u * unit_rows, unit_rows), unit_rows)] = (
                acc / amount
            ).astype(BF16)
            level = best * BASE2 + jnp.log(amount) * LOG2E
            eye_r = lax.broadcasted_iota(jnp.int32, (unit_rows, unit_rows), 0)
            eye_c = lax.broadcasted_iota(jnp.int32, (unit_rows, unit_rows), 1)
            lse[u] = jnp.sum(jnp.where(eye_r == eye_c, level, 0.0), axis=0, keepdims=True)
            for j in range(unit_rows // rows):
                d = u * (unit_rows // rows) + j

                @pl.when(d != me)
                def _():
                    o = lax.rem(d - me + ranks, ranks)
                    l_copy(o, d).start()
                    b_copy(o, d).start()

            return carry

        lax.fori_loop(0, units, unit, 0)
        for n in range(units * owners, ranks):
            q_arrived(n)

        fresh_k[t] = qkv[my_k].astype(F32)
        fresh_v[t] = qkv[my_k + 1].astype(F32)
        mine = qkv[pl.ds(my_q, row_blocks)].reshape(rows, HD).astype(F32)
        new_scores = []
        for n in range(STEPS):
            keys = jnp.concatenate([fresh_k[n]] * row_blocks, axis=0)
            s = jnp.sum(mine * keys, axis=1, keepdims=True) * BASE2
            new_scores.append(jnp.where(n <= t, s, LOW))
        pick_r = lax.broadcasted_iota(jnp.int32, (rows, unit_rows), 0)
        pick_c = lax.broadcasted_iota(jnp.int32, (rows, unit_rows), 1)

        def as_column(row):
            return jnp.sum(jnp.where(pick_c == pick_r + my_shift, row, 0.0), axis=1, keepdims=True)

        levels = [as_column(lse[my_unit])]
        for o in range(1, ranks):
            l_copy(o, ahead(o)).wait_recv()
            levels.append(as_column(recv_l[o]))
        best = functools.reduce(jnp.maximum, levels + new_scores)
        amount = jnp.zeros((rows, 1), F32)
        acc = jnp.zeros((rows, HD), F32)
        for n in range(STEPS):
            e = jnp.where(n <= t, jnp.exp2(new_scores[n] - best), 0.0)
            amount = amount + e
            acc = acc + e * jnp.concatenate([fresh_v[n]] * row_blocks, axis=0)
        for o in range(ranks):
            e = jnp.exp2(levels[o] - best)
            amount = amount + e
            if o == 0:
                got = outs[pl.ds(pl.multiple_of(me * rows, rows), rows)]
            else:
                b_copy(o, ahead(o)).wait_recv()
                got = recv_b[o]
            acc = acc + e * got.astype(F32)
        mix[pl.ds(my_block, row_blocks)] = (
            (acc / amount).astype(BF16).reshape(row_blocks, gen, HD)
        )
        for o in far_first:
            m_copy(o, ahead(o), me).start()

        @pl.when(t == 0)
        def _():
            later[4].wait()

        part[...] = jnp.zeros_like(part)
        for o in [0] + far_first[::-1]:
            d = behind(o)
            if o > 0:
                m_copy(o, ahead(o), d).wait_recv()
            b = d * row_blocks
            p = lax.div(b, q_heads)
            left = jnp.concatenate([mix[b + i] for i in range(row_blocks)], axis=1)
            depth = row_blocks * HD
            right = wo_s[pl.ds(pl.multiple_of(lax.rem(b, q_heads) * HD, HD), depth)]
            band = pl.ds(pl.multiple_of(p * gen, gen), gen)
            part[band] += jnp.dot(left, right, preferred_element_type=F32)
        cbuf[t, head_me] = part[...].astype(BF16)
        for o in range(1, heads):
            c_copy(t, o).start()
        for o in range(1, ranks):
            sq_copy(o, ahead(o)).wait_send()
            a_copy(o, ahead(o)).wait_send()
            q_copy(o, ahead(o), me).wait_send()
            l_copy(o, ahead(o)).wait_send()
            b_copy(o, ahead(o)).wait_send()
            m_copy(o, ahead(o), me).wait_send()
        for o in range(1, heads):
            c_arrival(t, o).wait_recv()

        @pl.when(t < STEPS - 1)
        def _():
            delta = cbuf[t, 0].astype(F32)
            for n in range(1, heads):
                delta = delta + cbuf[t, n].astype(F32)
            u_out[...] += delta
            h_out[...] = (h_out[...].astype(F32) + delta).astype(BF16)

        for o in range(1, heads):
            c_copy(t, o).wait_send()
        return carry

    lax.fori_loop(0, STEPS, step, 0)
    stores = [
        pltpu.make_async_copy(h_out, h_hbm, out_sem.at[0]),
        pltpu.make_async_copy(u_out, u_hbm, out_sem.at[1]),
        pltpu.make_async_copy(cbuf.at[STEPS - 1], c_hbm, out_sem.at[2]),
    ]
    for store in stores:
        store.start()
    for store in stores:
        store.wait()


def chip_kernel(
    chips, sides, heads, kv, group, width,
    lens_hbm, table_hbm, x_in, gain_hbm, freq_hbm, wq, wk, wv, wo, pk, pv, sk, sv,
    h_hbm, u_hbm, c_hbm,
    lens, gain, freq, table, cosine, sine, h_out, u_out, w_s, wo_s, pk_s, pv_s, sk_s, sv_s, bias,
    send_a, recv_a, own_a, sq_send, sq_recv, qkv, fresh_k, fresh_v,
    box_o, box_l, got_o, got_l, zone, zone_l, zone_c, mix, cbuf,
    load_sem, send_sem, recv_sem, send_p, recv_p, send_z, recv_z, send_m, recv_m,
    send_c, recv_c, small_sem, out_sem,
):
    samples = x_in.shape[0]
    depth = x_in.shape[1]
    gen = samples
    ranks = chips * sides
    own_count = samples // ranks
    per_unit = group + 2
    per = per_unit // sides
    half = group // sides
    unit_rows = group * gen
    pairs = kv // 2
    span = pk_s.shape[2]
    slots, page = sk_s.shape[0], sk_s.shape[2]
    pages = table.shape[0]
    suffix = slots * page
    own_rows = own_count * group
    pieces = recv_c.shape[2]
    piece = depth // pieces

    z = lax.axis_index("seq")
    side = lax.axis_index("side")
    me = z * sides + side
    head_me = lax.axis_index("head")
    order = list(range(chips - 1, -1, -1))
    peers = [(x, y) for x in order for y in range(sides) if x or y]

    def flip(v, x):
        bit = 1
        while bit <= x:
            if x & bit:
                v = v + bit * (1 - 2 * lax.rem(lax.div(v, bit), 2))
            bit *= 2
        return v

    def peer_rank(x, y):
        return flip(z, x) * sides + flip(side, y)

    def rank_id(d):
        return {"seq": lax.div(d, sides), "side": lax.rem(d, sides)}

    unit_width = per_unit * HD

    def w_loads(u):
        found = []
        base = u * unit_width
        pieces_of = (
            (wq, u * group, 0, half),
            (wk, u, half, 1),
            (wq, u * group + half, half + 1, half),
            (wv, u, 2 * half + 1, 1),
        )
        for n, (source, block, first, count) in enumerate(pieces_of):
            found.append(
                pltpu.make_async_copy(
                    source.at[:, pl.ds(pl.multiple_of(block * HD, HD), count * HD)],
                    w_s.at[:, pl.ds(pl.multiple_of(base + first * HD, HD), count * HD)],
                    load_sem.at[u * len(pieces_of) + n],
                )
            )
        return found

    small = [
        pltpu.make_async_copy(source, target, small_sem.at[n])
        for n, (source, target) in enumerate(
            ((x_in, h_out), (gain_hbm, gain), (lens_hbm, lens), (freq_hbm, freq), (table_hbm, table))
        )
    ]
    for load in small:
        load.start()
    for x in order:
        for load in w_loads(flip(z, x)):
            load.start()
    later = [
        pltpu.make_async_copy(source, target, load_sem.at[4 * kv + n])
        for n, (source, target) in enumerate(
            ((pk, pk_s), (pv, pv_s), (sk, sk_s), (sv, sv_s), (wo, wo_s))
        )
    ]

    barrier = pltpu.get_barrier_semaphore()
    for x, y in peers:
        pl.semaphore_signal(
            barrier, inc=1, device_id=rank_id(peer_rank(x, y)), device_id_type=MESH
        )
    for o in range(1, heads):
        pl.semaphore_signal(
            barrier, inc=1, device_id={"head": lax.rem(head_me + o, heads)}, device_id_type=MESH
        )

    u_out[...] = jnp.zeros_like(u_out)
    fresh_k[...] = jnp.zeros_like(fresh_k)
    fresh_v[...] = jnp.zeros_like(fresh_v)
    start = (me + 1 - 2 * lax.rem(me, 2)) * own_count

    def prepare():
        for load in small[2:]:
            load.wait()
        sample_line = lax.broadcasted_iota(jnp.int32, (samples, HD), 0)
        position = jnp.full((samples, HD), span * ranks, jnp.int32)
        for n in range(samples):
            position = jnp.where(sample_line == n, position + lens[n], position)
        low_half = lax.broadcasted_iota(jnp.int32, (samples, HD), 1) < HD // 2
        for n in range(STEPS):
            angle = (position + n).astype(F32) * freq[...]
            turn = jnp.sin(angle)
            cosine[n] = jnp.cos(angle)
            sine[n] = jnp.where(low_half, -turn, turn)
        line = lax.broadcasted_iota(jnp.int32, (own_rows, suffix), 0)
        column = lax.broadcasted_iota(jnp.int32, (own_rows, suffix), 1)
        which = lax.rem(line, own_count)
        slot = lax.div(column, page)
        offset = lax.rem(column, page)
        place = jnp.full((own_rows, suffix), 1 << 28, jnp.int32)
        length = jnp.zeros((own_rows, suffix), jnp.int32)
        table_line = lax.broadcasted_iota(jnp.int32, table.shape, 1)
        for j in range(own_count):
            mine = which == j
            entries = jnp.sum(
                jnp.where(table_line == start + j, table[...], 0), axis=1, keepdims=True
            )
            length = jnp.where(mine, lens[start + j], length)
            for n in range(pages):
                hit = jnp.logical_and(mine, slot == entries[n : n + 1, :])
                place = jnp.where(hit, n * page + offset, place)
        bias[...] = jnp.where(place < length, 0.0, LOW).astype(F32)

    for load in small[:2]:
        load.wait()
    pl.semaphore_wait(barrier, ranks - 1 + heads - 1)

    sel_row = lax.broadcasted_iota(jnp.int32, (own_rows, unit_rows), 0)
    sel_col = lax.broadcasted_iota(jnp.int32, (own_rows, unit_rows), 1)
    target = lax.div(sel_row, own_count) * gen + start + lax.rem(sel_row, own_count)
    chosen = jnp.where(sel_col == target, 1.0, 0.0).astype(BF16)
    gen_line = lax.broadcasted_iota(jnp.int32, (gen, HD), 0)

    def spread(lines, fill):
        found = []
        for g in range(group):
            value = jnp.full((gen, HD), fill, F32)
            for j in range(own_count):
                row = lines[g * own_count + j : g * own_count + j + 1]
                value = jnp.where(gen_line == start + j, row, value)
            found.append(value)
        return jnp.concatenate(found, axis=0)

    def eye():
        rows = lax.broadcasted_iota(jnp.int32, (unit_rows, unit_rows), 0)
        return rows == lax.broadcasted_iota(jnp.int32, (unit_rows, unit_rows), 1)

    def push(src, dst, phase, x, y):
        return pltpu.make_async_remote_copy(
            src_ref=src,
            dst_ref=dst,
            send_sem=send_sem.at[phase, x * sides + y],
            recv_sem=recv_sem.at[phase, me],
            device_id=rank_id(peer_rank(x, y)),
            device_id_type=MESH,
        )

    def arrived(dst, phase, source):
        pltpu.make_async_remote_copy(
            src_ref=dst,
            dst_ref=dst,
            send_sem=send_sem.at[phase, 0],
            recv_sem=recv_sem.at[phase, source],
            device_id=rank_id(source),
            device_id_type=MESH,
        ).wait_recv()

    def sq_copy(x, y):
        return push(sq_send, sq_recv.at[me], 0, x, y)

    def a_copy(x, y):
        return push(
            send_a.at[x, pl.ds(flip(side, y) * per, per)], recv_a.at[me], 1, x, y
        )

    def q_copy(x, y):
        place = qkv.at[pl.ds(me * per, half if x else per)]
        return push(place, place, 2, x, y)

    def p_copy(j, n):
        src, dst = ((box_o, got_o), (box_l, got_l))[n]
        return pltpu.make_async_remote_copy(
            src_ref=src.at[j, 1],
            dst_ref=dst.at[j],
            send_sem=send_p.at[j, n],
            recv_sem=recv_p.at[j, n],
            device_id={"side": 1 - side},
            device_id_type=MESH,
        )

    def z_copy(v, x, n, source, dest):
        buffer = (zone_l, zone)[n]
        return pltpu.make_async_remote_copy(
            src_ref=buffer.at[v, source],
            dst_ref=buffer.at[v, source],
            send_sem=send_z.at[v, x, n],
            recv_sem=recv_z.at[v, source, n],
            device_id={"seq": dest},
            device_id_type=MESH,
        )

    def m_copy(v, owner):
        place = mix.at[pl.ds((2 * v + owner) * group, group)]
        return pltpu.make_async_remote_copy(
            src_ref=place,
            dst_ref=place,
            send_sem=send_m.at[v],
            recv_sem=recv_m.at[v],
            device_id={"side": 1 - side},
            device_id_type=MESH,
        )

    def c_copy(t, o, n, source, dest, final):
        columns = pl.ds(n * piece, piece)
        place = cbuf.at[t, source, :, columns]
        return pltpu.make_async_remote_copy(
            src_ref=place,
            dst_ref=c_hbm.at[source, :, columns] if final else place,
            send_sem=send_c.at[t, o, n],
            recv_sem=recv_c.at[t, o, n],
            device_id={"head": dest},
            device_id_type=MESH,
        )

    def c_send(t, o, n, final):
        return c_copy(t, o, n, head_me, lax.rem(head_me + o, heads), final)

    def c_arrival(t, o, n, final):
        source = lax.rem(head_me + heads - o, heads)
        return c_copy(t, o, n, source, source, final)

    def either(t, act):
        @pl.when(t < STEPS - 1)
        def _():
            act(False)

        @pl.when(t == STEPS - 1)
        def _():
            act(True)

    def unit_queries(u):
        first = qkv[pl.ds(u * per_unit, half)]
        second = qkv[pl.ds(u * per_unit + per, half)]
        return jnp.concatenate([first, second], axis=0).reshape(unit_rows, HD)

    def out_part(u, first, count):
        left = jnp.concatenate([mix[u * group + i] for i in range(group)], axis=1)
        rows = pl.ds(pl.multiple_of(u * group * HD, HD), group * HD)
        return jnp.dot(
            left, wo_s[rows, first : first + count], preferred_element_type=F32
        )

    def step(t, carry):
        wide = h_out[...].astype(F32)
        scaled = (wide * gain[...]).astype(BF16)
        diag_r = lax.broadcasted_iota(jnp.int32, (samples, HD), 0)
        diag_c = lax.broadcasted_iota(jnp.int32, (samples, HD), 1)

        for x in order:
            u = flip(z, x)

            @pl.when(t == 0)
            def _():
                for load in w_loads(u):
                    load.wait()

            cols = pl.ds(pl.multiple_of(u * unit_width, HD), unit_width)
            got = jnp.dot(scaled, w_s[:, cols], preferred_element_type=F32)
            for i in range(per_unit):
                send_a[x, i] = got[:, i * HD : (i + 1) * HD].astype(BF16)
                if x == 0:
                    own_a[i] = got[:, i * HD : (i + 1) * HD]
            for y in range(sides):
                if x or y:
                    a_copy(x, y).start()
            if x == order[0]:
                squares = jnp.sum(wide * wide, axis=1, keepdims=True)
                sq_send[...] = jnp.sum(
                    jnp.where(diag_r == diag_c, squares, 0.0), axis=0, keepdims=True
                )
                for xx, yy in peers:
                    sq_copy(xx, yy).start()

        @pl.when(t == 0)
        def _():
            for load in later:
                load.start()
            prepare()

        total = sq_send[...]
        for x, y in peers:
            d = peer_rank(x, y)
            arrived(sq_recv.at[d], 0, d)
            total = total + sq_recv[d]
        total = jnp.sum(jnp.where(diag_r == diag_c, total, 0.0), axis=1, keepdims=True)
        inverse = lax.rsqrt(total / width + 1e-05)
        for x, y in peers:
            d = peer_rank(x, y)
            arrived(recv_a.at[d], 1, d)
        for i in range(per):
            value = own_a[side * per + i]
            for x, y in peers:
                value = value + recv_a[peer_rank(x, y), i].astype(F32)
            value = value * inverse
            turned = value * cosine[t] + pltpu.roll(value, HD // 2, 1) * sine[t]
            if i == half:
                turned = jnp.where(side == sides - 1, value, turned)
            qkv[me * per + i] = turned.astype(BF16)
        for x, y in [(0, 1)] + peers[::-1][1:]:
            q_copy(x, y).start()

        @pl.when(t == 0)
        def _():
            for load in later[:4]:
                load.wait()

        def pair_at(j):
            return lax.rem(lax.div(z, 2) + j, pairs)

        def merge(j, with_new):
            v = pair_at(j)
            for n in range(2):
                p_copy(j, n).wait_recv()
            levels = [box_l[j, 0], got_l[j]]
            values = [box_o[j, 0], got_o[j]]
            if with_new:
                keep = jnp.logical_and(lax.rem(z, 2) == side, j == 0)
                fresh_k[t] = qkv[z * per_unit + half].astype(F32)
                fresh_v[t] = qkv[z * per_unit + per + half].astype(F32)
                mine = unit_queries(z).astype(F32)
                for n in range(STEPS):
                    keys = jnp.concatenate([fresh_k[n]] * group, axis=0)
                    score = jnp.sum(mine * keys, axis=1, keepdims=True) * BASE2
                    score = jnp.where(jnp.logical_and(n <= t, keep), score, LOW)
                    levels.append(jnp.broadcast_to(score, (unit_rows, HD)))
                    values.append(jnp.concatenate([fresh_v[n]] * group, axis=0))
            best = functools.reduce(jnp.maximum, levels)
            amount = jnp.zeros((unit_rows, HD), F32)
            acc = jnp.zeros((unit_rows, HD), F32)
            for level, value in zip(levels, values):
                e = jnp.exp2(level - best)
                amount = amount + e
                acc = acc + e * value
            zone[v, z] = (acc / amount).astype(BF16)
            level = best + jnp.log(amount) * LOG2E
            zone_c[v] = level
            zone_l[v, z] = jnp.sum(jnp.where(eye(), level, 0.0), axis=0, keepdims=True)
            for x in order[:-1]:
                for n in range(2):
                    z_copy(v, x, n, z, flip(z, x)).start()

        def unit(i, carry):
            j = lax.div(i, 2)
            sub = lax.rem(i, 2)
            near_pair = lax.rem(z + sub, 2)
            far_pair = lax.rem(1 - side + sub, 2)
            late = lax.div(j + pairs - 1, pairs)
            parity = near_pair + late * (far_pair - near_pair)
            u = 2 * pair_at(j) + parity
            k = u
            for n in range(sides):
                owner = u * sides + n

                @pl.when(jnp.logical_and(u == z, owner != me))
                def _():
                    arrived(qkv.at[pl.ds(owner * per, per)], 2, owner)

                @pl.when(u != z)
                def _():
                    arrived(qkv.at[pl.ds(owner * per, half)], 2, owner)

            q = unit_queries(u)
            size = min(span, 1024)
            q_own = jnp.dot(chosen, q, preferred_element_type=F32).astype(BF16)
            scores = [
                lax.dot_general(q, pk_s[0, k, c : c + size], NT, preferred_element_type=F32)
                for c in range(0, span, size)
            ]
            near = lax.dot_general(
                q_own, sk_s[:, k].reshape(suffix, HD), NT, preferred_element_type=F32
            ) + bias[...]

            def soft(s, values):
                top = jnp.max(s, axis=1, keepdims=True)
                e = jnp.exp2((s - top) * BASE2)
                total = jnp.sum(e, axis=1, keepdims=True)
                return top, total, jnp.dot(e.astype(BF16), values, preferred_element_type=F32)

            parts = [
                soft(s, pv_s[0, k, n * size : (n + 1) * size]) for n, s in enumerate(scores)
            ]
            near_top, near_sum, near_acc = soft(near, sv_s[:, k].reshape(suffix, HD))
            parts.append(
                (
                    spread(jnp.broadcast_to(near_top, (own_rows, HD)), LOW),
                    spread(jnp.broadcast_to(near_sum, (own_rows, HD)), 0.0),
                    spread(near_acc, 0.0),
                )
            )
            best = functools.reduce(jnp.maximum, [part[0] for part in parts])
            amount = jnp.zeros((unit_rows, HD), F32)
            acc = jnp.zeros((unit_rows, HD), F32)
            for part_top, part_sum, part_acc in parts:
                weight = jnp.exp2((part_top - best) * BASE2)
                amount = amount + weight * part_sum
                acc = acc + weight * part_acc
            away = lax.rem(parity + side, 2)
            box_o[j, away] = acc / amount
            box_l[j, away] = best * BASE2 + jnp.log(amount) * LOG2E

            @pl.when(away == 1)
            def _():
                for n in range(2):
                    p_copy(j, n).start()

            @pl.when(jnp.logical_and(sub == 1, j < pairs - 1))
            def _():
                merge(j, True)

            return carry

        lax.fori_loop(0, kv, unit, 0)
        merge(pairs - 1, False)

        @pl.when(t == 0)
        def _():
            later[4].wait()

        for v in range(pairs):
            levels, values = [zone_c[v]], [zone[v, z]]
            for x in order[:-1]:
                source = flip(z, x)
                for n in range(2):
                    z_copy(v, x, n, source, source).wait_recv()
                levels.append(
                    jnp.sum(jnp.where(eye(), zone_l[v, source], 0.0), axis=1, keepdims=True)
                )
                values.append(zone[v, source])
            best = functools.reduce(jnp.maximum, levels)
            amount = jnp.zeros((unit_rows, HD), F32)
            acc = jnp.zeros((unit_rows, HD), F32)
            for level, value in zip(levels, values):
                e = jnp.exp2(level - best)
                amount = amount + e
                acc = acc + e * value.astype(F32)
            mix[pl.ds((2 * v + side) * group, group)] = (
                (acc / amount).astype(BF16).reshape(group, gen, HD)
            )
            m_copy(v, side).start()

        part = jnp.zeros((samples, depth), F32)
        for v in range(pairs):
            part = part + out_part(2 * v + side, 0, depth)
        for v in range(pairs):
            m_copy(v, 1 - side).wait_recv()
        for n in range(pieces):
            total = part[:, n * piece : (n + 1) * piece]
            for v in range(pairs):
                total = total + out_part(2 * v + 1 - side, n * piece, piece)
            cbuf[t, head_me, :, n * piece : (n + 1) * piece] = total.astype(BF16)

            def send(final):
                for o in range(1, heads):
                    c_send(t, o, n, final).start()

            either(t, send)

        @pl.when(t == STEPS - 1)
        def _():
            stores[2].start()

        for x, y in peers:
            sq_copy(x, y).wait_send()
            a_copy(x, y).wait_send()
            q_copy(x, y).wait_send()
        for j in range(pairs):
            for n in range(2):
                p_copy(j, n).wait_send()
            for x in order[:-1]:
                for n in range(2):
                    z_copy(j, x, n, z, flip(z, x)).wait_send()
            m_copy(j, side).wait_send()

        def finish(final):
            for n in range(pieces):
                for o in range(1, heads):
                    c_arrival(t, o, n, final).wait_recv()
            if not final:
                delta = cbuf[t, 0].astype(F32)
                for n in range(1, heads):
                    delta = delta + cbuf[t, n].astype(F32)
                u_out[...] += delta
                h_out[...] = (h_out[...].astype(F32) + delta).astype(BF16)
            for n in range(pieces):
                for o in range(1, heads):
                    c_send(t, o, n, final).wait_send()

        either(t, finish)

        @pl.when(t == STEPS - 2)
        def _():
            for store in stores[:2]:
                store.start()

        return carry

    stores = [
        pltpu.make_async_copy(h_out, h_hbm, out_sem.at[0]),
        pltpu.make_async_copy(u_out, u_hbm, out_sem.at[1]),
        pltpu.make_async_copy(cbuf.at[STEPS - 1, head_me], c_hbm.at[head_me], out_sem.at[2]),
    ]
    lax.fori_loop(0, STEPS, step, 0)
    for store in stores:
        store.wait()


def local(
    ranks, sides, heads,
    hidden, gain, w_query, w_key, w_value, w_out, prefix_keys, prefix_values,
    suffix_keys, suffix_values, suffix_lengths, page_table,
):
    samples, depth = hidden.shape
    prompts, kv, span, _ = prefix_keys.shape
    group = w_query.shape[1] // w_key.shape[1]
    gen = samples // prompts
    slots, _, page, _ = suffix_keys.shape
    own_rows = samples // ranks * group
    all_heads = kv * (group + 2)
    per = -(-all_heads * prompts // ranks)
    unit_rows = group * gen
    units = prompts * kv
    rows = units * unit_rows // ranks

    power = -np.arange(HD // 2, dtype=np.float64) * 2.0 / HD
    freq = np.tile(500000.0 ** power, 2).astype(np.float32).reshape(1, HD)

    chips = ranks // sides
    paired = (
        prompts == 1
        and sides == 2
        and kv == chips
        and kv >= 4
        and chips & (chips - 1) == 0
        and samples % ranks == 0
        and group % 2 == 0
    )
    weights = [
        pltpu.VMEM((depth, all_heads * HD), BF16),
        pltpu.VMEM(w_out.shape, BF16),
        pltpu.VMEM(prefix_keys.shape, BF16),
        pltpu.VMEM(prefix_values.shape, BF16),
        pltpu.VMEM(suffix_keys.shape, BF16),
        pltpu.VMEM(suffix_values.shape, BF16),
        pltpu.VMEM((own_rows, slots * page), F32),
    ]
    state = [
        pltpu.VMEM(page_table.shape[::-1], jnp.int32),
        pltpu.VMEM((STEPS, samples, HD), F32),
        pltpu.VMEM((STEPS, samples, HD), F32),
        pltpu.VMEM((samples, depth), BF16),
        pltpu.VMEM((samples, depth), F32),
    ]
    dma = pltpu.SemaphoreType.DMA
    if paired:
        pairs = kv // 2
        pieces = 2
        body = functools.partial(
            chip_kernel, chips, sides, heads, kv, group, float(depth * ranks)
        )
        scratch = [
            pltpu.SMEM(suffix_lengths.shape, jnp.int32),
            pltpu.VMEM((1, depth), F32),
            pltpu.VMEM((1, HD), F32),
        ] + state + weights + [
            pltpu.VMEM((chips, group + 2, gen, HD), BF16),
            pltpu.VMEM((ranks, per, gen, HD), BF16),
            pltpu.VMEM((group + 2, gen, HD), F32),
            pltpu.VMEM((1, HD), F32),
            pltpu.VMEM((ranks, 1, HD), F32),
            pltpu.VMEM((all_heads, gen, HD), BF16),
            pltpu.VMEM((STEPS, gen, HD), F32),
            pltpu.VMEM((STEPS, gen, HD), F32),
            pltpu.VMEM((pairs, 2, unit_rows, HD), F32),
            pltpu.VMEM((pairs, 2, unit_rows, HD), F32),
            pltpu.VMEM((pairs, unit_rows, HD), F32),
            pltpu.VMEM((pairs, unit_rows, HD), F32),
            pltpu.VMEM((pairs, chips, unit_rows, HD), BF16),
            pltpu.VMEM((pairs, chips, 1, unit_rows), F32),
            pltpu.VMEM((pairs, unit_rows, HD), F32),
            pltpu.VMEM((kv * group, gen, HD), BF16),
            pltpu.VMEM((STEPS, heads, samples, depth), BF16),
            dma((4 * kv + 5,)),
            dma((3, ranks)),
            dma((3, ranks)),
            dma((pairs, 2)),
            dma((pairs, 2)),
            dma((pairs, chips, 2)),
            dma((pairs, chips, 2)),
            dma((pairs,)),
            dma((pairs,)),
            dma((STEPS, heads, pieces)),
            dma((STEPS, heads, pieces)),
            dma((5,)),
            dma((3,)),
        ]
    else:
        body = functools.partial(
            kernel, ranks, sides, heads, prompts, kv, group, float(depth * ranks)
        )
        scratch = state + weights + [
            pltpu.VMEM((ranks, per, gen, HD), BF16),
            pltpu.VMEM((ranks, per, gen, HD), BF16),
            pltpu.VMEM((per, gen, HD), F32),
            pltpu.VMEM((1, HD), F32),
            pltpu.VMEM((ranks, 1, HD), F32),
            pltpu.VMEM((ranks * per, gen, HD), BF16),
            pltpu.VMEM((STEPS, gen, HD), F32),
            pltpu.VMEM((STEPS, gen, HD), F32),
            pltpu.VMEM((units * unit_rows, HD), BF16),
            pltpu.VMEM((units, 1, unit_rows), F32),
            pltpu.VMEM((ranks, rows, HD), BF16),
            pltpu.VMEM((ranks, 1, unit_rows), F32),
            pltpu.VMEM((prompts * kv * group, gen, HD), BF16),
            pltpu.VMEM((samples, depth), F32),
            pltpu.VMEM((STEPS, heads, samples, depth), BF16),
            dma((3 * kv + 5,)),
            dma((6, ranks)),
            dma((6, ranks)),
            dma((STEPS, heads)),
            dma((STEPS, heads)),
            dma((3,)),
        ]

    vmem = pl.BlockSpec(memory_space=pltpu.VMEM)
    smem = pl.BlockSpec(memory_space=pltpu.SMEM)
    hbm = pl.BlockSpec(memory_space=pl.ANY)
    store = pl.BlockSpec(memory_space=pltpu.HBM)
    first = [store] * 5 if paired else [smem, store] + [vmem] * 3
    held, added, last = pl.pallas_call(
        body,
        out_shape=(
            jax.ShapeDtypeStruct((samples, depth), BF16),
            jax.ShapeDtypeStruct((samples, depth), F32),
            jax.ShapeDtypeStruct((heads, samples, depth), BF16),
        ),
        in_specs=first + [hbm] * 8,
        out_specs=(store, store, store),
        scratch_shapes=scratch,
        compiler_params=pltpu.CompilerParams(
            collective_id=0, has_side_effects=True, vmem_limit_bytes=60 * 1024 * 1024
        ),
    )(
        suffix_lengths, page_table.T, hidden, gain.reshape(1, depth), freq,
        w_query, w_key, w_value, w_out, prefix_keys, prefix_values, suffix_keys, suffix_values,
    )
    delta = last[0].astype(F32)
    for n in range(1, heads):
        delta = delta + last[n].astype(F32)
    return (held.astype(F32) + delta).astype(BF16), added + delta


def solution(mesh):
    placed = (
        P("groups", ("seq", "side")),
        P(("seq", "side")),
        P(("seq", "side"), "head"),
        P(("seq", "side"), "head"),
        P(("seq", "side"), "head"),
        P("head", ("seq", "side")),
        P("groups", "head", ("seq", "side"), None),
        P("groups", "head", ("seq", "side"), None),
        P(("groups", "seq", "side"), "head", None, None),
        P(("groups", "seq", "side"), "head", None, None),
        P("groups"),
        P("groups", None),
    )
    ranks = mesh.shape["seq"] * mesh.shape["side"]
    return jax.shard_map(
        functools.partial(local, ranks, mesh.shape["side"], mesh.shape["head"]),
        mesh=mesh,
        in_specs=placed,
        out_specs=(P("groups", ("seq", "side")), P("groups", ("seq", "side"))),
        check_vma=False,
    )
```

```python
import functools
import math

import jax
import jax.numpy as jnp
import numpy as np
from jax import lax
from jax.experimental import pallas as pl
from jax.experimental.pallas import tpu as pltpu
from jax.sharding import PartitionSpec as P

HD = 128
STEPS = 3
LOW = -1e30
BASE2 = math.log2(math.e) / math.sqrt(HD)
LOG2E = math.log2(math.e)
MESH = pl.DeviceIdType.MESH
F32 = jnp.float32
BF16 = jnp.bfloat16
NT = (((1,), (1,)), ((), ()))
TN = (((0,), (0,)), ((), ()))


def kernel(
    ranks, sides, heads, prompts, kv, group, width,
    lens, table_hbm, x_in, gain, freq, wq, wk, wv, wo, pk, pv, sk, sv,
    h_hbm, u_hbm, c_hbm,
    table, cosine, sine, h_out, u_out, w_s, wo_s, pk_s, pv_s, sk_s, sv_s, bias, send_a, recv_a, own_a, sq_send, sq_recv,
    qkv, fresh_k, fresh_v, outs, lse, recv_b, recv_l, mix, part, cbuf,
    load_sem, send_sem, recv_sem, send_c, recv_c, out_sem,
):
    samples = x_in.shape[0]
    gen = samples // prompts
    own_count = samples // ranks
    q_heads = kv * group
    all_heads = q_heads + 2 * kv
    blocks = all_heads * prompts
    per = qkv.shape[0] // ranks
    unit_rows = group * gen
    units = prompts * kv
    rows = units * unit_rows // ranks
    row_blocks = rows // gen
    span = pk_s.shape[2]
    slots, page = sk_s.shape[0], sk_s.shape[2]
    pages = table.shape[0]
    suffix = slots * page
    own_rows = own_count * group

    me = lax.axis_index("seq") * sides + lax.axis_index("side")
    head_me = lax.axis_index("head")

    def rank_id(d):
        return {"seq": lax.div(d, sides), "side": lax.rem(d, sides)}

    per_unit = group + 2
    owners = per_unit // per
    loads = []
    for k in range(kv):
        base = k * per_unit * HD
        for source, first, count in ((wq, 0, group), (wk, group, 1), (wv, group + 1, 1)):
            loads.append(
                pltpu.make_async_copy(
                    source.at[:, pl.ds(k * count * HD, count * HD)],
                    w_s.at[:, pl.ds(base + first * HD, count * HD)],
                    load_sem.at[len(loads)],
                )
            )
    table_load = pltpu.make_async_copy(table_hbm, table, out_sem.at[0])
    table_load.start()
    for load in loads:
        load.start()
    later = [
        pltpu.make_async_copy(source, target, load_sem.at[len(loads) + n])
        for n, (source, target) in enumerate(
            ((pk, pk_s), (pv, pv_s), (sk, sk_s), (sv, sv_s), (wo, wo_s))
        )
    ]

    barrier = pltpu.get_barrier_semaphore()
    for o in range(1, ranks):
        pl.semaphore_signal(
            barrier, inc=1, device_id=rank_id(lax.rem(me + o, ranks)), device_id_type=MESH
        )
    for o in range(1, heads):
        pl.semaphore_signal(
            barrier, inc=1, device_id={"head": lax.rem(head_me + o, heads)}, device_id_type=MESH
        )

    start = (me + 1 - 2 * lax.rem(me, 2)) * own_count
    own_prompt = lax.div(start, gen)
    own_first = lax.rem(start, gen)
    line = lax.broadcasted_iota(jnp.int32, (own_rows, suffix), 0)
    column = lax.broadcasted_iota(jnp.int32, (own_rows, suffix), 1)
    which = lax.rem(line, own_count)
    slot = lax.div(column, page)
    offset = lax.rem(column, page)
    place = jnp.full((own_rows, suffix), 1 << 28, jnp.int32)
    length = jnp.zeros((own_rows, suffix), jnp.int32)
    table_load.wait()
    table_line = lax.broadcasted_iota(jnp.int32, table.shape, 1)
    for j in range(own_count):
        mine = which == j
        entries = jnp.sum(
            jnp.where(table_line == start + j, table[...], 0), axis=1, keepdims=True
        )
        length = jnp.where(mine, lens[start + j], length)
        for n in range(pages):
            hit = jnp.logical_and(mine, slot == entries[n : n + 1, :])
            place = jnp.where(hit, n * page + offset, place)
    bias[...] = jnp.where(place < length, 0.0, LOW).astype(F32)
    sample_line = lax.broadcasted_iota(jnp.int32, (samples, HD), 0)
    position = jnp.full((samples, HD), span * ranks, jnp.int32)
    for n in range(samples):
        position = jnp.where(sample_line == n, position + lens[n], position)
    low_half = lax.broadcasted_iota(jnp.int32, (samples, HD), 1) < HD // 2
    for n in range(STEPS):
        angle = (position + n).astype(F32) * freq[...]
        turn = jnp.sin(angle)
        cosine[n] = jnp.cos(angle)
        sine[n] = jnp.where(low_half, -turn, turn)
    fresh_k[...] = jnp.zeros_like(fresh_k)
    fresh_v[...] = jnp.zeros_like(fresh_v)
    h_out[...] = x_in[...]
    u_out[...] = jnp.zeros_like(u_out)

    pl.semaphore_wait(barrier, ranks - 1 + heads - 1)

    sel_row = lax.broadcasted_iota(jnp.int32, (own_rows, unit_rows), 0)
    sel_col = lax.broadcasted_iota(jnp.int32, (own_rows, unit_rows), 1)
    target = lax.div(sel_row, own_count) * gen + own_first + lax.rem(sel_row, own_count)
    chosen = jnp.where(sel_col == target, 1.0, 0.0).astype(F32)
    gen_line = lax.broadcasted_iota(jnp.int32, (gen, HD), 0)

    def spread(lines, fill):
        found = []
        for g in range(group):
            value = jnp.full((gen, HD), fill, F32)
            for j in range(own_count):
                row = lines[g * own_count + j : g * own_count + j + 1]
                value = jnp.where(gen_line == own_first + j, row, value)
            found.append(value)
        return jnp.concatenate(found, axis=0)


    my_block = me * row_blocks
    my_unit = lax.div(my_block, group)
    my_q = my_unit * per_unit + lax.rem(my_block, group)
    my_k = my_unit * per_unit + group
    my_shift = lax.rem(me * rows, unit_rows)

    def copy(src, dst, phase, o, d):
        return pltpu.make_async_remote_copy(
            src_ref=src,
            dst_ref=dst,
            send_sem=send_sem.at[phase, o],
            recv_sem=recv_sem.at[phase, o],
            device_id=rank_id(d),
            device_id_type=MESH,
        )

    def sq_copy(o, d):
        return copy(sq_send, sq_recv.at[o], 0, o, d)

    def a_copy(o, d):
        return copy(send_a.at[d], recv_a.at[o], 1, o, d)

    def q_copy(o, d, owner):
        place = qkv.at[pl.ds(owner * per, per)]
        return copy(place, place, 2, o, d)

    def b_copy(o, d):
        return copy(outs.at[pl.ds(pl.multiple_of(d * rows, rows), rows)], recv_b.at[o], 3, o, d)

    def l_copy(o, d):
        return copy(lse.at[lax.div(d * rows, unit_rows)], recv_l.at[o], 4, o, d)

    def m_copy(o, d, owner):
        place = mix.at[pl.ds(owner * row_blocks, row_blocks)]
        return copy(place, place, 5, o, d)

    def c_copy(t, o):
        return pltpu.make_async_remote_copy(
            src_ref=cbuf.at[t, head_me],
            dst_ref=cbuf.at[t, head_me],
            send_sem=send_c.at[t, o],
            recv_sem=recv_c.at[t, o],
            device_id={"head": lax.rem(head_me + o, heads)},
            device_id_type=MESH,
        )

    def c_arrival(t, o):
        source = lax.rem(head_me + heads - o, heads)
        return pltpu.make_async_remote_copy(
            src_ref=cbuf.at[t, source],
            dst_ref=cbuf.at[t, source],
            send_sem=send_c.at[t, o],
            recv_sem=recv_c.at[t, o],
            device_id={"head": source},
            device_id_type=MESH,
        )

    def ahead(o):
        return lax.rem(me + o, ranks)

    def behind(o):
        return lax.rem(me + ranks - o, ranks)

    far_first = sorted(range(1, ranks), key=lambda o: abs(2 * o - ranks))

    def step(t, carry):
        wide = h_out[...].astype(F32)
        scaled = (wide * gain[...]).astype(BF16)
        squares = jnp.sum(wide * wide, axis=1, keepdims=True)
        diag_r = lax.broadcasted_iota(jnp.int32, (samples, HD), 0)
        diag_c = lax.broadcasted_iota(jnp.int32, (samples, HD), 1)
        sq_send[...] = jnp.sum(jnp.where(diag_r == diag_c, squares, 0.0), axis=0, keepdims=True)
        for o in range(1, ranks):
            sq_copy(o, ahead(o)).start()

        @pl.when(t == 0)
        def _():
            for load in loads:
                load.wait()
            for load in later:
                load.start()

        def chunk(d):
            if prompts == 1 and blocks == per * ranks:
                wide_cols = per * HD
                cols = pl.ds(pl.multiple_of(d * wide_cols, wide_cols), wide_cols)
                got = jnp.dot(scaled, w_s[:, cols], preferred_element_type=F32)
                return [got[:, i * HD : (i + 1) * HD] for i in range(per)]
            found = []
            for i in range(per):
                b = jnp.minimum(d * per + i, blocks - 1)
                p = lax.div(b, all_heads)
                cols = pl.ds(pl.multiple_of(lax.rem(b, all_heads) * HD, HD), HD)
                got = jnp.dot(scaled, w_s[:, cols], preferred_element_type=F32)
                pick = got[0:gen]
                for n in range(1, prompts):
                    pick = jnp.where(p == n, got[n * gen : (n + 1) * gen], pick)
                found.append(pick)
            return found

        for o in far_first:
            d = ahead(o)
            for i, piece in enumerate(chunk(d)):
                send_a[d, i] = piece.astype(BF16)
            a_copy(o, d).start()
        for i, piece in enumerate(chunk(me)):
            own_a[i] = piece

        total = sq_send[...]
        for o in range(1, ranks):
            sq_copy(o, ahead(o)).wait_recv()
            total = total + sq_recv[o]
        total = jnp.sum(jnp.where(diag_r == diag_c, total, 0.0), axis=1, keepdims=True)
        inverse = lax.rsqrt(total / width + 1e-05)
        for o in range(1, ranks):
            a_copy(o, ahead(o)).wait_recv()
        for i in range(per):
            value = own_a[i]
            for o in range(1, ranks):
                value = value + recv_a[o, i].astype(F32)
            b = jnp.minimum(me * per + i, blocks - 1)
            p = lax.div(b, all_heads)
            plain = lax.rem(b, per_unit) == per_unit - 1
            inv, cos, sin = inverse[0:gen], cosine[t, 0:gen], sine[t, 0:gen]
            for n in range(1, prompts):
                band = slice(n * gen, (n + 1) * gen)
                inv = jnp.where(p == n, inverse[band], inv)
                cos = jnp.where(p == n, cosine[t, band], cos)
                sin = jnp.where(p == n, sine[t, band], sin)
            value = value * inv
            turned = value * cos + pltpu.roll(value, HD // 2, 1) * sin
            qkv[me * per + i] = jnp.where(plain, value, turned).astype(BF16)
        for o in far_first:
            q_copy(o, ahead(o), me).start()

        def q_arrived(owner):
            @pl.when(owner != me)
            def _():
                q_copy(lax.rem(me - owner + ranks, ranks), owner, owner).wait_recv()

        @pl.when(t == 0)
        def _():
            for load in later[:4]:
                load.wait()

        def unit(i, carry):
            u = lax.rem(my_unit + 2 * lax.div(i, 2), units)
            u = u + lax.rem(i, 2) * (1 - 2 * lax.rem(u, 2))
            for n in range(owners):
                q_arrived(u * owners + n)
            p = lax.div(u, kv)
            k = lax.rem(u, kv)
            q = qkv[pl.ds(u * per_unit, group)].reshape(unit_rows, HD)
            size = min(span, 1024)
            q_own = jnp.dot(chosen.astype(BF16), q, preferred_element_type=F32).astype(BF16)
            scores = [
                lax.dot_general(q, pk_s[p, k, c : c + size], NT, preferred_element_type=F32)
                for c in range(0, span, size)
            ]
            near = lax.dot_general(
                q_own, sk_s[:, k].reshape(suffix, HD), NT, preferred_element_type=F32
            ) + bias[...]

            def soft(s, values):
                top = jnp.max(s, axis=1, keepdims=True)
                e = jnp.exp2((s - top) * BASE2)
                total = jnp.sum(e, axis=1, keepdims=True)
                return top, total, jnp.dot(e.astype(BF16), values, preferred_element_type=F32)

            parts = [
                soft(s, pv_s[p, k, n * size : (n + 1) * size]) for n, s in enumerate(scores)
            ]
            near_top, near_sum, near_acc = soft(near, sv_s[:, k].reshape(suffix, HD))
            near_top = jnp.where(p == own_prompt, near_top, LOW)
            parts.append(
                (
                    spread(jnp.broadcast_to(near_top, (own_rows, HD)), LOW),
                    spread(jnp.broadcast_to(near_sum, (own_rows, HD)), 0.0),
                    spread(near_acc, 0.0),
                )
            )
            best = functools.reduce(jnp.maximum, [part[0] for part in parts])
            amount = jnp.zeros((unit_rows, HD), F32)
            acc = jnp.zeros((unit_rows, HD), F32)
            for part_top, part_sum, part_acc in parts:
                weight = jnp.exp2((part_top - best) * BASE2)
                amount = amount + weight * part_sum
                acc = acc + weight * part_acc
            outs[pl.ds(pl.multiple_of(u * unit_rows, unit_rows), unit_rows)] = (
                acc / amount
            ).astype(BF16)
            level = best * BASE2 + jnp.log(amount) * LOG2E
            eye_r = lax.broadcasted_iota(jnp.int32, (unit_rows, unit_rows), 0)
            eye_c = lax.broadcasted_iota(jnp.int32, (unit_rows, unit_rows), 1)
            lse[u] = jnp.sum(jnp.where(eye_r == eye_c, level, 0.0), axis=0, keepdims=True)
            for j in range(unit_rows // rows):
                d = u * (unit_rows // rows) + j

                @pl.when(d != me)
                def _():
                    o = lax.rem(d - me + ranks, ranks)
                    l_copy(o, d).start()
                    b_copy(o, d).start()

            return carry

        lax.fori_loop(0, units, unit, 0)
        for n in range(units * owners, ranks):
            q_arrived(n)

        fresh_k[t] = qkv[my_k].astype(F32)
        fresh_v[t] = qkv[my_k + 1].astype(F32)
        mine = qkv[pl.ds(my_q, row_blocks)].reshape(rows, HD).astype(F32)
        new_scores = []
        for n in range(STEPS):
            keys = jnp.concatenate([fresh_k[n]] * row_blocks, axis=0)
            s = jnp.sum(mine * keys, axis=1, keepdims=True) * BASE2
            new_scores.append(jnp.where(n <= t, s, LOW))
        pick_r = lax.broadcasted_iota(jnp.int32, (rows, unit_rows), 0)
        pick_c = lax.broadcasted_iota(jnp.int32, (rows, unit_rows), 1)

        def as_column(row):
            return jnp.sum(jnp.where(pick_c == pick_r + my_shift, row, 0.0), axis=1, keepdims=True)

        levels = [as_column(lse[my_unit])]
        for o in range(1, ranks):
            l_copy(o, ahead(o)).wait_recv()
            levels.append(as_column(recv_l[o]))
        best = functools.reduce(jnp.maximum, levels + new_scores)
        amount = jnp.zeros((rows, 1), F32)
        acc = jnp.zeros((rows, HD), F32)
        for n in range(STEPS):
            e = jnp.where(n <= t, jnp.exp2(new_scores[n] - best), 0.0)
            amount = amount + e
            acc = acc + e * jnp.concatenate([fresh_v[n]] * row_blocks, axis=0)
        for o in range(ranks):
            e = jnp.exp2(levels[o] - best)
            amount = amount + e
            if o == 0:
                got = outs[pl.ds(pl.multiple_of(me * rows, rows), rows)]
            else:
                b_copy(o, ahead(o)).wait_recv()
                got = recv_b[o]
            acc = acc + e * got.astype(F32)
        mix[pl.ds(my_block, row_blocks)] = (
            (acc / amount).astype(BF16).reshape(row_blocks, gen, HD)
        )
        for o in far_first:
            m_copy(o, ahead(o), me).start()

        @pl.when(t == 0)
        def _():
            later[4].wait()

        part[...] = jnp.zeros_like(part)
        for o in [0] + far_first[::-1]:
            d = behind(o)
            if o > 0:
                m_copy(o, ahead(o), d).wait_recv()
            b = d * row_blocks
            p = lax.div(b, q_heads)
            left = jnp.concatenate([mix[b + i] for i in range(row_blocks)], axis=1)
            depth = row_blocks * HD
            right = wo_s[pl.ds(pl.multiple_of(lax.rem(b, q_heads) * HD, HD), depth)]
            band = pl.ds(pl.multiple_of(p * gen, gen), gen)
            part[band] += jnp.dot(left, right, preferred_element_type=F32)
        cbuf[t, head_me] = part[...].astype(BF16)
        for o in range(1, heads):
            c_copy(t, o).start()
        for o in range(1, ranks):
            sq_copy(o, ahead(o)).wait_send()
            a_copy(o, ahead(o)).wait_send()
            q_copy(o, ahead(o), me).wait_send()
            l_copy(o, ahead(o)).wait_send()
            b_copy(o, ahead(o)).wait_send()
            m_copy(o, ahead(o), me).wait_send()
        for o in range(1, heads):
            c_arrival(t, o).wait_recv()

        @pl.when(t < STEPS - 1)
        def _():
            delta = cbuf[t, 0].astype(F32)
            for n in range(1, heads):
                delta = delta + cbuf[t, n].astype(F32)
            u_out[...] += delta
            h_out[...] = (h_out[...].astype(F32) + delta).astype(BF16)

        for o in range(1, heads):
            c_copy(t, o).wait_send()
        return carry

    lax.fori_loop(0, STEPS, step, 0)
    stores = [
        pltpu.make_async_copy(h_out, h_hbm, out_sem.at[0]),
        pltpu.make_async_copy(u_out, u_hbm, out_sem.at[1]),
        pltpu.make_async_copy(cbuf.at[STEPS - 1], c_hbm, out_sem.at[2]),
    ]
    for store in stores:
        store.start()
    for store in stores:
        store.wait()


def chip_kernel(
    chips, sides, heads, kv, group, width,
    lens_hbm, table_hbm, x_in, gain_hbm, freq_hbm, wq, wk, wv, wo, pk, pv, sk, sv,
    h_hbm, u_hbm, c_hbm,
    lens, gain, freq, table, cosine, sine, h_out, u_out, w_s, wo_s, pk_s, pv_s, sk_s, sv_s, bias,
    send_a, recv_a, own_a, sq_send, sq_recv, qkv, fresh_k, fresh_v,
    box_o, box_l, got_o, got_l, zone, zone_l, zone_c, mix, cbuf,
    load_sem, send_sem, recv_sem, send_p, recv_p, send_z, recv_z, send_m, recv_m,
    send_c, recv_c, small_sem, out_sem,
):
    samples = x_in.shape[0]
    depth = x_in.shape[1]
    gen = samples
    ranks = chips * sides
    own_count = samples // ranks
    per_unit = group + 2
    per = per_unit // sides
    half = group // sides
    unit_rows = group * gen
    pairs = kv // 2
    span = pk_s.shape[2]
    slots, page = sk_s.shape[0], sk_s.shape[2]
    pages = table.shape[0]
    suffix = slots * page
    own_rows = own_count * group
    pieces = recv_c.shape[2]
    piece = depth // pieces

    z = lax.axis_index("seq")
    side = lax.axis_index("side")
    me = z * sides + side
    head_me = lax.axis_index("head")
    order = list(range(chips - 1, -1, -1))
    peers = [(x, y) for x in order for y in range(sides) if x or y]

    def flip(v, x):
        bit = 1
        while bit <= x:
            if x & bit:
                v = v + bit * (1 - 2 * lax.rem(lax.div(v, bit), 2))
            bit *= 2
        return v

    def peer_rank(x, y):
        return flip(z, x) * sides + flip(side, y)

    def rank_id(d):
        return {"seq": lax.div(d, sides), "side": lax.rem(d, sides)}

    unit_width = per_unit * HD

    def w_loads(u):
        found = []
        base = u * unit_width
        pieces_of = (
            (wq, u * group, 0, half),
            (wk, u, half, 1),
            (wq, u * group + half, half + 1, half),
            (wv, u, 2 * half + 1, 1),
        )
        for n, (source, block, first, count) in enumerate(pieces_of):
            found.append(
                pltpu.make_async_copy(
                    source.at[:, pl.ds(pl.multiple_of(block * HD, HD), count * HD)],
                    w_s.at[:, pl.ds(pl.multiple_of(base + first * HD, HD), count * HD)],
                    load_sem.at[u * len(pieces_of) + n],
                )
            )
        return found

    small = [
        pltpu.make_async_copy(source, target, small_sem.at[n])
        for n, (source, target) in enumerate(
            ((x_in, h_out), (gain_hbm, gain), (lens_hbm, lens), (freq_hbm, freq), (table_hbm, table))
        )
    ]
    for load in small:
        load.start()
    for x in order:
        for load in w_loads(flip(z, x)):
            load.start()
    later = [
        pltpu.make_async_copy(source, target, load_sem.at[4 * kv + n])
        for n, (source, target) in enumerate(
            ((pk, pk_s), (pv, pv_s), (sk, sk_s), (sv, sv_s), (wo, wo_s))
        )
    ]

    barrier = pltpu.get_barrier_semaphore()
    for x, y in peers:
        pl.semaphore_signal(
            barrier, inc=1, device_id=rank_id(peer_rank(x, y)), device_id_type=MESH
        )
    for o in range(1, heads):
        pl.semaphore_signal(
            barrier, inc=1, device_id={"head": lax.rem(head_me + o, heads)}, device_id_type=MESH
        )

    u_out[...] = jnp.zeros_like(u_out)
    fresh_k[...] = jnp.zeros_like(fresh_k)
    fresh_v[...] = jnp.zeros_like(fresh_v)
    start = (me + 1 - 2 * lax.rem(me, 2)) * own_count

    def prepare():
        for load in small[2:]:
            load.wait()
        sample_line = lax.broadcasted_iota(jnp.int32, (samples, HD), 0)
        position = jnp.full((samples, HD), span * ranks, jnp.int32)
        for n in range(samples):
            position = jnp.where(sample_line == n, position + lens[n], position)
        low_half = lax.broadcasted_iota(jnp.int32, (samples, HD), 1) < HD // 2
        for n in range(STEPS):
            angle = (position + n).astype(F32) * freq[...]
            turn = jnp.sin(angle)
            cosine[n] = jnp.cos(angle)
            sine[n] = jnp.where(low_half, -turn, turn)
        line = lax.broadcasted_iota(jnp.int32, (own_rows, suffix), 0)
        column = lax.broadcasted_iota(jnp.int32, (own_rows, suffix), 1)
        which = lax.rem(line, own_count)
        slot = lax.div(column, page)
        offset = lax.rem(column, page)
        place = jnp.full((own_rows, suffix), 1 << 28, jnp.int32)
        length = jnp.zeros((own_rows, suffix), jnp.int32)
        table_line = lax.broadcasted_iota(jnp.int32, table.shape, 1)
        for j in range(own_count):
            mine = which == j
            entries = jnp.sum(
                jnp.where(table_line == start + j, table[...], 0), axis=1, keepdims=True
            )
            length = jnp.where(mine, lens[start + j], length)
            for n in range(pages):
                hit = jnp.logical_and(mine, slot == entries[n : n + 1, :])
                place = jnp.where(hit, n * page + offset, place)
        bias[...] = jnp.where(place < length, 0.0, LOW).astype(F32)

    for load in small[:2]:
        load.wait()
    pl.semaphore_wait(barrier, ranks - 1 + heads - 1)

    sel_row = lax.broadcasted_iota(jnp.int32, (own_rows, unit_rows), 0)
    sel_col = lax.broadcasted_iota(jnp.int32, (own_rows, unit_rows), 1)
    target = lax.div(sel_row, own_count) * gen + start + lax.rem(sel_row, own_count)
    chosen = jnp.where(sel_col == target, 1.0, 0.0).astype(BF16)
    gen_line = lax.broadcasted_iota(jnp.int32, (gen, HD), 0)

    def spread(lines, fill):
        found = []
        for g in range(group):
            value = jnp.full((gen, HD), fill, F32)
            for j in range(own_count):
                row = lines[g * own_count + j : g * own_count + j + 1]
                value = jnp.where(gen_line == start + j, row, value)
            found.append(value)
        return jnp.concatenate(found, axis=0)

    def eye():
        rows = lax.broadcasted_iota(jnp.int32, (unit_rows, unit_rows), 0)
        return rows == lax.broadcasted_iota(jnp.int32, (unit_rows, unit_rows), 1)

    def push(src, dst, phase, x, y):
        return pltpu.make_async_remote_copy(
            src_ref=src,
            dst_ref=dst,
            send_sem=send_sem.at[phase, x * sides + y],
            recv_sem=recv_sem.at[phase, me],
            device_id=rank_id(peer_rank(x, y)),
            device_id_type=MESH,
        )

    def arrived(dst, phase, source):
        pltpu.make_async_remote_copy(
            src_ref=dst,
            dst_ref=dst,
            send_sem=send_sem.at[phase, 0],
            recv_sem=recv_sem.at[phase, source],
            device_id=rank_id(source),
            device_id_type=MESH,
        ).wait_recv()

    def sq_copy(x, y):
        return push(sq_send, sq_recv.at[me], 0, x, y)

    def a_copy(x, y):
        return push(
            send_a.at[x, pl.ds(flip(side, y) * per, per)], recv_a.at[me], 1, x, y
        )

    def q_copy(x, y):
        place = qkv.at[pl.ds(me * per, half if x else per)]
        return push(place, place, 2, x, y)

    def p_copy(j, n):
        src, dst = ((box_o, got_o), (box_l, got_l))[n]
        return pltpu.make_async_remote_copy(
            src_ref=src.at[j, 1],
            dst_ref=dst.at[j],
            send_sem=send_p.at[j, n],
            recv_sem=recv_p.at[j, n],
            device_id={"side": 1 - side},
            device_id_type=MESH,
        )

    def z_copy(v, x, n, source, dest):
        buffer = (zone_l, zone)[n]
        return pltpu.make_async_remote_copy(
            src_ref=buffer.at[v, source],
            dst_ref=buffer.at[v, source],
            send_sem=send_z.at[v, x, n],
            recv_sem=recv_z.at[v, source, n],
            device_id={"seq": dest},
            device_id_type=MESH,
        )

    def m_copy(v, owner):
        place = mix.at[pl.ds((2 * v + owner) * group, group)]
        return pltpu.make_async_remote_copy(
            src_ref=place,
            dst_ref=place,
            send_sem=send_m.at[v],
            recv_sem=recv_m.at[v],
            device_id={"side": 1 - side},
            device_id_type=MESH,
        )

    def c_copy(t, o, n, source, dest, final):
        columns = pl.ds(n * piece, piece)
        place = cbuf.at[t, source, :, columns]
        return pltpu.make_async_remote_copy(
            src_ref=place,
            dst_ref=c_hbm.at[source, :, columns] if final else place,
            send_sem=send_c.at[t, o, n],
            recv_sem=recv_c.at[t, o, n],
            device_id={"head": dest},
            device_id_type=MESH,
        )

    def c_send(t, o, n, final):
        return c_copy(t, o, n, head_me, lax.rem(head_me + o, heads), final)

    def c_arrival(t, o, n, final):
        source = lax.rem(head_me + heads - o, heads)
        return c_copy(t, o, n, source, source, final)

    def either(t, act):
        @pl.when(t < STEPS - 1)
        def _():
            act(False)

        @pl.when(t == STEPS - 1)
        def _():
            act(True)

    def unit_queries(u):
        first = qkv[pl.ds(u * per_unit, half)]
        second = qkv[pl.ds(u * per_unit + per, half)]
        return jnp.concatenate([first, second], axis=0).reshape(unit_rows, HD)

    def out_part(u, first, count):
        left = jnp.concatenate([mix[u * group + i] for i in range(group)], axis=1)
        rows = pl.ds(pl.multiple_of(u * group * HD, HD), group * HD)
        return jnp.dot(
            left, wo_s[rows, first : first + count], preferred_element_type=F32
        )

    def step(t, carry):
        wide = h_out[...].astype(F32)
        scaled = (wide * gain[...]).astype(BF16)
        diag_r = lax.broadcasted_iota(jnp.int32, (samples, HD), 0)
        diag_c = lax.broadcasted_iota(jnp.int32, (samples, HD), 1)

        for x in order:
            u = flip(z, x)

            @pl.when(t == 0)
            def _():
                for load in w_loads(u):
                    load.wait()

            cols = pl.ds(pl.multiple_of(u * unit_width, HD), unit_width)
            got = jnp.dot(scaled, w_s[:, cols], preferred_element_type=F32)
            for i in range(per_unit):
                send_a[x, i] = got[:, i * HD : (i + 1) * HD].astype(BF16)
                if x == 0:
                    own_a[i] = got[:, i * HD : (i + 1) * HD]
            for y in range(sides):
                if x or y:
                    a_copy(x, y).start()
            if x == order[0]:
                squares = jnp.sum(wide * wide, axis=1, keepdims=True)
                sq_send[...] = jnp.sum(
                    jnp.where(diag_r == diag_c, squares, 0.0), axis=0, keepdims=True
                )
                for xx, yy in peers:
                    sq_copy(xx, yy).start()

        @pl.when(t == 0)
        def _():
            for load in later:
                load.start()
            prepare()

        total = sq_send[...]
        for x, y in peers:
            d = peer_rank(x, y)
            arrived(sq_recv.at[d], 0, d)
            total = total + sq_recv[d]
        total = jnp.sum(jnp.where(diag_r == diag_c, total, 0.0), axis=1, keepdims=True)
        inverse = lax.rsqrt(total / width + 1e-05)
        for x, y in peers:
            d = peer_rank(x, y)
            arrived(recv_a.at[d], 1, d)
        for i in range(per):
            value = own_a[side * per + i]
            for x, y in peers:
                value = value + recv_a[peer_rank(x, y), i].astype(F32)
            value = value * inverse
            turned = value * cosine[t] + pltpu.roll(value, HD // 2, 1) * sine[t]
            if i == half:
                turned = jnp.where(side == sides - 1, value, turned)
            qkv[me * per + i] = turned.astype(BF16)
        for x, y in [(0, 1)] + peers[::-1][1:]:
            q_copy(x, y).start()

        @pl.when(t == 0)
        def _():
            for load in later[:4]:
                load.wait()

        def pair_at(j):
            return lax.rem(lax.div(z, 2) + j, pairs)

        def blend(levels, values):
            best = functools.reduce(jnp.maximum, levels)
            amount = jnp.zeros((unit_rows, HD), F32)
            acc = jnp.zeros((unit_rows, HD), F32)
            for level, value in zip(levels, values):
                e = jnp.exp2(level - best)
                amount = amount + e
                acc = acc + e * value.astype(F32)
            return acc / amount, best + jnp.log(amount) * LOG2E

        def add_new():
            mine = unit_queries(z).astype(F32)
            levels, values = [box_l[0, 0]], [box_o[0, 0]]
            for n in range(STEPS):
                keys = jnp.concatenate([fresh_k[n]] * group, axis=0)
                score = jnp.sum(mine * keys, axis=1, keepdims=True) * BASE2
                score = jnp.where(n <= t, score, LOW)
                levels.append(jnp.broadcast_to(score, (unit_rows, HD)))
                values.append(jnp.concatenate([fresh_v[n]] * group, axis=0))
            value, level = blend(levels, values)
            box_o[0, 0] = value
            box_l[0, 0] = level

        def merge(j):
            v = pair_at(j)
            for n in range(2):
                p_copy(j, n).wait_recv()
            value, level = blend([box_l[j, 0], got_l[j]], [box_o[j, 0], got_o[j]])
            zone[v, z] = value.astype(BF16)
            zone_c[v] = level
            zone_l[v, z] = jnp.sum(jnp.where(eye(), level, 0.0), axis=0, keepdims=True)
            for x in order[:-1]:
                for n in range(2):
                    z_copy(v, x, n, z, flip(z, x)).start()

        def unit(i, carry):
            j = lax.div(i, 2)
            sub = lax.rem(i, 2)
            near_pair = lax.rem(z + sub, 2)
            far_pair = lax.rem(1 - side + sub, 2)
            late = lax.div(j + pairs - 1, pairs)
            parity = near_pair + late * (far_pair - near_pair)
            u = 2 * pair_at(j) + parity
            k = u
            for n in range(sides):
                owner = u * sides + n

                @pl.when(jnp.logical_and(u == z, owner != me))
                def _():
                    arrived(qkv.at[pl.ds(owner * per, per)], 2, owner)

                @pl.when(u != z)
                def _():
                    arrived(qkv.at[pl.ds(owner * per, half)], 2, owner)

            q = unit_queries(u)
            size = min(span, 1024)
            q_own = jnp.dot(chosen, q, preferred_element_type=F32).astype(BF16)
            scores = [
                lax.dot_general(q, pk_s[0, k, c : c + size], NT, preferred_element_type=F32)
                for c in range(0, span, size)
            ]
            near = lax.dot_general(
                q_own, sk_s[:, k].reshape(suffix, HD), NT, preferred_element_type=F32
            ) + bias[...]

            def soft(s, values):
                top = jnp.max(s, axis=1, keepdims=True)
                e = jnp.exp2((s - top) * BASE2)
                total = jnp.sum(e, axis=1, keepdims=True)
                return top, total, jnp.dot(e.astype(BF16), values, preferred_element_type=F32)

            parts = [
                soft(s, pv_s[0, k, n * size : (n + 1) * size]) for n, s in enumerate(scores)
            ]
            near_top, near_sum, near_acc = soft(near, sv_s[:, k].reshape(suffix, HD))
            parts.append(
                (
                    spread(jnp.broadcast_to(near_top, (own_rows, HD)), LOW),
                    spread(jnp.broadcast_to(near_sum, (own_rows, HD)), 0.0),
                    spread(near_acc, 0.0),
                )
            )
            best = functools.reduce(jnp.maximum, [part[0] for part in parts])
            amount = jnp.zeros((unit_rows, HD), F32)
            acc = jnp.zeros((unit_rows, HD), F32)
            for part_top, part_sum, part_acc in parts:
                weight = jnp.exp2((part_top - best) * BASE2)
                amount = amount + weight * part_sum
                acc = acc + weight * part_acc
            away = lax.rem(parity + side, 2)
            box_o[j, away] = acc / amount
            box_l[j, away] = best * BASE2 + jnp.log(amount) * LOG2E

            @pl.when(away == 1)
            def _():
                for n in range(2):
                    p_copy(j, n).start()

            @pl.when(jnp.logical_and(i == 1, lax.rem(z + side, 2) == 0))
            def _():
                fresh_k[t] = qkv[z * per_unit + half].astype(F32)
                fresh_v[t] = qkv[z * per_unit + per + half].astype(F32)
                add_new()

            @pl.when(sub == 1)
            def _():
                merge(j)

            return carry

        lax.fori_loop(0, kv, unit, 0)

        @pl.when(t == 0)
        def _():
            later[4].wait()

        def settle(v, carry):
            levels, values = [zone_c[v]], [zone[v, z]]
            for x in order[:-1]:
                source = flip(z, x)
                for n in range(2):
                    z_copy(v, x, n, source, source).wait_recv()
                levels.append(
                    jnp.sum(jnp.where(eye(), zone_l[v, source], 0.0), axis=1, keepdims=True)
                )
                values.append(zone[v, source])
            value, _ = blend(levels, values)
            mix[pl.ds((2 * v + side) * group, group)] = value.astype(BF16).reshape(group, gen, HD)
            m_copy(v, side).start()
            return carry

        lax.fori_loop(0, pairs, settle, 0)

        def sum_out(i, part):
            v = lax.rem(i, pairs)
            theirs = lax.div(i, pairs)

            @pl.when(theirs == 1)
            def _():
                m_copy(v, 1 - side).wait_recv()

            return part + out_part(2 * v + lax.rem(side + theirs, 2), 0, depth)

        part = lax.fori_loop(0, 2 * pairs, sum_out, jnp.zeros((samples, depth), F32))
        for n in range(pieces):
            total = part[:, n * piece : (n + 1) * piece]
            cbuf[t, head_me, :, n * piece : (n + 1) * piece] = total.astype(BF16)

            def send(final):
                for o in range(1, heads):
                    c_send(t, o, n, final).start()

            either(t, send)

        @pl.when(t == STEPS - 1)
        def _():
            stores[2].start()

        for x, y in peers:
            sq_copy(x, y).wait_send()
            a_copy(x, y).wait_send()
            q_copy(x, y).wait_send()
        for j in range(pairs):
            for n in range(2):
                p_copy(j, n).wait_send()
            for x in order[:-1]:
                for n in range(2):
                    z_copy(j, x, n, z, flip(z, x)).wait_send()
            m_copy(j, side).wait_send()

        def finish(final):
            for n in range(pieces):
                for o in range(1, heads):
                    c_arrival(t, o, n, final).wait_recv()
            if not final:
                delta = cbuf[t, 0].astype(F32)
                for n in range(1, heads):
                    delta = delta + cbuf[t, n].astype(F32)
                u_out[...] += delta
                h_out[...] = (h_out[...].astype(F32) + delta).astype(BF16)
            for n in range(pieces):
                for o in range(1, heads):
                    c_send(t, o, n, final).wait_send()

        either(t, finish)

        @pl.when(t == STEPS - 2)
        def _():
            for store in stores[:2]:
                store.start()

        return carry

    stores = [
        pltpu.make_async_copy(h_out, h_hbm, out_sem.at[0]),
        pltpu.make_async_copy(u_out, u_hbm, out_sem.at[1]),
        pltpu.make_async_copy(cbuf.at[STEPS - 1, head_me], c_hbm.at[head_me], out_sem.at[2]),
    ]
    lax.fori_loop(0, STEPS, step, 0)
    for store in stores:
        store.wait()


def local(
    ranks, sides, heads,
    hidden, gain, w_query, w_key, w_value, w_out, prefix_keys, prefix_values,
    suffix_keys, suffix_values, suffix_lengths, page_table,
):
    samples, depth = hidden.shape
    prompts, kv, span, _ = prefix_keys.shape
    group = w_query.shape[1] // w_key.shape[1]
    gen = samples // prompts
    slots, _, page, _ = suffix_keys.shape
    own_rows = samples // ranks * group
    all_heads = kv * (group + 2)
    per = -(-all_heads * prompts // ranks)
    unit_rows = group * gen
    units = prompts * kv
    rows = units * unit_rows // ranks

    power = -np.arange(HD // 2, dtype=np.float64) * 2.0 / HD
    freq = np.tile(500000.0 ** power, 2).astype(np.float32).reshape(1, HD)

    chips = ranks // sides
    paired = (
        prompts == 1
        and sides == 2
        and kv == chips
        and kv >= 4
        and chips & (chips - 1) == 0
        and samples % ranks == 0
        and group % 2 == 0
    )
    weights = [
        pltpu.VMEM((depth, all_heads * HD), BF16),
        pltpu.VMEM(w_out.shape, BF16),
        pltpu.VMEM(prefix_keys.shape, BF16),
        pltpu.VMEM(prefix_values.shape, BF16),
        pltpu.VMEM(suffix_keys.shape, BF16),
        pltpu.VMEM(suffix_values.shape, BF16),
        pltpu.VMEM((own_rows, slots * page), F32),
    ]
    state = [
        pltpu.VMEM(page_table.shape[::-1], jnp.int32),
        pltpu.VMEM((STEPS, samples, HD), F32),
        pltpu.VMEM((STEPS, samples, HD), F32),
        pltpu.VMEM((samples, depth), BF16),
        pltpu.VMEM((samples, depth), F32),
    ]
    dma = pltpu.SemaphoreType.DMA
    if paired:
        pairs = kv // 2
        pieces = 1
        body = functools.partial(
            chip_kernel, chips, sides, heads, kv, group, float(depth * ranks)
        )
        scratch = [
            pltpu.SMEM(suffix_lengths.shape, jnp.int32),
            pltpu.VMEM((1, depth), F32),
            pltpu.VMEM((1, HD), F32),
        ] + state + weights + [
            pltpu.VMEM((chips, group + 2, gen, HD), BF16),
            pltpu.VMEM((ranks, per, gen, HD), BF16),
            pltpu.VMEM((group + 2, gen, HD), F32),
            pltpu.VMEM((1, HD), F32),
            pltpu.VMEM((ranks, 1, HD), F32),
            pltpu.VMEM((all_heads, gen, HD), BF16),
            pltpu.VMEM((STEPS, gen, HD), F32),
            pltpu.VMEM((STEPS, gen, HD), F32),
            pltpu.VMEM((pairs, 2, unit_rows, HD), F32),
            pltpu.VMEM((pairs, 2, unit_rows, HD), F32),
            pltpu.VMEM((pairs, unit_rows, HD), F32),
            pltpu.VMEM((pairs, unit_rows, HD), F32),
            pltpu.VMEM((pairs, chips, unit_rows, HD), BF16),
            pltpu.VMEM((pairs, chips, 1, unit_rows), F32),
            pltpu.VMEM((pairs, unit_rows, HD), F32),
            pltpu.VMEM((kv * group, gen, HD), BF16),
            pltpu.VMEM((STEPS, heads, samples, depth), BF16),
            dma((4 * kv + 5,)),
            dma((3, ranks)),
            dma((3, ranks)),
            dma((pairs, 2)),
            dma((pairs, 2)),
            dma((pairs, chips, 2)),
            dma((pairs, chips, 2)),
            dma((pairs,)),
            dma((pairs,)),
            dma((STEPS, heads, pieces)),
            dma((STEPS, heads, pieces)),
            dma((5,)),
            dma((3,)),
        ]
    else:
        body = functools.partial(
            kernel, ranks, sides, heads, prompts, kv, group, float(depth * ranks)
        )
        scratch = state + weights + [
            pltpu.VMEM((ranks, per, gen, HD), BF16),
            pltpu.VMEM((ranks, per, gen, HD), BF16),
            pltpu.VMEM((per, gen, HD), F32),
            pltpu.VMEM((1, HD), F32),
            pltpu.VMEM((ranks, 1, HD), F32),
            pltpu.VMEM((ranks * per, gen, HD), BF16),
            pltpu.VMEM((STEPS, gen, HD), F32),
            pltpu.VMEM((STEPS, gen, HD), F32),
            pltpu.VMEM((units * unit_rows, HD), BF16),
            pltpu.VMEM((units, 1, unit_rows), F32),
            pltpu.VMEM((ranks, rows, HD), BF16),
            pltpu.VMEM((ranks, 1, unit_rows), F32),
            pltpu.VMEM((prompts * kv * group, gen, HD), BF16),
            pltpu.VMEM((samples, depth), F32),
            pltpu.VMEM((STEPS, heads, samples, depth), BF16),
            dma((3 * kv + 5,)),
            dma((6, ranks)),
            dma((6, ranks)),
            dma((STEPS, heads)),
            dma((STEPS, heads)),
            dma((3,)),
        ]

    vmem = pl.BlockSpec(memory_space=pltpu.VMEM)
    smem = pl.BlockSpec(memory_space=pltpu.SMEM)
    hbm = pl.BlockSpec(memory_space=pl.ANY)
    store = pl.BlockSpec(memory_space=pltpu.HBM)
    first = [store] * 5 if paired else [smem, store] + [vmem] * 3
    held, added, last = pl.pallas_call(
        body,
        out_shape=(
            jax.ShapeDtypeStruct((samples, depth), BF16),
            jax.ShapeDtypeStruct((samples, depth), F32),
            jax.ShapeDtypeStruct((heads, samples, depth), BF16),
        ),
        in_specs=first + [hbm] * 8,
        out_specs=(store, store, store),
        scratch_shapes=scratch,
        compiler_params=pltpu.CompilerParams(
            collective_id=0, has_side_effects=True, vmem_limit_bytes=60 * 1024 * 1024
        ),
    )(
        suffix_lengths, page_table.T, hidden, gain.reshape(1, depth), freq,
        w_query, w_key, w_value, w_out, prefix_keys, prefix_values, suffix_keys, suffix_values,
    )
    delta = last[0].astype(F32)
    for n in range(1, heads):
        delta = delta + last[n].astype(F32)
    return (held.astype(F32) + delta).astype(BF16), added + delta


def solution(mesh):
    placed = (
        P("groups", ("seq", "side")),
        P(("seq", "side")),
        P(("seq", "side"), "head"),
        P(("seq", "side"), "head"),
        P(("seq", "side"), "head"),
        P("head", ("seq", "side")),
        P("groups", "head", ("seq", "side"), None),
        P("groups", "head", ("seq", "side"), None),
        P(("groups", "seq", "side"), "head", None, None),
        P(("groups", "seq", "side"), "head", None, None),
        P("groups"),
        P("groups", None),
    )
    ranks = mesh.shape["seq"] * mesh.shape["side"]
    return jax.shard_map(
        functools.partial(local, ranks, mesh.shape["side"], mesh.shape["head"]),
        mesh=mesh,
        in_specs=placed,
        out_specs=(P("groups", ("seq", "side")), P("groups", ("seq", "side"))),
        check_vma=False,
    )
```

```python
import functools
import math

import jax
import jax.numpy as jnp
import numpy as np
from jax import lax
from jax.experimental import pallas as pl
from jax.experimental.pallas import tpu as pltpu
from jax.sharding import PartitionSpec as P

HD = 128
STEPS = 3
LOW = -1e30
BASE2 = math.log2(math.e) / math.sqrt(HD)
LOG2E = math.log2(math.e)
MESH = pl.DeviceIdType.MESH
F32 = jnp.float32
BF16 = jnp.bfloat16
NT = (((1,), (1,)), ((), ()))
TN = (((0,), (0,)), ((), ()))


def kernel(
    ranks, sides, heads, prompts, kv, group, width,
    lens, table_hbm, x_in, gain, freq, wq, wk, wv, wo, pk, pv, sk, sv,
    h_hbm, u_hbm, c_hbm,
    table, cosine, sine, h_out, u_out, w_s, wo_s, pk_s, pv_s, sk_s, sv_s, bias, send_a, recv_a, own_a, sq_send, sq_recv,
    qkv, fresh_k, fresh_v, outs, lse, recv_b, recv_l, mix, part, cbuf,
    load_sem, send_sem, recv_sem, send_c, recv_c, out_sem,
):
    samples = x_in.shape[0]
    gen = samples // prompts
    own_count = samples // ranks
    q_heads = kv * group
    all_heads = q_heads + 2 * kv
    blocks = all_heads * prompts
    per = qkv.shape[0] // ranks
    unit_rows = group * gen
    units = prompts * kv
    rows = units * unit_rows // ranks
    row_blocks = rows // gen
    span = pk_s.shape[2]
    slots, page = sk_s.shape[0], sk_s.shape[2]
    pages = table.shape[0]
    suffix = slots * page
    own_rows = own_count * group

    me = lax.axis_index("seq") * sides + lax.axis_index("side")
    head_me = lax.axis_index("head")

    def rank_id(d):
        return {"seq": lax.div(d, sides), "side": lax.rem(d, sides)}

    per_unit = group + 2
    owners = per_unit // per
    loads = []
    for k in range(kv):
        base = k * per_unit * HD
        for source, first, count in ((wq, 0, group), (wk, group, 1), (wv, group + 1, 1)):
            loads.append(
                pltpu.make_async_copy(
                    source.at[:, pl.ds(k * count * HD, count * HD)],
                    w_s.at[:, pl.ds(base + first * HD, count * HD)],
                    load_sem.at[len(loads)],
                )
            )
    table_load = pltpu.make_async_copy(table_hbm, table, out_sem.at[0])
    table_load.start()
    for load in loads:
        load.start()
    later = [
        pltpu.make_async_copy(source, target, load_sem.at[len(loads) + n])
        for n, (source, target) in enumerate(
            ((pk, pk_s), (pv, pv_s), (sk, sk_s), (sv, sv_s), (wo, wo_s))
        )
    ]

    barrier = pltpu.get_barrier_semaphore()
    for o in range(1, ranks):
        pl.semaphore_signal(
            barrier, inc=1, device_id=rank_id(lax.rem(me + o, ranks)), device_id_type=MESH
        )
    for o in range(1, heads):
        pl.semaphore_signal(
            barrier, inc=1, device_id={"head": lax.rem(head_me + o, heads)}, device_id_type=MESH
        )

    start = (me + 1 - 2 * lax.rem(me, 2)) * own_count
    own_prompt = lax.div(start, gen)
    own_first = lax.rem(start, gen)
    line = lax.broadcasted_iota(jnp.int32, (own_rows, suffix), 0)
    column = lax.broadcasted_iota(jnp.int32, (own_rows, suffix), 1)
    which = lax.rem(line, own_count)
    slot = lax.div(column, page)
    offset = lax.rem(column, page)
    place = jnp.full((own_rows, suffix), 1 << 28, jnp.int32)
    length = jnp.zeros((own_rows, suffix), jnp.int32)
    table_load.wait()
    table_line = lax.broadcasted_iota(jnp.int32, table.shape, 1)
    for j in range(own_count):
        mine = which == j
        entries = jnp.sum(
            jnp.where(table_line == start + j, table[...], 0), axis=1, keepdims=True
        )
        length = jnp.where(mine, lens[start + j], length)
        for n in range(pages):
            hit = jnp.logical_and(mine, slot == entries[n : n + 1, :])
            place = jnp.where(hit, n * page + offset, place)
    bias[...] = jnp.where(place < length, 0.0, LOW).astype(F32)
    sample_line = lax.broadcasted_iota(jnp.int32, (samples, HD), 0)
    position = jnp.full((samples, HD), span * ranks, jnp.int32)
    for n in range(samples):
        position = jnp.where(sample_line == n, position + lens[n], position)
    low_half = lax.broadcasted_iota(jnp.int32, (samples, HD), 1) < HD // 2
    for n in range(STEPS):
        angle = (position + n).astype(F32) * freq[...]
        turn = jnp.sin(angle)
        cosine[n] = jnp.cos(angle)
        sine[n] = jnp.where(low_half, -turn, turn)
    fresh_k[...] = jnp.zeros_like(fresh_k)
    fresh_v[...] = jnp.zeros_like(fresh_v)
    h_out[...] = x_in[...]
    u_out[...] = jnp.zeros_like(u_out)

    pl.semaphore_wait(barrier, ranks - 1 + heads - 1)

    sel_row = lax.broadcasted_iota(jnp.int32, (own_rows, unit_rows), 0)
    sel_col = lax.broadcasted_iota(jnp.int32, (own_rows, unit_rows), 1)
    target = lax.div(sel_row, own_count) * gen + own_first + lax.rem(sel_row, own_count)
    chosen = jnp.where(sel_col == target, 1.0, 0.0).astype(F32)
    gen_line = lax.broadcasted_iota(jnp.int32, (gen, HD), 0)

    def spread(lines, fill):
        found = []
        for g in range(group):
            value = jnp.full((gen, HD), fill, F32)
            for j in range(own_count):
                row = lines[g * own_count + j : g * own_count + j + 1]
                value = jnp.where(gen_line == own_first + j, row, value)
            found.append(value)
        return jnp.concatenate(found, axis=0)


    my_block = me * row_blocks
    my_unit = lax.div(my_block, group)
    my_q = my_unit * per_unit + lax.rem(my_block, group)
    my_k = my_unit * per_unit + group
    my_shift = lax.rem(me * rows, unit_rows)

    def copy(src, dst, phase, o, d):
        return pltpu.make_async_remote_copy(
            src_ref=src,
            dst_ref=dst,
            send_sem=send_sem.at[phase, o],
            recv_sem=recv_sem.at[phase, o],
            device_id=rank_id(d),
            device_id_type=MESH,
        )

    def sq_copy(o, d):
        return copy(sq_send, sq_recv.at[o], 0, o, d)

    def a_copy(o, d):
        return copy(send_a.at[d], recv_a.at[o], 1, o, d)

    def q_copy(o, d, owner):
        place = qkv.at[pl.ds(owner * per, per)]
        return copy(place, place, 2, o, d)

    def b_copy(o, d):
        return copy(outs.at[pl.ds(pl.multiple_of(d * rows, rows), rows)], recv_b.at[o], 3, o, d)

    def l_copy(o, d):
        return copy(lse.at[lax.div(d * rows, unit_rows)], recv_l.at[o], 4, o, d)

    def m_copy(o, d, owner):
        place = mix.at[pl.ds(owner * row_blocks, row_blocks)]
        return copy(place, place, 5, o, d)

    def c_copy(t, o):
        return pltpu.make_async_remote_copy(
            src_ref=cbuf.at[t, head_me],
            dst_ref=cbuf.at[t, head_me],
            send_sem=send_c.at[t, o],
            recv_sem=recv_c.at[t, o],
            device_id={"head": lax.rem(head_me + o, heads)},
            device_id_type=MESH,
        )

    def c_arrival(t, o):
        source = lax.rem(head_me + heads - o, heads)
        return pltpu.make_async_remote_copy(
            src_ref=cbuf.at[t, source],
            dst_ref=cbuf.at[t, source],
            send_sem=send_c.at[t, o],
            recv_sem=recv_c.at[t, o],
            device_id={"head": source},
            device_id_type=MESH,
        )

    def ahead(o):
        return lax.rem(me + o, ranks)

    def behind(o):
        return lax.rem(me + ranks - o, ranks)

    far_first = sorted(range(1, ranks), key=lambda o: abs(2 * o - ranks))

    def step(t, carry):
        wide = h_out[...].astype(F32)
        scaled = (wide * gain[...]).astype(BF16)
        squares = jnp.sum(wide * wide, axis=1, keepdims=True)
        diag_r = lax.broadcasted_iota(jnp.int32, (samples, HD), 0)
        diag_c = lax.broadcasted_iota(jnp.int32, (samples, HD), 1)
        sq_send[...] = jnp.sum(jnp.where(diag_r == diag_c, squares, 0.0), axis=0, keepdims=True)
        for o in range(1, ranks):
            sq_copy(o, ahead(o)).start()

        @pl.when(t == 0)
        def _():
            for load in loads:
                load.wait()
            for load in later:
                load.start()

        def chunk(d):
            if prompts == 1 and blocks == per * ranks:
                wide_cols = per * HD
                cols = pl.ds(pl.multiple_of(d * wide_cols, wide_cols), wide_cols)
                got = jnp.dot(scaled, w_s[:, cols], preferred_element_type=F32)
                return [got[:, i * HD : (i + 1) * HD] for i in range(per)]
            found = []
            for i in range(per):
                b = jnp.minimum(d * per + i, blocks - 1)
                p = lax.div(b, all_heads)
                cols = pl.ds(pl.multiple_of(lax.rem(b, all_heads) * HD, HD), HD)
                got = jnp.dot(scaled, w_s[:, cols], preferred_element_type=F32)
                pick = got[0:gen]
                for n in range(1, prompts):
                    pick = jnp.where(p == n, got[n * gen : (n + 1) * gen], pick)
                found.append(pick)
            return found

        for o in far_first:
            d = ahead(o)
            for i, piece in enumerate(chunk(d)):
                send_a[d, i] = piece.astype(BF16)
            a_copy(o, d).start()
        for i, piece in enumerate(chunk(me)):
            own_a[i] = piece

        total = sq_send[...]
        for o in range(1, ranks):
            sq_copy(o, ahead(o)).wait_recv()
            total = total + sq_recv[o]
        total = jnp.sum(jnp.where(diag_r == diag_c, total, 0.0), axis=1, keepdims=True)
        inverse = lax.rsqrt(total / width + 1e-05)
        for o in range(1, ranks):
            a_copy(o, ahead(o)).wait_recv()
        for i in range(per):
            value = own_a[i]
            for o in range(1, ranks):
                value = value + recv_a[o, i].astype(F32)
            b = jnp.minimum(me * per + i, blocks - 1)
            p = lax.div(b, all_heads)
            plain = lax.rem(b, per_unit) == per_unit - 1
            inv, cos, sin = inverse[0:gen], cosine[t, 0:gen], sine[t, 0:gen]
            for n in range(1, prompts):
                band = slice(n * gen, (n + 1) * gen)
                inv = jnp.where(p == n, inverse[band], inv)
                cos = jnp.where(p == n, cosine[t, band], cos)
                sin = jnp.where(p == n, sine[t, band], sin)
            value = value * inv
            turned = value * cos + pltpu.roll(value, HD // 2, 1) * sin
            qkv[me * per + i] = jnp.where(plain, value, turned).astype(BF16)
        for o in far_first:
            q_copy(o, ahead(o), me).start()

        def q_arrived(owner):
            @pl.when(owner != me)
            def _():
                q_copy(lax.rem(me - owner + ranks, ranks), owner, owner).wait_recv()

        @pl.when(t == 0)
        def _():
            for load in later[:4]:
                load.wait()

        def unit(i, carry):
            u = lax.rem(my_unit + 2 * lax.div(i, 2), units)
            u = u + lax.rem(i, 2) * (1 - 2 * lax.rem(u, 2))
            for n in range(owners):
                q_arrived(u * owners + n)
            p = lax.div(u, kv)
            k = lax.rem(u, kv)
            q = qkv[pl.ds(u * per_unit, group)].reshape(unit_rows, HD)
            size = min(span, 1024)
            q_own = jnp.dot(chosen.astype(BF16), q, preferred_element_type=F32).astype(BF16)
            scores = [
                lax.dot_general(q, pk_s[p, k, c : c + size], NT, preferred_element_type=F32)
                for c in range(0, span, size)
            ]
            near = lax.dot_general(
                q_own, sk_s[:, k].reshape(suffix, HD), NT, preferred_element_type=F32
            ) + bias[...]

            def soft(s, values):
                top = jnp.max(s, axis=1, keepdims=True)
                e = jnp.exp2((s - top) * BASE2)
                total = jnp.sum(e, axis=1, keepdims=True)
                return top, total, jnp.dot(e.astype(BF16), values, preferred_element_type=F32)

            parts = [
                soft(s, pv_s[p, k, n * size : (n + 1) * size]) for n, s in enumerate(scores)
            ]
            near_top, near_sum, near_acc = soft(near, sv_s[:, k].reshape(suffix, HD))
            near_top = jnp.where(p == own_prompt, near_top, LOW)
            parts.append(
                (
                    spread(jnp.broadcast_to(near_top, (own_rows, HD)), LOW),
                    spread(jnp.broadcast_to(near_sum, (own_rows, HD)), 0.0),
                    spread(near_acc, 0.0),
                )
            )
            best = functools.reduce(jnp.maximum, [part[0] for part in parts])
            amount = jnp.zeros((unit_rows, HD), F32)
            acc = jnp.zeros((unit_rows, HD), F32)
            for part_top, part_sum, part_acc in parts:
                weight = jnp.exp2((part_top - best) * BASE2)
                amount = amount + weight * part_sum
                acc = acc + weight * part_acc
            outs[pl.ds(pl.multiple_of(u * unit_rows, unit_rows), unit_rows)] = (
                acc / amount
            ).astype(BF16)
            level = best * BASE2 + jnp.log(amount) * LOG2E
            eye_r = lax.broadcasted_iota(jnp.int32, (unit_rows, unit_rows), 0)
            eye_c = lax.broadcasted_iota(jnp.int32, (unit_rows, unit_rows), 1)
            lse[u] = jnp.sum(jnp.where(eye_r == eye_c, level, 0.0), axis=0, keepdims=True)
            for j in range(unit_rows // rows):
                d = u * (unit_rows // rows) + j

                @pl.when(d != me)
                def _():
                    o = lax.rem(d - me + ranks, ranks)
                    l_copy(o, d).start()
                    b_copy(o, d).start()

            return carry

        lax.fori_loop(0, units, unit, 0)
        for n in range(units * owners, ranks):
            q_arrived(n)

        fresh_k[t] = qkv[my_k].astype(F32)
        fresh_v[t] = qkv[my_k + 1].astype(F32)
        mine = qkv[pl.ds(my_q, row_blocks)].reshape(rows, HD).astype(F32)
        new_scores = []
        for n in range(STEPS):
            keys = jnp.concatenate([fresh_k[n]] * row_blocks, axis=0)
            s = jnp.sum(mine * keys, axis=1, keepdims=True) * BASE2
            new_scores.append(jnp.where(n <= t, s, LOW))
        pick_r = lax.broadcasted_iota(jnp.int32, (rows, unit_rows), 0)
        pick_c = lax.broadcasted_iota(jnp.int32, (rows, unit_rows), 1)

        def as_column(row):
            return jnp.sum(jnp.where(pick_c == pick_r + my_shift, row, 0.0), axis=1, keepdims=True)

        levels = [as_column(lse[my_unit])]
        for o in range(1, ranks):
            l_copy(o, ahead(o)).wait_recv()
            levels.append(as_column(recv_l[o]))
        best = functools.reduce(jnp.maximum, levels + new_scores)
        amount = jnp.zeros((rows, 1), F32)
        acc = jnp.zeros((rows, HD), F32)
        for n in range(STEPS):
            e = jnp.where(n <= t, jnp.exp2(new_scores[n] - best), 0.0)
            amount = amount + e
            acc = acc + e * jnp.concatenate([fresh_v[n]] * row_blocks, axis=0)
        for o in range(ranks):
            e = jnp.exp2(levels[o] - best)
            amount = amount + e
            if o == 0:
                got = outs[pl.ds(pl.multiple_of(me * rows, rows), rows)]
            else:
                b_copy(o, ahead(o)).wait_recv()
                got = recv_b[o]
            acc = acc + e * got.astype(F32)
        mix[pl.ds(my_block, row_blocks)] = (
            (acc / amount).astype(BF16).reshape(row_blocks, gen, HD)
        )
        for o in far_first:
            m_copy(o, ahead(o), me).start()

        @pl.when(t == 0)
        def _():
            later[4].wait()

        part[...] = jnp.zeros_like(part)
        for o in [0] + far_first[::-1]:
            d = behind(o)
            if o > 0:
                m_copy(o, ahead(o), d).wait_recv()
            b = d * row_blocks
            p = lax.div(b, q_heads)
            left = jnp.concatenate([mix[b + i] for i in range(row_blocks)], axis=1)
            depth = row_blocks * HD
            right = wo_s[pl.ds(pl.multiple_of(lax.rem(b, q_heads) * HD, HD), depth)]
            band = pl.ds(pl.multiple_of(p * gen, gen), gen)
            part[band] += jnp.dot(left, right, preferred_element_type=F32)
        cbuf[t, head_me] = part[...].astype(BF16)
        for o in range(1, heads):
            c_copy(t, o).start()
        for o in range(1, ranks):
            sq_copy(o, ahead(o)).wait_send()
            a_copy(o, ahead(o)).wait_send()
            q_copy(o, ahead(o), me).wait_send()
            l_copy(o, ahead(o)).wait_send()
            b_copy(o, ahead(o)).wait_send()
            m_copy(o, ahead(o), me).wait_send()
        for o in range(1, heads):
            c_arrival(t, o).wait_recv()

        @pl.when(t < STEPS - 1)
        def _():
            delta = cbuf[t, 0].astype(F32)
            for n in range(1, heads):
                delta = delta + cbuf[t, n].astype(F32)
            u_out[...] += delta
            h_out[...] = (h_out[...].astype(F32) + delta).astype(BF16)

        for o in range(1, heads):
            c_copy(t, o).wait_send()
        return carry

    lax.fori_loop(0, STEPS, step, 0)
    stores = [
        pltpu.make_async_copy(h_out, h_hbm, out_sem.at[0]),
        pltpu.make_async_copy(u_out, u_hbm, out_sem.at[1]),
        pltpu.make_async_copy(cbuf.at[STEPS - 1], c_hbm, out_sem.at[2]),
    ]
    for store in stores:
        store.start()
    for store in stores:
        store.wait()


def chip_kernel(
    chips, sides, heads, kv, group, width,
    lens_hbm, table_hbm, x_in, gain_hbm, freq_hbm, wq, wk, wv, wo, pk, pv, sk, sv,
    h_hbm, u_hbm, c_hbm,
    lens, gain, freq, table, cosine, sine, h_out, u_out, w_s, wo_s, pk_s, pv_s, sk_s, sv_s, bias,
    send_a, recv_a, own_a, sq_send, sq_recv, qkv, fresh_k, fresh_v,
    box_o, box_l, got_o, got_l, zone, zone_l, zone_c, mix, cbuf,
    load_sem, send_sem, recv_sem, send_p, recv_p, send_z, recv_z, send_m, recv_m,
    send_c, recv_c, small_sem, out_sem,
):
    samples = x_in.shape[0]
    depth = x_in.shape[1]
    gen = samples
    ranks = chips * sides
    own_count = samples // ranks
    per_unit = group + 2
    per = per_unit // sides
    half = group // sides
    unit_rows = group * gen
    pairs = kv // 2
    span = pk_s.shape[2]
    slots, page = sk_s.shape[0], sk_s.shape[2]
    pages = table.shape[0]
    suffix = slots * page
    own_rows = own_count * group
    pieces = recv_c.shape[2]
    piece = depth // pieces

    z = lax.axis_index("seq")
    side = lax.axis_index("side")
    me = z * sides + side
    head_me = lax.axis_index("head")
    order = list(range(chips - 1, -1, -1))
    peers = [(x, y) for x in order for y in range(sides) if x or y]

    def flip(v, x):
        bit = 1
        while bit <= x:
            if x & bit:
                v = v + bit * (1 - 2 * lax.rem(lax.div(v, bit), 2))
            bit *= 2
        return v

    def peer_rank(x, y):
        return flip(z, x) * sides + flip(side, y)

    def rank_id(d):
        return {"seq": lax.div(d, sides), "side": lax.rem(d, sides)}

    unit_width = per_unit * HD

    def w_loads(u):
        found = []
        base = u * unit_width
        pieces_of = (
            (wq, u * group, 0, half),
            (wk, u, half, 1),
            (wq, u * group + half, half + 1, half),
            (wv, u, 2 * half + 1, 1),
        )
        for n, (source, block, first, count) in enumerate(pieces_of):
            found.append(
                pltpu.make_async_copy(
                    source.at[:, pl.ds(pl.multiple_of(block * HD, HD), count * HD)],
                    w_s.at[:, pl.ds(pl.multiple_of(base + first * HD, HD), count * HD)],
                    load_sem.at[u * len(pieces_of) + n],
                )
            )
        return found

    small = [
        pltpu.make_async_copy(source, target, small_sem.at[n])
        for n, (source, target) in enumerate(
            ((x_in, h_out), (gain_hbm, gain), (lens_hbm, lens), (freq_hbm, freq), (table_hbm, table))
        )
    ]
    for load in small:
        load.start()
    for x in order:
        for load in w_loads(flip(z, x)):
            load.start()
    later = [
        pltpu.make_async_copy(source, target, load_sem.at[4 * kv + n])
        for n, (source, target) in enumerate(
            ((pk, pk_s), (pv, pv_s), (sk, sk_s), (sv, sv_s), (wo, wo_s))
        )
    ]

    barrier = pltpu.get_barrier_semaphore()
    for x, y in peers:
        pl.semaphore_signal(
            barrier, inc=1, device_id=rank_id(peer_rank(x, y)), device_id_type=MESH
        )
    for o in range(1, heads):
        pl.semaphore_signal(
            barrier, inc=1, device_id={"head": lax.rem(head_me + o, heads)}, device_id_type=MESH
        )

    u_out[...] = jnp.zeros_like(u_out)
    fresh_k[...] = jnp.zeros_like(fresh_k)
    fresh_v[...] = jnp.zeros_like(fresh_v)
    start = (me + 1 - 2 * lax.rem(me, 2)) * own_count

    def prepare():
        for load in small[2:]:
            load.wait()
        sample_line = lax.broadcasted_iota(jnp.int32, (samples, HD), 0)
        position = jnp.full((samples, HD), span * ranks, jnp.int32)
        for n in range(samples):
            position = jnp.where(sample_line == n, position + lens[n], position)
        low_half = lax.broadcasted_iota(jnp.int32, (samples, HD), 1) < HD // 2
        for n in range(STEPS):
            angle = (position + n).astype(F32) * freq[...]
            turn = jnp.sin(angle)
            cosine[n] = jnp.cos(angle)
            sine[n] = jnp.where(low_half, -turn, turn)
        line = lax.broadcasted_iota(jnp.int32, (own_rows, suffix), 0)
        column = lax.broadcasted_iota(jnp.int32, (own_rows, suffix), 1)
        which = lax.rem(line, own_count)
        slot = lax.div(column, page)
        offset = lax.rem(column, page)
        place = jnp.full((own_rows, suffix), 1 << 28, jnp.int32)
        length = jnp.zeros((own_rows, suffix), jnp.int32)
        table_line = lax.broadcasted_iota(jnp.int32, table.shape, 1)
        for j in range(own_count):
            mine = which == j
            entries = jnp.sum(
                jnp.where(table_line == start + j, table[...], 0), axis=1, keepdims=True
            )
            length = jnp.where(mine, lens[start + j], length)
            for n in range(pages):
                hit = jnp.logical_and(mine, slot == entries[n : n + 1, :])
                place = jnp.where(hit, n * page + offset, place)
        bias[...] = jnp.where(place < length, 0.0, LOW).astype(F32)

    for load in small[:2]:
        load.wait()
    pl.semaphore_wait(barrier, ranks - 1 + heads - 1)

    sel_row = lax.broadcasted_iota(jnp.int32, (own_rows, unit_rows), 0)
    sel_col = lax.broadcasted_iota(jnp.int32, (own_rows, unit_rows), 1)
    target = lax.div(sel_row, own_count) * gen + start + lax.rem(sel_row, own_count)
    chosen = jnp.where(sel_col == target, 1.0, 0.0).astype(BF16)
    gen_line = lax.broadcasted_iota(jnp.int32, (gen, HD), 0)

    def spread(lines, fill):
        found = []
        for g in range(group):
            value = jnp.full((gen, HD), fill, F32)
            for j in range(own_count):
                row = lines[g * own_count + j : g * own_count + j + 1]
                value = jnp.where(gen_line == start + j, row, value)
            found.append(value)
        return jnp.concatenate(found, axis=0)

    def eye():
        rows = lax.broadcasted_iota(jnp.int32, (unit_rows, unit_rows), 0)
        return rows == lax.broadcasted_iota(jnp.int32, (unit_rows, unit_rows), 1)

    def push(src, dst, phase, x, y):
        return pltpu.make_async_remote_copy(
            src_ref=src,
            dst_ref=dst,
            send_sem=send_sem.at[phase, x * sides + y],
            recv_sem=recv_sem.at[phase, me],
            device_id=rank_id(peer_rank(x, y)),
            device_id_type=MESH,
        )

    def arrived(dst, phase, source):
        pltpu.make_async_remote_copy(
            src_ref=dst,
            dst_ref=dst,
            send_sem=send_sem.at[phase, 0],
            recv_sem=recv_sem.at[phase, source],
            device_id=rank_id(source),
            device_id_type=MESH,
        ).wait_recv()

    def sq_copy(x, y):
        return push(sq_send, sq_recv.at[me], 0, x, y)

    def a_copy(x, y):
        return push(
            send_a.at[x, pl.ds(flip(side, y) * per, per)], recv_a.at[me], 1, x, y
        )

    def q_copy(x, y):
        place = qkv.at[pl.ds(me * per, half if x else per)]
        return push(place, place, 2, x, y)

    def p_copy(j, n):
        src, dst = ((box_o, got_o), (box_l, got_l))[n]
        return pltpu.make_async_remote_copy(
            src_ref=src.at[j, 1],
            dst_ref=dst.at[j],
            send_sem=send_p.at[j, n],
            recv_sem=recv_p.at[j, n],
            device_id={"side": 1 - side},
            device_id_type=MESH,
        )

    def z_copy(v, x, n, source, dest):
        buffer = (zone_l, zone)[n]
        return pltpu.make_async_remote_copy(
            src_ref=buffer.at[v, source],
            dst_ref=buffer.at[v, source],
            send_sem=send_z.at[v, x, n],
            recv_sem=recv_z.at[v, source, n],
            device_id={"seq": dest},
            device_id_type=MESH,
        )

    def m_copy(v, owner):
        place = mix.at[pl.ds((2 * v + owner) * group, group)]
        return pltpu.make_async_remote_copy(
            src_ref=place,
            dst_ref=place,
            send_sem=send_m.at[v],
            recv_sem=recv_m.at[v],
            device_id={"side": 1 - side},
            device_id_type=MESH,
        )

    def c_copy(t, o, n, source, dest, final):
        columns = pl.ds(n * piece, piece)
        place = cbuf.at[t, source, :, columns]
        return pltpu.make_async_remote_copy(
            src_ref=place,
            dst_ref=c_hbm.at[source, :, columns] if final else place,
            send_sem=send_c.at[t, o, n],
            recv_sem=recv_c.at[t, o, n],
            device_id={"head": dest},
            device_id_type=MESH,
        )

    def c_send(t, o, n, final):
        return c_copy(t, o, n, head_me, lax.rem(head_me + o, heads), final)

    def c_arrival(t, o, n, final):
        source = lax.rem(head_me + heads - o, heads)
        return c_copy(t, o, n, source, source, final)

    def either(t, act):
        @pl.when(t < STEPS - 1)
        def _():
            act(False)

        @pl.when(t == STEPS - 1)
        def _():
            act(True)

    def unit_queries(u):
        first = qkv[pl.ds(u * per_unit, half)]
        second = qkv[pl.ds(u * per_unit + per, half)]
        return jnp.concatenate([first, second], axis=0).reshape(unit_rows, HD)

    def out_part(u, first, count):
        left = jnp.concatenate([mix[u * group + i] for i in range(group)], axis=1)
        rows = pl.ds(pl.multiple_of(u * group * HD, HD), group * HD)
        return jnp.dot(
            left, wo_s[rows, first : first + count], preferred_element_type=F32
        )

    def step(t, carry):
        wide = h_out[...].astype(F32)
        scaled = (wide * gain[...]).astype(BF16)
        diag_r = lax.broadcasted_iota(jnp.int32, (samples, HD), 0)
        diag_c = lax.broadcasted_iota(jnp.int32, (samples, HD), 1)

        for x in order:
            u = flip(z, x)

            @pl.when(t == 0)
            def _():
                for load in w_loads(u):
                    load.wait()

            cols = pl.ds(pl.multiple_of(u * unit_width, HD), unit_width)
            got = jnp.dot(scaled, w_s[:, cols], preferred_element_type=F32)
            for i in range(per_unit):
                send_a[x, i] = got[:, i * HD : (i + 1) * HD].astype(BF16)
                if x == 0:
                    own_a[i] = got[:, i * HD : (i + 1) * HD]
            for y in range(sides):
                if x or y:
                    a_copy(x, y).start()
            if x == order[0]:
                squares = jnp.sum(wide * wide, axis=1, keepdims=True)
                sq_send[...] = jnp.sum(
                    jnp.where(diag_r == diag_c, squares, 0.0), axis=0, keepdims=True
                )
                for xx, yy in peers:
                    sq_copy(xx, yy).start()

        @pl.when(t == 0)
        def _():
            for load in later:
                load.start()
            prepare()

        total = sq_send[...]
        for x, y in peers:
            d = peer_rank(x, y)
            arrived(sq_recv.at[d], 0, d)
            total = total + sq_recv[d]
        total = jnp.sum(jnp.where(diag_r == diag_c, total, 0.0), axis=1, keepdims=True)
        inverse = lax.rsqrt(total / width + 1e-05)
        for x, y in peers:
            d = peer_rank(x, y)
            arrived(recv_a.at[d], 1, d)
        for i in range(per):
            value = own_a[side * per + i]
            for x, y in peers:
                value = value + recv_a[peer_rank(x, y), i].astype(F32)
            value = value * inverse
            turned = value * cosine[t] + pltpu.roll(value, HD // 2, 1) * sine[t]
            if i == half:
                turned = jnp.where(side == sides - 1, value, turned)
            qkv[me * per + i] = turned.astype(BF16)
        for x, y in [(0, 1)] + peers[::-1][1:]:
            q_copy(x, y).start()

        @pl.when(t == 0)
        def _():
            for load in later[:4]:
                load.wait()

        def pair_at(j):
            return lax.rem(lax.div(z, 2) + j, pairs)

        def blend(levels, values):
            best = functools.reduce(jnp.maximum, levels)
            amount = jnp.zeros((unit_rows, HD), F32)
            acc = jnp.zeros((unit_rows, HD), F32)
            for level, value in zip(levels, values):
                e = jnp.exp2(level - best)
                amount = amount + e
                acc = acc + e * value.astype(F32)
            return acc / amount, best + jnp.log(amount) * LOG2E

        def add_new():
            mine = unit_queries(z).astype(F32)
            levels, values = [box_l[0, 0]], [box_o[0, 0]]
            for n in range(STEPS):
                keys = jnp.concatenate([fresh_k[n]] * group, axis=0)
                score = jnp.sum(mine * keys, axis=1, keepdims=True) * BASE2
                score = jnp.where(n <= t, score, LOW)
                levels.append(jnp.broadcast_to(score, (unit_rows, HD)))
                values.append(jnp.concatenate([fresh_v[n]] * group, axis=0))
            value, level = blend(levels, values)
            box_o[0, 0] = value
            box_l[0, 0] = level

        def merge(j):
            v = pair_at(j)
            for n in range(2):
                p_copy(j, n).wait_recv()
            value, level = blend([box_l[j, 0], got_l[j]], [box_o[j, 0], got_o[j]])
            zone[v, z] = value.astype(BF16)
            zone_c[v] = level
            zone_l[v, z] = jnp.sum(jnp.where(eye(), level, 0.0), axis=0, keepdims=True)
            for n in range(2):
                for x in order[:-1]:
                    z_copy(v, x, n, z, flip(z, x)).start()

        def unit(i, carry):
            j = lax.div(i, 2)
            sub = lax.rem(i, 2)
            near_pair = lax.rem(z + sub, 2)
            far_pair = lax.rem(1 - side + sub, 2)
            late = lax.div(j + pairs - 1, pairs)
            parity = near_pair + late * (far_pair - near_pair)
            u = 2 * pair_at(j) + parity
            k = u
            for n in range(sides):
                owner = u * sides + n

                @pl.when(jnp.logical_and(u == z, owner != me))
                def _():
                    arrived(qkv.at[pl.ds(owner * per, per)], 2, owner)

                @pl.when(u != z)
                def _():
                    arrived(qkv.at[pl.ds(owner * per, half)], 2, owner)

            q = unit_queries(u)
            size = min(span, 1024)
            q_own = jnp.dot(chosen, q, preferred_element_type=F32).astype(BF16)
            scores = [
                lax.dot_general(q, pk_s[0, k, c : c + size], NT, preferred_element_type=F32)
                for c in range(0, span, size)
            ]
            near = lax.dot_general(
                q_own, sk_s[:, k].reshape(suffix, HD), NT, preferred_element_type=F32
            ) + bias[...]

            def soft(s, values):
                top = jnp.max(s, axis=1, keepdims=True)
                e = jnp.exp2((s - top) * BASE2)
                total = jnp.sum(e, axis=1, keepdims=True)
                return top, total, jnp.dot(e.astype(BF16), values, preferred_element_type=F32)

            parts = [
                soft(s, pv_s[0, k, n * size : (n + 1) * size]) for n, s in enumerate(scores)
            ]
            near_top, near_sum, near_acc = soft(near, sv_s[:, k].reshape(suffix, HD))
            parts.append(
                (
                    spread(jnp.broadcast_to(near_top, (own_rows, HD)), LOW),
                    spread(jnp.broadcast_to(near_sum, (own_rows, HD)), 0.0),
                    spread(near_acc, 0.0),
                )
            )
            best = functools.reduce(jnp.maximum, [part[0] for part in parts])
            amount = jnp.zeros((unit_rows, HD), F32)
            acc = jnp.zeros((unit_rows, HD), F32)
            for part_top, part_sum, part_acc in parts:
                weight = jnp.exp2((part_top - best) * BASE2)
                amount = amount + weight * part_sum
                acc = acc + weight * part_acc
            away = lax.rem(parity + side, 2)
            box_o[j, away] = acc / amount
            box_l[j, away] = best * BASE2 + jnp.log(amount) * LOG2E

            @pl.when(away == 1)
            def _():
                for n in range(2):
                    p_copy(j, n).start()

            @pl.when(jnp.logical_and(i == 1, lax.rem(z + side, 2) == 0))
            def _():
                fresh_k[t] = qkv[z * per_unit + half].astype(F32)
                fresh_v[t] = qkv[z * per_unit + per + half].astype(F32)
                add_new()

            @pl.when(sub == 1)
            def _():
                merge(j)

            return carry

        lax.fori_loop(0, kv, unit, 0)

        @pl.when(t == 0)
        def _():
            later[4].wait()

        def settle(v, carry):
            levels, values = [zone_c[v]], [zone[v, z]]
            for x in order[:-1]:
                source = flip(z, x)
                for n in range(2):
                    z_copy(v, x, n, source, source).wait_recv()
                levels.append(
                    jnp.sum(jnp.where(eye(), zone_l[v, source], 0.0), axis=1, keepdims=True)
                )
                values.append(zone[v, source])
            value, _ = blend(levels, values)
            mix[pl.ds((2 * v + side) * group, group)] = value.astype(BF16).reshape(group, gen, HD)
            m_copy(v, side).start()
            return carry

        lax.fori_loop(0, pairs, settle, 0)

        def sum_out(i, part):
            v = lax.rem(i, pairs)
            theirs = lax.div(i, pairs)

            @pl.when(theirs == 1)
            def _():
                m_copy(v, 1 - side).wait_recv()

            return part + out_part(2 * v + lax.rem(side + theirs, 2), 0, depth)

        part = lax.fori_loop(0, 2 * pairs, sum_out, jnp.zeros((samples, depth), F32))
        for n in range(pieces):
            total = part[:, n * piece : (n + 1) * piece]
            cbuf[t, head_me, :, n * piece : (n + 1) * piece] = total.astype(BF16)

            def send(final):
                for o in range(1, heads):
                    c_send(t, o, n, final).start()

            either(t, send)

        @pl.when(t == STEPS - 1)
        def _():
            stores[2].start()

        for x, y in peers:
            sq_copy(x, y).wait_send()
            a_copy(x, y).wait_send()
            q_copy(x, y).wait_send()
        for j in range(pairs):
            for n in range(2):
                p_copy(j, n).wait_send()
            for x in order[:-1]:
                for n in range(2):
                    z_copy(j, x, n, z, flip(z, x)).wait_send()
            m_copy(j, side).wait_send()

        def finish(final):
            for n in range(pieces):
                for o in range(1, heads):
                    c_arrival(t, o, n, final).wait_recv()
            if not final:
                delta = cbuf[t, 0].astype(F32)
                for n in range(1, heads):
                    delta = delta + cbuf[t, n].astype(F32)
                u_out[...] += delta
                h_out[...] = (h_out[...].astype(F32) + delta).astype(BF16)
            for n in range(pieces):
                for o in range(1, heads):
                    c_send(t, o, n, final).wait_send()

        either(t, finish)

        @pl.when(t == STEPS - 2)
        def _():
            for store in stores[:2]:
                store.start()

        return carry

    stores = [
        pltpu.make_async_copy(h_out, h_hbm, out_sem.at[0]),
        pltpu.make_async_copy(u_out, u_hbm, out_sem.at[1]),
        pltpu.make_async_copy(cbuf.at[STEPS - 1, head_me], c_hbm.at[head_me], out_sem.at[2]),
    ]
    lax.fori_loop(0, STEPS, step, 0)
    for store in stores:
        store.wait()


def local(
    ranks, sides, heads,
    hidden, gain, w_query, w_key, w_value, w_out, prefix_keys, prefix_values,
    suffix_keys, suffix_values, suffix_lengths, page_table,
):
    samples, depth = hidden.shape
    prompts, kv, span, _ = prefix_keys.shape
    group = w_query.shape[1] // w_key.shape[1]
    gen = samples // prompts
    slots, _, page, _ = suffix_keys.shape
    own_rows = samples // ranks * group
    all_heads = kv * (group + 2)
    per = -(-all_heads * prompts // ranks)
    unit_rows = group * gen
    units = prompts * kv
    rows = units * unit_rows // ranks

    power = -np.arange(HD // 2, dtype=np.float64) * 2.0 / HD
    freq = np.tile(500000.0 ** power, 2).astype(np.float32).reshape(1, HD)

    chips = ranks // sides
    paired = (
        prompts == 1
        and sides == 2
        and kv == chips
        and kv >= 4
        and chips & (chips - 1) == 0
        and samples % ranks == 0
        and group % 2 == 0
    )
    weights = [
        pltpu.VMEM((depth, all_heads * HD), BF16),
        pltpu.VMEM(w_out.shape, BF16),
        pltpu.VMEM(prefix_keys.shape, BF16),
        pltpu.VMEM(prefix_values.shape, BF16),
        pltpu.VMEM(suffix_keys.shape, BF16),
        pltpu.VMEM(suffix_values.shape, BF16),
        pltpu.VMEM((own_rows, slots * page), F32),
    ]
    state = [
        pltpu.VMEM(page_table.shape[::-1], jnp.int32),
        pltpu.VMEM((STEPS, samples, HD), F32),
        pltpu.VMEM((STEPS, samples, HD), F32),
        pltpu.VMEM((samples, depth), BF16),
        pltpu.VMEM((samples, depth), F32),
    ]
    dma = pltpu.SemaphoreType.DMA
    if paired:
        pairs = kv // 2
        pieces = 1
        body = functools.partial(
            chip_kernel, chips, sides, heads, kv, group, float(depth * ranks)
        )
        scratch = [
            pltpu.SMEM(suffix_lengths.shape, jnp.int32),
            pltpu.VMEM((1, depth), F32),
            pltpu.VMEM((1, HD), F32),
        ] + state + weights + [
            pltpu.VMEM((chips, group + 2, gen, HD), BF16),
            pltpu.VMEM((ranks, per, gen, HD), BF16),
            pltpu.VMEM((group + 2, gen, HD), F32),
            pltpu.VMEM((1, HD), F32),
            pltpu.VMEM((ranks, 1, HD), F32),
            pltpu.VMEM((all_heads, gen, HD), BF16),
            pltpu.VMEM((STEPS, gen, HD), F32),
            pltpu.VMEM((STEPS, gen, HD), F32),
            pltpu.VMEM((pairs, 2, unit_rows, HD), F32),
            pltpu.VMEM((pairs, 2, unit_rows, HD), F32),
            pltpu.VMEM((pairs, unit_rows, HD), F32),
            pltpu.VMEM((pairs, unit_rows, HD), F32),
            pltpu.VMEM((pairs, chips, unit_rows, HD), BF16),
            pltpu.VMEM((pairs, chips, 1, unit_rows), F32),
            pltpu.VMEM((pairs, unit_rows, HD), F32),
            pltpu.VMEM((kv * group, gen, HD), BF16),
            pltpu.VMEM((STEPS, heads, samples, depth), BF16),
            dma((4 * kv + 5,)),
            dma((3, ranks)),
            dma((3, ranks)),
            dma((pairs, 2)),
            dma((pairs, 2)),
            dma((pairs, chips, 2)),
            dma((pairs, chips, 2)),
            dma((pairs,)),
            dma((pairs,)),
            dma((STEPS, heads, pieces)),
            dma((STEPS, heads, pieces)),
            dma((5,)),
            dma((3,)),
        ]
    else:
        body = functools.partial(
            kernel, ranks, sides, heads, prompts, kv, group, float(depth * ranks)
        )
        scratch = state + weights + [
            pltpu.VMEM((ranks, per, gen, HD), BF16),
            pltpu.VMEM((ranks, per, gen, HD), BF16),
            pltpu.VMEM((per, gen, HD), F32),
            pltpu.VMEM((1, HD), F32),
            pltpu.VMEM((ranks, 1, HD), F32),
            pltpu.VMEM((ranks * per, gen, HD), BF16),
            pltpu.VMEM((STEPS, gen, HD), F32),
            pltpu.VMEM((STEPS, gen, HD), F32),
            pltpu.VMEM((units * unit_rows, HD), BF16),
            pltpu.VMEM((units, 1, unit_rows), F32),
            pltpu.VMEM((ranks, rows, HD), BF16),
            pltpu.VMEM((ranks, 1, unit_rows), F32),
            pltpu.VMEM((prompts * kv * group, gen, HD), BF16),
            pltpu.VMEM((samples, depth), F32),
            pltpu.VMEM((STEPS, heads, samples, depth), BF16),
            dma((3 * kv + 5,)),
            dma((6, ranks)),
            dma((6, ranks)),
            dma((STEPS, heads)),
            dma((STEPS, heads)),
            dma((3,)),
        ]

    vmem = pl.BlockSpec(memory_space=pltpu.VMEM)
    smem = pl.BlockSpec(memory_space=pltpu.SMEM)
    hbm = pl.BlockSpec(memory_space=pl.ANY)
    store = pl.BlockSpec(memory_space=pltpu.HBM)
    first = [store] * 5 if paired else [smem, store] + [vmem] * 3
    held, added, last = pl.pallas_call(
        body,
        out_shape=(
            jax.ShapeDtypeStruct((samples, depth), BF16),
            jax.ShapeDtypeStruct((samples, depth), F32),
            jax.ShapeDtypeStruct((heads, samples, depth), BF16),
        ),
        in_specs=first + [hbm] * 8,
        out_specs=(store, store, store),
        scratch_shapes=scratch,
        compiler_params=pltpu.CompilerParams(
            collective_id=0, has_side_effects=True, vmem_limit_bytes=60 * 1024 * 1024
        ),
    )(
        suffix_lengths, page_table.T, hidden, gain.reshape(1, depth), freq,
        w_query, w_key, w_value, w_out, prefix_keys, prefix_values, suffix_keys, suffix_values,
    )
    delta = last[0].astype(F32)
    for n in range(1, heads):
        delta = delta + last[n].astype(F32)
    return (held.astype(F32) + delta).astype(BF16), added + delta


def solution(mesh):
    placed = (
        P("groups", ("seq", "side")),
        P(("seq", "side")),
        P(("seq", "side"), "head"),
        P(("seq", "side"), "head"),
        P(("seq", "side"), "head"),
        P("head", ("seq", "side")),
        P("groups", "head", ("seq", "side"), None),
        P("groups", "head", ("seq", "side"), None),
        P(("groups", "seq", "side"), "head", None, None),
        P(("groups", "seq", "side"), "head", None, None),
        P("groups"),
        P("groups", None),
    )
    ranks = mesh.shape["seq"] * mesh.shape["side"]
    return jax.shard_map(
        functools.partial(local, ranks, mesh.shape["side"], mesh.shape["head"]),
        mesh=mesh,
        in_specs=placed,
        out_specs=(P("groups", ("seq", "side")), P("groups", ("seq", "side"))),
        check_vma=False,
    )
```
